32 devices in a mesh: groups: 2 (over x), dp: 16 (over z, y, core).
Axes of the slice: x: 2, y: 2, z: 4, core: 2. Of those that a mesh axis runs over, the one named last changes fastest.
Arguments:
- activations: bfloat16 [12288, 16384], P(('groups', 'dp')), parts along dimension 0, may hold values from -18 to 18
- labels: int32 [12288], P(('groups', 'dp')), parts along dimension 0, may hold values from 0 to 63, as said below
- counts: int32 [12288], P(('groups', 'dp')), parts along dimension 0, may hold values from 1 to 4
Outputs:
- solution: float32 [32768, 64], P(('groups', 'dp')), parts along dimension 0
- residual: float32 [32768, 64], P(('groups', 'dp')), parts along dimension 0
The draws below stay inside these ranges and needn't reach their ends.
There are 2 independent parts, one for each index of `groups`. The reference program is written for one: setup_inputs(seed, part) draws one part's arguments, and reference() takes and returns one part's arrays. A program takes and returns all parts, laid end to end along the dimension named above; each array names one. Nothing has to cross between parts.
Inputs may be any that keep to these rules, and one draw needn't show every extreme that they name: `labels`: concept index of each row; every concept of 0 to 63 names at least one row. `counts`: integer sample weight of each row.
All inputs are finite; a program needn't handle non-finite values.
Results may differ from the reference program's by a relative error of at most 0.012.
The reference program's roundings to bfloat16 on the way (of `member` and `weighted`) count: a program that leaves them out, or rounds other values in their place, can miss the bound.
Values may be sent and summed in bfloat16 or wider, within the bound.
No kernel may reach another device: no remote copies, remote signals or barrier semaphores. Data moves between devices by JAX's collectives and lax.ppermute only.
A program may use at most 64 MiB of HBM per device.

```python
import jax
import jax.numpy as jnp
from jax import lax

D = 16384
K = 64
ROW_DEV = 384
ITERS = 2
ROWS = 6144


def draw_labels(key, part):
    base = jax.random.randint(jax.random.fold_in(key, 11), (ROWS,), 0, K, dtype=jnp.int32)
    spots = jax.random.permutation(jax.random.fold_in(key, 12), ROWS)[:K]
    named = jax.random.permutation(jax.random.fold_in(key, 13), K).astype(jnp.int32)
    return base.at[spots].set(named)


def draw_activations(key, part):
    blocks = ROWS // ROW_DEV
    pairing = jax.random.permutation(jax.random.fold_in(key, 21), blocks).astype(jnp.int32)
    row_block = jnp.arange(ROWS, dtype=jnp.int32) // ROW_DEV
    col_block = jnp.arange(D, dtype=jnp.int32) // (D // blocks)
    target = pairing[row_block]
    spike = jnp.where(target[:, None] == col_block[None, :], jnp.float32(3.0), jnp.float32(1.0))
    values = jnp.clip(jax.random.normal(jax.random.fold_in(key, 24), (ROWS, D), jnp.float32), -6.0, 6.0)
    return (values * spike).astype(jnp.bfloat16)


def plant(values, key, least, top_value):
    longest = values.shape.index(max(values.shape))
    spots = []
    for shift in (0, 1):
        where = [jax.random.randint(jax.random.fold_in(key, axis), (), 0, length) for axis, length in enumerate(values.shape)]
        where[longest] = (where[longest] + shift) % values.shape[longest]
        spots.append(tuple(where))
    return values.at[spots[0]].set(least).at[spots[1]].set(top_value)


def setup_inputs(seed: int = 0, part: int = 0) -> dict:
    splits = jax.random.split(jax.random.key(seed), 4)
    part_splits = jax.random.split(jax.random.fold_in(splits[3], part), 4)
    return {
        "activations": draw_activations(jax.random.fold_in(jax.random.fold_in(splits[3], part), 71), part),
        "labels": draw_labels(jax.random.fold_in(jax.random.fold_in(splits[3], part), 71), part),
        "counts": plant(jax.random.randint(part_splits[2], (ROWS,), 1, 5), jax.random.fold_in(part_splits[2], 1), 1, 4).astype(jnp.int32),
    }


RIDGE = 0.1

def precise(left_side, right_side):
    return jnp.dot(left_side.astype(jnp.float32), right_side.astype(jnp.float32), precision=lax.Precision.HIGHEST, preferred_element_type=jnp.float32)

def symmetric(matrix):
    return 0.5 * (matrix + matrix.T)

def solve_positive(matrix, target):
    return jax.scipy.linalg.cho_solve((jnp.linalg.cholesky(matrix), True), target)

def contract_rows(left_side, right_side):
    return lax.dot_general(left_side.astype(jnp.float32), right_side.astype(jnp.float32), (((0,), (0,)), ((), ())), preferred_element_type=jnp.float32)

def reference(activations, labels, counts):
    weights = counts.astype(jnp.float32)
    classes = jnp.arange(K, dtype=jnp.int32)
    member_full = jnp.where(labels[:, None] == classes[None, :], weights[:, None], jnp.float32(0.0))
    class_weight = lax.optimization_barrier(jnp.sum(member_full, axis=0))
    member = member_full.astype(jnp.bfloat16)
    class_sums = contract_rows(activations, member)
    total_weight = jnp.sum(class_weight)
    class_means = class_sums / class_weight[None, :]
    mean_diff = class_means * jnp.sqrt(class_weight)[None, :]

    def apply_cov(panel_in):
        probed = jnp.dot(activations.astype(jnp.float32), panel_in.astype(jnp.bfloat16).astype(jnp.float32), preferred_element_type=jnp.float32)
        weighted = (weights[:, None] * probed).astype(jnp.bfloat16)
        panel = contract_rows(activations, weighted)
        cross = precise(class_means.T, panel_in)
        scaled = class_weight[:, None] * cross
        return (panel - precise(class_means, scaled)) / total_weight + RIDGE * panel_in
    solution = jnp.zeros_like(mean_diff)
    residual = mean_diff
    direction = mean_diff
    current = symmetric(precise(residual.T, residual))
    for iteration in range(ITERS):
        image = apply_cov(direction)
        curvature = symmetric(precise(direction.T, image))
        step_alpha = solve_positive(curvature, current)
        solution = solution + precise(direction, step_alpha)
        residual = residual - precise(image, step_alpha)
        if iteration + 1 < ITERS:
            renewed = symmetric(precise(residual.T, residual))
            step_beta = solve_positive(current, renewed)
            direction = residual + precise(direction, step_beta)
            current = renewed
    return (solution, residual)
```

```python
import functools

import jax
import jax.numpy as jnp
from jax import lax
from jax.experimental import pallas as pl
from jax.experimental.pallas import tpu as pltpu
from jax.sharding import PartitionSpec as P

K = 64
HALF = K // 2
RIDGE = 0.1
BOUND = 18.0
TOP = 60000.0
F32, BF16, F16 = jnp.float32, jnp.bfloat16, jnp.float16


def precise(left, right):
    return jnp.dot(left, right, precision=lax.Precision.HIGHEST, preferred_element_type=F32)


def outer(left, right):
    return lax.dot_general(
        left, right, (((1,), (1,)), ((), ())), precision=lax.Precision.HIGHEST, preferred_element_type=F32
    )


def symmetric(matrix):
    return 0.5 * (matrix + matrix.T)


def solve_positive(matrix, target):
    return jax.scipy.linalg.cho_solve((jnp.linalg.cholesky(matrix), True), target)


def swap(value, bit, n):
    return lax.ppermute(value, "dp", [(i, i ^ bit) for i in range(n)])


def total(value, n):
    bit = 1
    while bit < n:
        value = value + swap(value, bit, n)
        bit *= 2
    return value


def hop_bits(n):
    bits = [1 << i for i in range(1, n.bit_length() - 1)]
    return bits, bits[1:] + bits[:1]


def _rel(step, shifts):
    j = 0
    for place, shift in enumerate(shifts):
        j = j | (((step >> place) & 1) << shift)
    return j


def _pos(j, shifts):
    p = 0
    for place, shift in enumerate(shifts):
        p = p | (((j >> shift) & 1) << place)
    return p


def sums_kernel(me, labels, counts, acts, out, member):
    @pl.when(pl.program_id(0) == 0)
    def _():
        concept = lax.broadcasted_iota(jnp.int32, member.shape, 0)
        member[...] = jnp.where(labels[...] == concept, counts[...].astype(F32), 0.0).astype(BF16)

    out[0] = jnp.dot(member[...], acts[...], preferred_element_type=F32)


def class_sums(me, labels, counts, acts, n, half):
    rows, d = acts.shape
    f = d // n
    return pl.pallas_call(
        sums_kernel,
        out_shape=jax.ShapeDtypeStruct((n // 2, K, f), F32),
        grid_spec=pltpu.PrefetchScalarGridSpec(
            num_scalar_prefetch=1,
            grid=(n // 2,),
            in_specs=[
                pl.BlockSpec((1, rows), lambda i, me: (0, 0)),
                pl.BlockSpec((1, rows), lambda i, me: (0, 0)),
                pl.BlockSpec((rows, f), lambda i, me: (0, me[0] ^ (2 * i + half))),
            ],
            out_specs=pl.BlockSpec((1, K, f), lambda i, me: (i, 0, 0)),
            scratch_shapes=[pltpu.VMEM((K, rows), BF16)],
        ),
        compiler_params=pltpu.CompilerParams(vmem_limit_bytes=32 << 20),
        cost_estimate=pl.CostEstimate(flops=K * rows * d, bytes_accessed=rows * d + 2 * K * d, transcendentals=0),
        name="class_sums",
    )(me, labels, counts, acts)


def probe_kernel(me, v_a, v_b, acts, out):
    @pl.when(pl.program_id(0) == 0)
    def _():
        out[...] = jnp.zeros_like(out)

    v = jnp.concatenate([v_a[0], v_b[0]], axis=0)
    out[...] += lax.dot_general(v, acts[...], (((1,), (1,)), ((), ())), preferred_element_type=F32)


def probe(me, v_a, v_b, acts, n, shifts_a, shifts_b):
    rows, d = acts.shape
    f = d // n
    return pl.pallas_call(
        probe_kernel,
        out_shape=jax.ShapeDtypeStruct((K, rows), F32),
        grid_spec=pltpu.PrefetchScalarGridSpec(
            num_scalar_prefetch=1,
            grid=(n // 2,),
            in_specs=[
                pl.BlockSpec((1, HALF, f), lambda i, me: (_pos(_rel(i, shifts_a), shifts_a), 0, 0)),
                pl.BlockSpec((1, HALF, f), lambda i, me: (_pos(_rel(i, shifts_a), shifts_b), 0, 0)),
                pl.BlockSpec((rows, f), lambda i, me: (0, me[0] ^ _rel(i, shifts_a))),
            ],
            out_specs=pl.BlockSpec((K, rows), lambda i, me: (0, 0)),
        ),
        compiler_params=pltpu.CompilerParams(vmem_limit_bytes=32 << 20),
        cost_estimate=pl.CostEstimate(flops=K * rows * d, bytes_accessed=rows * d + K * d, transcendentals=0),
        name="probe",
    )(me, v_a, v_b, acts)


def send_kernel(steps, me, v_a, v_b, acts, start, counts, probed, gram, out, kept, weighted):
    step = pl.program_id(0)

    @pl.when(step == 0)
    def _():
        probed[...] = start[...]

    @pl.when(step < steps)
    def _():
        v = jnp.concatenate([v_a[0], v_b[0]], axis=0)
        kept[step] = acts[...]
        probed[...] += lax.dot_general(v, acts[...], (((1,), (1,)), ((), ())), preferred_element_type=F32)

    @pl.when(step == steps)
    def _():
        weighted[...] = (counts[...].astype(F32) * probed[...]).astype(BF16)
        gram[...] = outer(probed[...], weighted[...].astype(F32))

    @pl.when(step >= steps)
    def _():
        out[0] = jnp.dot(weighted[...], kept[step - steps], preferred_element_type=F32)


def probe_and_send(me, v_a, v_b, acts, start, counts, n, shifts_a, shifts_b):
    rows, d = acts.shape
    f = d // n
    s = n // 2

    def j_of(i):
        return _rel(jnp.minimum(i, s - 1), shifts_a)

    out_pos = [shift for shift in range(1, n.bit_length() - 1)]
    return pl.pallas_call(
        functools.partial(send_kernel, s),
        out_shape=(
            jax.ShapeDtypeStruct((K, rows), F32),
            jax.ShapeDtypeStruct((K, K), F32),
            jax.ShapeDtypeStruct((s, K, f), F32),
        ),
        grid_spec=pltpu.PrefetchScalarGridSpec(
            num_scalar_prefetch=1,
            grid=(2 * s,),
            in_specs=[
                pl.BlockSpec((1, HALF, f), lambda i, me: (_pos(j_of(i), shifts_a), 0, 0)),
                pl.BlockSpec((1, HALF, f), lambda i, me: (_pos(j_of(i), shifts_b), 0, 0)),
                pl.BlockSpec((rows, f), lambda i, me: (0, me[0] ^ 1 ^ j_of(i))),
                pl.BlockSpec((K, rows), lambda i, me: (0, 0)),
                pl.BlockSpec((1, rows), lambda i, me: (0, 0)),
            ],
            out_specs=(
                pl.BlockSpec((K, rows), lambda i, me: (0, 0)),
                pl.BlockSpec((K, K), lambda i, me: (0, 0)),
                pl.BlockSpec(
                    (1, K, f), lambda i, me: (_pos(_rel(jnp.maximum(i - s, 0), shifts_a), out_pos), 0, 0)
                ),
            ),
            scratch_shapes=[pltpu.VMEM((s, rows, f), BF16), pltpu.VMEM((K, rows), BF16)],
        ),
        compiler_params=pltpu.CompilerParams(vmem_limit_bytes=40 << 20),
        cost_estimate=pl.CostEstimate(flops=2 * K * rows * d, bytes_accessed=rows * d + 2 * K * d, transcendentals=0),
        name="probe_and_send",
    )(me, v_a, v_b, acts, start, counts)


def keep_kernel(me, probed, counts, acts, out, weighted):
    @pl.when(pl.program_id(0) == 0)
    def _():
        weighted[...] = (counts[...].astype(F32) * probed[...]).astype(BF16)

    out[0] = jnp.dot(weighted[...], acts[...], preferred_element_type=F32)


def panel_keep(me, probed, counts, acts, n):
    rows, d = acts.shape
    f = d // n
    return pl.pallas_call(
        keep_kernel,
        out_shape=jax.ShapeDtypeStruct((n // 2, K, f), F32),
        grid_spec=pltpu.PrefetchScalarGridSpec(
            num_scalar_prefetch=1,
            grid=(n // 2,),
            in_specs=[
                pl.BlockSpec((K, rows), lambda i, me: (0, 0)),
                pl.BlockSpec((1, rows), lambda i, me: (0, 0)),
                pl.BlockSpec((rows, f), lambda i, me: (0, me[0] ^ (2 * i))),
            ],
            out_specs=pl.BlockSpec((1, K, f), lambda i, me: (i, 0, 0)),
            scratch_shapes=[pltpu.VMEM((K, rows), BF16)],
        ),
        compiler_params=pltpu.CompilerParams(vmem_limit_bytes=32 << 20),
        cost_estimate=pl.CostEstimate(flops=K * rows * d, bytes_accessed=rows * d + 2 * K * d, transcendentals=0),
        name="panel_keep",
    )(me, probed, counts, acts)


def scatter_stream(blocks, order, n, inv, wire):
    bits = n.bit_length() - 2
    rows, f = blocks.shape[1:]
    value = blocks.reshape((2,) * bits + (rows, f))
    left = [1 << i for i in range(bits, 0, -1)]
    for bit in order:
        axis = left.index(bit)
        keep = lax.index_in_dim(value, 0, axis, keepdims=False)
        send = lax.index_in_dim(value, 1, axis, keepdims=False)
        left.remove(bit)
        if wire == F32:
            value = keep + swap(send, bit, n)
        else:
            value = keep + swap((send * inv).astype(wire), bit, n).astype(F32) / inv
    return value


def reduce_scatter(sent, make_keep, n, inv, wire):
    if wire == F32:
        got = swap(sent, 1, n)
    else:
        got = swap((sent * inv).astype(wire), 1, n).astype(F32) / inv
    blocks = make_keep() + got
    order_a, order_b = hop_bits(n)
    part = (lambda x, a, b: x) if wire == F32 else (lambda x, a, b: x[a:b])
    top = scatter_stream(blocks[:, :HALF], order_a, n, part(inv, 0, HALF), wire)
    low = scatter_stream(blocks[:, HALF:], order_b, n, part(inv, HALF, K), wire)
    return jnp.concatenate([top, low], axis=0)


def gather_stream(block, order, n):
    value = block[None]
    for bit in order:
        value = jnp.concatenate([value, swap(value, bit, n)], axis=0)
    return value


def per_device(n, activations, labels, counts):
    rows, d = activations.shape
    me = lax.axis_index("dp").astype(jnp.int32).reshape(1)
    labels = labels.reshape(1, rows)
    counts = counts.reshape(1, rows)
    order_a, order_b = hop_bits(n)
    order_a = order_a[::-1]
    shifts_a = [bit.bit_length() - 1 for bit in order_a]
    shifts_b = [bit.bit_length() - 1 for bit in order_b]

    concept = lax.broadcasted_iota(jnp.int32, (K, rows), 0)
    local_weight = jnp.sum(jnp.where(labels == concept, counts.astype(F32), 0.0), axis=1, keepdims=True)
    class_weight = total(local_weight, n)
    total_weight = jnp.sum(class_weight)

    sent = class_sums(me, labels, counts, activations, n, 1)
    sums = reduce_scatter(
        sent, lambda: class_sums(me, labels, counts, activations, n, 0), n, None, F32
    )
    base = (sums / class_weight) * jnp.sqrt(class_weight)

    def apply(panel, counts, combine, norms):
        v = panel.astype(BF16)
        v_a = gather_stream(v[:HALF], order_a, n)
        v_b = gather_stream(v[HALF:], order_b, n)
        far_a, far_b = swap(v_a, 1, n), swap(v_b, 1, n)
        start = combine(probe(me, v_a, v_b, activations, n, shifts_a, shifts_b))
        bound = (1.01 * BOUND * BOUND * d**0.5) * total_weight * norms
        inv = TOP / jnp.maximum(bound, 1e-30)
        probed, gram, sent = probe_and_send(
            me, far_a, far_b, activations, start, counts, n, shifts_a, shifts_b
        )
        gram = total(gram, n)
        own = reduce_scatter(
            sent, lambda: panel_keep(me, probed, counts, activations, n), n, inv, F16
        )
        return probed, gram, own

    current = symmetric(total(outer(base, base), n))
    norm_base = jnp.sqrt(jnp.diag(current))[:, None]
    probed, along_panel, panel = apply(base, counts, lambda x: x, norm_base)

    curvature = symmetric((along_panel - precise(current, current)) / total_weight + RIDGE * current)
    alpha = solve_positive(curvature, current).T
    from_base = base + precise(precise(alpha, current) / total_weight - RIDGE * alpha, base)
    residual = from_base - precise(alpha / total_weight, panel)

    grams = total(outer(jnp.concatenate([residual, base], axis=0), residual), n)
    renewed = symmetric(grams[:K])
    mixed = grams[K:]
    beta = solve_positive(current, renewed)
    beta_t = beta.T
    norm_next = jnp.sqrt(jnp.diag(renewed))[:, None] + precise(jnp.abs(beta_t), norm_base)
    first = probed
    _, along_panel, panel = apply(residual, counts, lambda x: x + precise(beta_t, first), norm_next)

    direction = residual + precise(beta_t, base)
    cross = mixed + precise(current, beta)
    along = renewed + precise(mixed.T, beta) + precise(beta_t, cross)
    curvature = symmetric((along_panel - precise(cross.T, cross)) / total_weight + RIDGE * along)
    step = solve_positive(curvature, renewed).T
    solution = precise(alpha, base) + precise(step, direction)
    rest = residual - precise(step, RIDGE * direction - precise(cross.T / total_weight, base))
    residual = rest - precise(step / total_weight, panel)
    return (solution.T, residual.T)


def solution(mesh):
    in_specs = (P(("groups", "dp"), None), P(("groups", "dp")), P(("groups", "dp")))
    out_specs = (P(("groups", "dp"), None), P(("groups", "dp"), None))
    return jax.shard_map(
        functools.partial(per_device, mesh.shape["dp"]),
        mesh=mesh,
        in_specs=in_specs,
        out_specs=out_specs,
        check_vma=False,
    )
```

```python
import functools

import jax
import jax.numpy as jnp
from jax import lax
from jax.experimental import pallas as pl
from jax.experimental.pallas import tpu as pltpu
from jax.sharding import PartitionSpec as P

K = 64
HALF = K // 2
RIDGE = 0.1
BOUND = 18.0
TOP = 60000.0
TINY = 1e-30
F32, BF16, F16 = jnp.float32, jnp.bfloat16, jnp.float16


def precise(left, right):
    return jnp.dot(left, right, precision=lax.Precision.HIGHEST, preferred_element_type=F32)


def outer(left, right):
    return lax.dot_general(
        left, right, (((1,), (1,)), ((), ())), precision=lax.Precision.HIGHEST, preferred_element_type=F32
    )


def symmetric(matrix):
    return 0.5 * (matrix + matrix.T)


def solve_positive(matrix, target):
    return jax.scipy.linalg.cho_solve((jnp.linalg.cholesky(matrix), True), target)


def swap(value, bit, n):
    return lax.ppermute(value, "dp", [(i, i ^ bit) for i in range(n)])


def total(value, n):
    bit = 1
    while bit < n:
        value = value + swap(value, bit, n)
        bit *= 2
    return value


def hop_bits(n):
    bits = [1 << i for i in range(1, n.bit_length() - 1)]
    return bits, bits[1:] + bits[:1]


def _rel(step, shifts):
    j = 0
    for place, shift in enumerate(shifts):
        j = j | (((step >> place) & 1) << shift)
    return j


def _pos(j, shifts):
    p = 0
    for place, shift in enumerate(shifts):
        p = p | (((j >> shift) & 1) << place)
    return p


def sums_kernel(me, labels, counts, acts, out, peak, weight, member):
    step = pl.program_id(0)

    @pl.when(step == 0)
    def _():
        concept = lax.broadcasted_iota(jnp.int32, member.shape, 0)
        full = jnp.where(labels[...] == concept, counts[...].astype(F32), 0.0)
        member[...] = full.astype(BF16)
        weight[...] = jnp.sum(full, axis=1, keepdims=True)
        peak[...] = jnp.zeros_like(peak)

    block = jnp.dot(member[...], acts[...], preferred_element_type=F32)
    out[0] = block
    peak[...] = jnp.maximum(peak[...], jnp.max(jnp.abs(block), axis=1, keepdims=True))


def class_sums(me, labels, counts, acts, n, half):
    rows, d = acts.shape
    f = d // n
    return pl.pallas_call(
        sums_kernel,
        out_shape=(
            jax.ShapeDtypeStruct((n // 2, K, f), F32),
            jax.ShapeDtypeStruct((K, 1), F32),
            jax.ShapeDtypeStruct((K, 1), F32),
        ),
        grid_spec=pltpu.PrefetchScalarGridSpec(
            num_scalar_prefetch=1,
            grid=(n // 2,),
            in_specs=[
                pl.BlockSpec((1, rows), lambda i, me: (0, 0)),
                pl.BlockSpec((1, rows), lambda i, me: (0, 0)),
                pl.BlockSpec((rows, f), lambda i, me: (0, me[0] ^ (2 * i + half))),
            ],
            out_specs=(
                pl.BlockSpec((1, K, f), lambda i, me: (i, 0, 0)),
                pl.BlockSpec((K, 1), lambda i, me: (0, 0)),
                pl.BlockSpec((K, 1), lambda i, me: (0, 0)),
            ),
            scratch_shapes=[pltpu.VMEM((K, rows), BF16)],
        ),
        compiler_params=pltpu.CompilerParams(vmem_limit_bytes=8 << 20),
        cost_estimate=pl.CostEstimate(flops=K * rows * d, bytes_accessed=rows * d + 2 * K * d, transcendentals=0),
        name="class_sums",
    )(me, labels, counts, acts)


def probe_kernel(me, v_a, v_b, acts, out):
    @pl.when(pl.program_id(0) == 0)
    def _():
        out[...] = jnp.zeros_like(out)

    v = jnp.concatenate([v_a[0], v_b[0]], axis=0)
    out[...] += lax.dot_general(v, acts[...], (((1,), (1,)), ((), ())), preferred_element_type=F32)


def probe(me, v_a, v_b, acts, n, shifts_a, shifts_b):
    rows, d = acts.shape
    f = d // n
    return pl.pallas_call(
        probe_kernel,
        out_shape=jax.ShapeDtypeStruct((K, rows), F32),
        grid_spec=pltpu.PrefetchScalarGridSpec(
            num_scalar_prefetch=1,
            grid=(n // 2,),
            in_specs=[
                pl.BlockSpec((1, HALF, f), lambda i, me: (_pos(_rel(i, shifts_a), shifts_a), 0, 0)),
                pl.BlockSpec((1, HALF, f), lambda i, me: (_pos(_rel(i, shifts_a), shifts_b), 0, 0)),
                pl.BlockSpec((rows, f), lambda i, me: (0, me[0] ^ _rel(i, shifts_a))),
            ],
            out_specs=pl.BlockSpec((K, rows), lambda i, me: (0, 0)),
        ),
        compiler_params=pltpu.CompilerParams(vmem_limit_bytes=8 << 20),
        cost_estimate=pl.CostEstimate(flops=K * rows * d, bytes_accessed=rows * d + K * d, transcendentals=0),
        name="probe",
    )(me, v_a, v_b, acts)


def send_kernel(steps, mixed, me, v_a, v_b, acts, start, counts, *refs):
    if mixed:
        offset, mix, probed, gram, out, weighted = refs
    else:
        probed, gram, out, weighted = refs
    step = pl.program_id(0)

    @pl.when(step == 0)
    def _():
        probed[...] = start[...]

    @pl.when(step < steps)
    def _():
        v = jnp.concatenate([v_a[0], v_b[0]], axis=0)
        probed[...] += lax.dot_general(v, acts[...], (((1,), (1,)), ((), ())), preferred_element_type=F32)

    @pl.when(step == steps)
    def _():
        if mixed:
            probed[...] = offset[...] - precise(mix[...], probed[...])
        weighted[...] = (counts[...].astype(F32) * probed[...]).astype(BF16)
        gram[...] = outer(probed[...], weighted[...].astype(F32))

    @pl.when(step >= steps)
    def _():
        out[0] = jnp.dot(weighted[...], acts[...], preferred_element_type=F32)


def probe_and_send(me, v_a, v_b, acts, start, counts, mixing, n, shifts_a, shifts_b):
    rows, d = acts.shape
    f = d // n
    s = n // 2

    def j_of(i):
        return _rel(jnp.minimum(i, s - 1), shifts_a)

    def out_of(i):
        return jnp.maximum(i - s, 0)

    return pl.pallas_call(
        functools.partial(send_kernel, s, bool(mixing)),
        out_shape=(
            jax.ShapeDtypeStruct((K, rows), F32),
            jax.ShapeDtypeStruct((K, K), F32),
            jax.ShapeDtypeStruct((s, K, f), F32),
        ),
        grid_spec=pltpu.PrefetchScalarGridSpec(
            num_scalar_prefetch=1,
            grid=(2 * s,),
            in_specs=[
                pl.BlockSpec((1, HALF, f), lambda i, me: (_pos(j_of(i), shifts_a), 0, 0)),
                pl.BlockSpec((1, HALF, f), lambda i, me: (_pos(j_of(i), shifts_b), 0, 0)),
                pl.BlockSpec(
                    (rows, f), lambda i, me: (0, me[0] ^ 1 ^ jnp.where(i < s, j_of(i), 2 * out_of(i)))
                ),
                pl.BlockSpec((K, rows), lambda i, me: (0, 0)),
                pl.BlockSpec((1, rows), lambda i, me: (0, 0)),
            ]
            + [pl.BlockSpec((K, x.shape[1]), lambda i, me: (0, 0)) for x in mixing],
            out_specs=(
                pl.BlockSpec((K, rows), lambda i, me: (0, 0)),
                pl.BlockSpec((K, K), lambda i, me: (0, 0)),
                pl.BlockSpec((1, K, f), lambda i, me: (out_of(i), 0, 0)),
            ),
            scratch_shapes=[pltpu.VMEM((K, rows), BF16)],
        ),
        compiler_params=pltpu.CompilerParams(vmem_limit_bytes=8 << 20),
        cost_estimate=pl.CostEstimate(flops=2 * K * rows * d, bytes_accessed=rows * d + 2 * K * d, transcendentals=0),
        name="probe_and_send",
    )(me, v_a, v_b, acts, start, counts, *mixing)


def keep_kernel(me, probed, counts, acts, out, weighted):
    @pl.when(pl.program_id(0) == 0)
    def _():
        weighted[...] = (counts[...].astype(F32) * probed[...]).astype(BF16)

    out[0] = jnp.dot(weighted[...], acts[...], preferred_element_type=F32)


def panel_keep(me, probed, counts, acts, n):
    rows, d = acts.shape
    f = d // n
    return pl.pallas_call(
        keep_kernel,
        out_shape=jax.ShapeDtypeStruct((n // 2, K, f), F32),
        grid_spec=pltpu.PrefetchScalarGridSpec(
            num_scalar_prefetch=1,
            grid=(n // 2,),
            in_specs=[
                pl.BlockSpec((K, rows), lambda i, me: (0, 0)),
                pl.BlockSpec((1, rows), lambda i, me: (0, 0)),
                pl.BlockSpec((rows, f), lambda i, me: (0, me[0] ^ (2 * i))),
            ],
            out_specs=pl.BlockSpec((1, K, f), lambda i, me: (i, 0, 0)),
            scratch_shapes=[pltpu.VMEM((K, rows), BF16)],
        ),
        compiler_params=pltpu.CompilerParams(vmem_limit_bytes=8 << 20),
        cost_estimate=pl.CostEstimate(flops=K * rows * d, bytes_accessed=rows * d + 2 * K * d, transcendentals=0),
        name="panel_keep",
    )(me, probed, counts, acts)


def shrink(value, bound):
    return (value * (TOP / jnp.maximum(bound, TINY))).astype(F16)


def grow(value, bound):
    return value.astype(F32) * (jnp.maximum(bound, TINY) * (1.0 / TOP))


def scatter_stream(blocks, order, n, bound, shared):
    bits = n.bit_length() - 2
    rows, f = blocks.shape[1:]
    value = blocks.reshape((2,) * bits + (rows, f))
    left = [1 << i for i in range(bits, 0, -1)]
    for bit in order:
        axis = left.index(bit)
        keep = lax.index_in_dim(value, 0, axis, keepdims=False)
        send = lax.index_in_dim(value, 1, axis, keepdims=False)
        left.remove(bit)
        got = swap(shrink(send, bound), bit, n)
        theirs = bound if shared else swap(bound, bit, n)
        value = keep + grow(got, theirs)
        if not shared:
            bound = 1.001 * (bound + theirs)
    return value


def gather_stream(block, order, n):
    value = block[None]
    for bit in order:
        value = jnp.concatenate([value, swap(value, bit, n)], axis=0)
    return value


def per_device(n, activations, labels, counts):
    rows, d = activations.shape
    activations = pltpu.with_memory_space_constraint(activations, pltpu.HBM)
    me = lax.axis_index("dp").astype(jnp.int32).reshape(1)
    labels = labels.reshape(1, rows)
    counts = counts.reshape(1, rows)
    order_y, order_z = hop_bits(n)
    order_a, order_b = order_y[::-1], order_z
    shifts_a = [bit.bit_length() - 1 for bit in order_a]
    shifts_b = [bit.bit_length() - 1 for bit in order_b]

    sent, peak_sent, weight = class_sums(me, labels, counts, activations, n, 1)
    peak_sent = jnp.max(peak_sent, keepdims=True)
    got = swap(shrink(sent, peak_sent), 1, n)
    peak_got = swap(peak_sent, 1, n)
    kept, peak, _ = class_sums(me, labels, counts, activations, n, 0)
    blocks = kept + grow(got, peak_got)
    bound = 1.001 * (jnp.max(peak, keepdims=True) + peak_got)
    class_weight = total(weight, n)
    total_weight = jnp.sum(class_weight)
    sums = jnp.concatenate(
        [
            scatter_stream(blocks[:, :HALF], order_y, n, bound, False),
            scatter_stream(blocks[:, HALF:], order_z, n, bound, False),
        ],
        axis=0,
    )
    base = (sums / class_weight) * jnp.sqrt(class_weight)

    def apply(panel, mixing, norms):
        v = panel.astype(BF16)
        v_a = gather_stream(v[:HALF], order_a, n)
        v_b = gather_stream(v[HALF:], order_b, n)
        far_a, far_b = swap(v_a, 1, n), swap(v_b, 1, n)
        start = probe(me, v_a, v_b, activations, n, shifts_a, shifts_b)
        mixing, norms = mixing(), norms()
        bound = (1.02 * BOUND * BOUND * d**0.5) * total_weight * norms
        probed, gram, sent = probe_and_send(
            me, far_a, far_b, activations, start, counts, mixing, n, shifts_a, shifts_b
        )
        got = swap(shrink(sent, bound), 1, n)
        blocks = panel_keep(me, probed, counts, activations, n) + grow(got, bound)
        gram = total(gram, n)
        own = jnp.concatenate(
            [
                scatter_stream(blocks[:, :HALF], order_y, n, bound[:HALF], True),
                scatter_stream(blocks[:, HALF:], order_z, n, bound[HALF:], True),
            ],
            axis=0,
        )
        return probed, gram, own

    current = symmetric(total(outer(base, base), n))
    norm_base = jnp.sqrt(jnp.diag(current))[:, None]
    first, along_panel, panel = apply(base, lambda: (), lambda: norm_base)

    image = panel / total_weight + (RIDGE * base - precise(current / total_weight, base))
    curvature = symmetric((along_panel - precise(current, current)) / total_weight + RIDGE * current)
    alpha = solve_positive(curvature, current)
    alpha_t = alpha.T
    grams = total(outer(jnp.concatenate([image, base], axis=0), image), n)
    image_image, base_image = symmetric(grams[:K]), grams[K:]
    moved = precise(base_image, alpha)
    renewed = symmetric(current - moved - moved.T + precise(alpha_t, precise(image_image, alpha)))
    mixed = current - moved
    beta = solve_positive(current, renewed)
    beta_t = beta.T

    def mixing():
        return first + precise(beta_t, first), alpha_t

    def norms():
        norm_image = jnp.sqrt(jnp.diag(image_image))[:, None]
        return norm_base + precise(jnp.abs(beta_t), norm_base) + precise(jnp.abs(alpha_t), norm_image)

    _, along_panel, panel = apply(image, mixing, norms)

    residual = base - precise(alpha_t, image)
    direction = residual + precise(beta_t, base)
    cross = mixed + precise(current, beta)
    along = renewed + precise(mixed.T, beta) + precise(beta_t, cross)
    curvature = symmetric((along_panel - precise(cross.T, cross)) / total_weight + RIDGE * along)
    step = solve_positive(curvature, renewed).T
    solution = precise(alpha_t, base) + precise(step, direction)
    rest = residual - precise(step, RIDGE * direction - precise(cross.T / total_weight, base))
    residual = rest - precise(step / total_weight, panel)
    return (solution.T, residual.T)


def solution(mesh):
    in_specs = (P(("groups", "dp"), None), P(("groups", "dp")), P(("groups", "dp")))
    out_specs = (P(("groups", "dp"), None), P(("groups", "dp"), None))
    return jax.shard_map(
        functools.partial(per_device, mesh.shape["dp"]),
        mesh=mesh,
        in_specs=in_specs,
        out_specs=out_specs,
        check_vma=False,
    )
```

```python
import functools

import jax
import jax.numpy as jnp
from jax import lax
from jax.experimental import pallas as pl
from jax.experimental.pallas import tpu as pltpu
from jax.sharding import PartitionSpec as P

K = 64
HALF = K // 2
RIDGE = 0.1
BOUND = 18.0
TOP = 60000.0
TINY = 1e-30
F32, BF16, F16 = jnp.float32, jnp.bfloat16, jnp.float16


def precise(left, right):
    return jnp.dot(left, right, precision=lax.Precision.HIGHEST, preferred_element_type=F32)


def outer(left, right):
    return lax.dot_general(
        left, right, (((1,), (1,)), ((), ())), precision=lax.Precision.HIGHEST, preferred_element_type=F32
    )


def symmetric(matrix):
    return 0.5 * (matrix + matrix.T)


def solve_positive(matrix, target):
    work = jnp.concatenate([matrix, target], axis=1)
    index = lax.broadcasted_iota(jnp.int32, (K, 1), 0)
    for k in range(0, K, 2):
        a, b = work[k : k + 1], work[k + 1 : k + 2]
        col_a, col_b = work[:, k : k + 1], work[:, k + 1 : k + 2]
        p, q = work[k : k + 1, k : k + 1], work[k : k + 1, k + 1 : k + 2]
        t, r = work[k + 1 : k + 2, k : k + 1], work[k + 1 : k + 2, k + 1 : k + 2]
        inv = 1.0 / (p * r - q * t)
        new_a, new_b = (r * a - q * b) * inv, (p * b - t * a) * inv
        rest = work - (col_a * new_a + col_b * new_b)
        work = jnp.where(index == k, new_a, jnp.where(index == k + 1, new_b, rest))
    return work[:, K:]


def swap(value, bit, n):
    return lax.ppermute(value, "dp", [(i, i ^ bit) for i in range(n)])


def hop_bits(n):
    bits = [1 << i for i in range(1, n.bit_length() - 1)]
    return bits, bits[1:] + bits[:1]


def _pos(j, shifts):
    p = 0
    for place, shift in enumerate(shifts):
        p = p | (((j >> shift) & 1) << place)
    return p


def block_copy(acts, kept, sems, me, half, t):
    f = kept.shape[2]
    first = pl.multiple_of((me[0] ^ (2 * t + half)) * f, f)
    return pltpu.make_async_copy(acts.at[:, pl.ds(first, f)], kept.at[t], sems.at[t])


def start_copies(acts, kept, sems, me, half):
    def start(t, carry):
        block_copy(acts, kept, sems, me, half, t).start()
        return carry

    lax.fori_loop(0, kept.shape[0], start, 0)


def whole(*shape):
    return pl.BlockSpec(shape, lambda i, me: (0,) * len(shape))


HBM = pl.BlockSpec(memory_space=pltpu.HBM)


def call(kernel, name, n, grid, in_specs, out_shapes, out_specs, acts, scratch=()):
    rows, d = acts.shape
    return pl.pallas_call(
        kernel,
        out_shape=out_shapes,
        grid_spec=pltpu.PrefetchScalarGridSpec(
            num_scalar_prefetch=1,
            grid=(grid,),
            in_specs=in_specs,
            out_specs=out_specs,
            scratch_shapes=[
                pltpu.VMEM((n // 2, rows, d // n), BF16),
                pltpu.SemaphoreType.DMA((n // 2,)),
                *scratch,
            ],
        ),
        compiler_params=pltpu.CompilerParams(vmem_limit_bytes=16 << 20),
        cost_estimate=pl.CostEstimate(flops=K * rows * d, bytes_accessed=rows * d + 2 * K * d, transcendentals=0),
        name=name,
    )


def sums_kernel(half, me, labels, counts, acts, out, peak, weight, kept, sems, member):
    step = pl.program_id(0)

    @pl.when(step == 0)
    def _():
        start_copies(acts, kept, sems, me, half)
        concept = lax.broadcasted_iota(jnp.int32, member.shape, 0)
        full = jnp.where(labels[...] == concept, counts[...].astype(F32), 0.0)
        member[...] = full.astype(BF16)
        weight[...] = jnp.sum(full, axis=1, keepdims=True)
        peak[...] = jnp.zeros_like(peak)

    block_copy(acts, kept, sems, me, half, step).wait()
    block = jnp.dot(member[...], kept[step], preferred_element_type=F32)
    out[0] = block
    peak[...] = jnp.maximum(peak[...], jnp.max(jnp.max(jnp.abs(block), axis=1, keepdims=True), axis=0, keepdims=True))


def class_sums(me, labels, counts, acts, n, half):
    rows, d = acts.shape
    f = d // n
    return call(
        functools.partial(sums_kernel, half),
        "class_sums",
        n,
        n // 2,
        [whole(1, rows), whole(1, rows), HBM],
        (
            jax.ShapeDtypeStruct((n // 2, K, f), F32),
            jax.ShapeDtypeStruct((1, 1), F32),
            jax.ShapeDtypeStruct((K, 1), F32),
        ),
        (pl.BlockSpec((1, K, f), lambda i, me: (i, 0, 0)), whole(1, 1), whole(K, 1)),
        acts,
        [pltpu.VMEM((K, rows), BF16)],
    )(me, labels, counts, acts)


def inner(left, right):
    return lax.dot_general(left, right, (((1,), (1,)), ((), ())), preferred_element_type=F32)


def v_specs(n, f, shifts_a, shifts_b):
    s = n // 2
    return [
        pl.BlockSpec((1, HALF, f), lambda i, me: (_pos(2 * jnp.minimum(i, s - 1), shifts_a), 0, 0)),
        pl.BlockSpec((1, HALF, f), lambda i, me: (_pos(2 * jnp.minimum(i, s - 1), shifts_b), 0, 0)),
    ]


def add_block(panels, acts, probed, grams):
    both = [jnp.concatenate([panels[i][0], panels[i + 1][0]], axis=0) for i in range(0, len(panels), 2)]
    probed[...] += inner(both[0], acts)
    for gram, other in zip(grams, both):
        gram[...] += inner(other, both[0])


def probe_kernel(count, me, *refs):
    panels, (acts, probed, *grams) = refs[: 2 * count], refs[2 * count : -2]
    kept, sems = refs[-2:]
    step = pl.program_id(0)

    @pl.when(step == 0)
    def _():
        start_copies(acts, kept, sems, me, 0)
        for ref in (probed, *grams):
            ref[...] = jnp.zeros_like(ref)

    block_copy(acts, kept, sems, me, 0, step).wait()
    add_block(panels, kept[step], probed, grams)


def probe(me, panels, acts, n, shifts):
    rows, d = acts.shape
    count = len(panels) // 2
    return call(
        functools.partial(probe_kernel, count),
        "probe",
        n,
        n // 2,
        v_specs(n, d // n, *shifts) * count + [HBM],
        (jax.ShapeDtypeStruct((K, rows), F32),) + (jax.ShapeDtypeStruct((K, K), F32),) * count,
        (whole(K, rows),) + (whole(K, K),) * count,
        acts,
    )(me, *panels, acts)


def column(row_or_matrix):
    eye = lax.broadcasted_iota(jnp.int32, (K, K), 0) == lax.broadcasted_iota(jnp.int32, (K, K), 1)
    diagonal = jnp.where(eye, row_or_matrix, 0.0)
    return jnp.sum(diagonal, axis=1, keepdims=True), jnp.sum(diagonal, axis=0, keepdims=True)


def finish_first(gram, total_weight, bounded):
    current = symmetric(gram[...])
    gram[...] = current
    norms, _ = column(current)
    return bounded(jnp.sqrt(norms), total_weight[...])


def finish_second(probed, image_image, base_image, more, total_weight, bounded):
    first, current, alpha_t, inverse, renewed, mixed, beta_t = more
    moved = outer(base_image[...], alpha_t[...])
    twice = outer(precise(alpha_t[...], symmetric(image_image[...])), alpha_t[...])
    new = symmetric(current[...] - moved - moved.T + twice)
    beta = precise(new, inverse[...])
    renewed[...] = new
    mixed[...] = current[...] - moved
    beta_t[...] = beta
    probed[...] = first[...] + precise(beta, first[...]) - precise(alpha_t[...], probed[...])
    base_col, base_row = column(current[...])
    _, image_row = column(image_image[...])
    norms = jnp.sqrt(base_col)
    norms += jnp.sum(jnp.abs(beta) * jnp.sqrt(base_row), axis=1, keepdims=True)
    norms += jnp.sum(jnp.abs(alpha_t[...]) * jnp.sqrt(image_row), axis=1, keepdims=True)
    return bounded(norms, total_weight[...])


def send_kernel(steps, count, d, me, *refs):
    panels, refs = refs[: 2 * count], refs[2 * count :]
    acts, counts, total_weight, start, refs = refs[0], refs[1], refs[2], refs[3], refs[4:]
    starts, refs = refs[:count], refs[count:]
    second = count == 2
    given, refs = refs[: 4 * second], refs[4 * second :]
    probed, along, bound, out, *refs = refs
    grams, refs = refs[:count], refs[count:]
    made, (kept, sems, weighted) = refs[: 3 * second], refs[3 * second :]
    step = pl.program_id(0)

    @pl.when(step == 0)
    def _():
        start_copies(acts, kept, sems, me, 1)
        for ref, begin in zip((probed, *grams), (start, *starts)):
            ref[...] = begin[...]

    @pl.when(step < steps)
    def _():
        block_copy(acts, kept, sems, me, 1, step).wait()
        add_block(panels, kept[step], probed, grams)

    @pl.when(step == steps)
    def _():
        def bounded(norms, weight):
            return (1.02 * BOUND * BOUND * d**0.5) * weight * norms

        if second:
            bound[...] = finish_second(probed, *grams, (*given, *made), total_weight, bounded)
        else:
            bound[...] = finish_first(*grams, total_weight, bounded)
        weighted[...] = (counts[...].astype(F32) * probed[...]).astype(BF16)
        along[...] = outer(probed[...], weighted[...].astype(F32))

    @pl.when(step >= steps)
    def _():
        out[0] = jnp.dot(weighted[...], kept[step - steps], preferred_element_type=F32)


def probe_and_send(me, panels, acts, counts, total_weight, starts, given, n, shifts):
    rows, d = acts.shape
    f = d // n
    s = n // 2
    count = len(panels) // 2
    square = jax.ShapeDtypeStruct((K, K), F32)
    made = 3 if given else 0
    return call(
        functools.partial(send_kernel, s, count, d),
        "probe_and_send",
        n,
        2 * s,
        v_specs(n, f, *shifts) * count
        + [HBM, whole(1, rows), whole(1, 1)]
        + [whole(*x.shape) for x in (*starts, *given)],
        (
            jax.ShapeDtypeStruct((K, rows), F32),
            square,
            jax.ShapeDtypeStruct((K, 1), F32),
            jax.ShapeDtypeStruct((s, K, f), F32),
        )
        + (square,) * (count + made),
        (
            whole(K, rows),
            whole(K, K),
            whole(K, 1),
            pl.BlockSpec((1, K, f), lambda i, me: (jnp.maximum(i - s, 0), 0, 0)),
        )
        + (whole(K, K),) * (count + made),
        acts,
        [pltpu.VMEM((K, rows), BF16)],
    )(me, *panels, acts, counts, total_weight, *starts, *given)


def keep_kernel(me, probed, counts, acts, out, kept, sems, weighted):
    step = pl.program_id(0)

    @pl.when(step == 0)
    def _():
        start_copies(acts, kept, sems, me, 0)
        weighted[...] = (counts[...].astype(F32) * probed[...]).astype(BF16)

    block_copy(acts, kept, sems, me, 0, step).wait()
    out[0] = jnp.dot(weighted[...], kept[step], preferred_element_type=F32)


def panel_keep(me, probed, counts, acts, n):
    rows, d = acts.shape
    f = d // n
    return call(
        keep_kernel,
        "panel_keep",
        n,
        n // 2,
        [whole(K, rows), whole(1, rows), HBM],
        jax.ShapeDtypeStruct((n // 2, K, f), F32),
        pl.BlockSpec((1, K, f), lambda i, me: (i, 0, 0)),
        acts,
        [pltpu.VMEM((K, rows), BF16)],
    )(me, probed, counts, acts)


def alpha_kernel(along, current, total_weight, alpha_t, inverse):
    now = current[...]
    curvature = (along[...] - precise(now, now)) / total_weight[...] + RIDGE * now
    eye = lax.broadcasted_iota(jnp.int32, (K, K), 0) == lax.broadcasted_iota(jnp.int32, (K, K), 1)
    alpha_t[...] = solve_positive(symmetric(curvature), now).T
    inverse[...] = symmetric(solve_positive(now, jnp.where(eye, 1.0, 0.0)))


def last_kernel(along, current, renewed, mixed, beta_t, alpha_t, total_weight, on_base, on_image, on_panel, out_base, out_image):
    now, beta, alpha, weight = current[...], beta_t[...], alpha_t[...], total_weight[...]
    cross = mixed[...] + outer(now, beta)
    half = outer(mixed[...].T, beta)
    length = renewed[...] + half + precise(beta, cross)
    cross_t = cross.T
    curvature = (along[...] - outer(cross_t, cross_t)) / weight + RIDGE * length
    step = solve_positive(symmetric(curvature), renewed[...]).T
    eye = lax.broadcasted_iota(jnp.int32, (K, K), 0) == lax.broadcasted_iota(jnp.int32, (K, K), 1)
    identity = jnp.where(eye, 1.0, 0.0)
    direction_base = precise(step, identity + beta)
    direction_image = precise(step, alpha)
    out_base[...] = alpha + direction_base
    out_image[...] = -direction_image
    on_base[...] = identity - RIDGE * direction_base + precise(step, cross_t) / weight
    on_image[...] = RIDGE * direction_image - alpha
    on_panel[...] = step / weight


def small(kernel, name, outs, *args):
    return pl.pallas_call(
        kernel, out_shape=(jax.ShapeDtypeStruct((K, K), F32),) * outs, name=name,
        cost_estimate=pl.CostEstimate(flops=1 << 26, bytes_accessed=1 << 20, transcendentals=0),
    )(*args)


def shrink(value, bound):
    return (value * (TOP / jnp.maximum(bound, TINY))).astype(F16)


def grow(value, bound):
    return value.astype(F32) * (jnp.maximum(bound, TINY) * (1.0 / TOP))


def split_blocks(value, left, bit):
    axis = left.index(bit)
    keep = lax.index_in_dim(value, 0, axis, keepdims=False)
    send = lax.index_in_dim(value, 1, axis, keepdims=False)
    return keep, send, [other for other in left if other != bit]


def reduce_scatter(blocks, n, swap_a, swap_b, along=None):
    bits = n.bit_length() - 2
    shape = (2,) * bits + (HALF, blocks.shape[2])
    a, b = blocks[:, :HALF].reshape(shape), blocks[:, HALF:].reshape(shape)
    left_a = left_b = [1 << i for i in range(bits, 0, -1)]
    for bit_a, bit_b in zip(*hop_bits(n)):
        keep_a, send_a, left_a = split_blocks(a, left_a, bit_a)
        keep_b, send_b, left_b = split_blocks(b, left_b, bit_b)
        a, b = keep_a + swap_a(send_a, bit_a), keep_b + swap_b(send_b, bit_b)
        if along is not None:
            along = along + swap(along, bit_a, n)
    return jnp.concatenate([a, b], axis=0), along


class Packed:
    def __init__(self, n, bound, weight):
        self.n, self.bound, self.weight = n, bound, weight

    def __call__(self, send, bit):
        f = send.shape[-1]
        power = jnp.ceil(jnp.log2(jnp.maximum(self.bound, TINY)))
        value = (send * jnp.exp2(15.0 - power)).astype(F16).reshape(-1, f)
        row = lax.broadcasted_iota(jnp.int32, (16, f), 0)
        tail = jnp.where(row == 0, power, 0.0)
        if self.weight is not None:
            high = jnp.floor(self.weight * (1.0 / 1024.0))
            low = self.weight - 1024.0 * high
            tail = jnp.where(row == 1, _widen(high, f), jnp.where(row == 2, _widen(low, f), tail))
        got = swap(jnp.concatenate([value, tail.astype(F16)], axis=0), bit, self.n)
        count = value.shape[0]
        theirs = got[count : count + 1, :1].astype(F32)
        if self.weight is not None:
            other = got[count + 1 : count + 3, :K].astype(F32)
            self.weight = self.weight + (1024.0 * other[:1] + other[1:])
        self.bound = 1.001 * (self.bound + jnp.exp2(theirs))
        return got[:count].reshape(send.shape).astype(F32) * jnp.exp2(theirs - 15.0)


def _widen(row, f):
    return row if f == K else jnp.pad(row, ((0, 0), (0, f - K)))


def gather_stream(block, order, n):
    value = block[None]
    for bit in order:
        value = jnp.concatenate([value, swap(value, bit, n)], axis=0)
    return value


def per_device(n, activations, labels, counts):
    rows, d = activations.shape
    activations = pltpu.with_memory_space_constraint(activations, pltpu.HBM)
    me = lax.axis_index("dp").astype(jnp.int32).reshape(1)
    labels = labels.reshape(1, rows)
    counts = counts.reshape(1, rows)
    order_y, order_z = hop_bits(n)
    order_a, order_b = order_y[::-1], order_z
    shifts = [[bit.bit_length() - 1 for bit in order] for order in (order_a, order_b)]

    sent, peak_sent, weight = class_sums(me, labels, counts, activations, n, 1)
    core = Packed(n, peak_sent, weight.T)
    got = core(sent, 1)
    kept, peak, _ = class_sums(me, labels, counts, activations, n, 0)
    bound = 1.001 * (peak + core.bound)
    stream = Packed(n, bound, core.weight)
    sums, _ = reduce_scatter(kept + got, n, stream, Packed(n, bound, None))
    class_weight = stream.weight.T
    total_weight = jnp.sum(class_weight, keepdims=True)
    base = (sums / class_weight) * jnp.sqrt(class_weight)

    def gather(panel):
        v = panel.astype(BF16)
        near = gather_stream(v[:HALF], order_a, n), gather_stream(v[HALF:], order_b, n)
        return near, tuple(swap(x, 1, n) for x in near)

    def scatter(probed, along, bound, sent):
        got = grow(swap(shrink(sent, bound), 1, n), bound)
        along = along + swap(along, 1, n)
        blocks = panel_keep(me, probed, counts, activations, n) + got
        top, low = bound[:HALF], bound[HALF:]
        return reduce_scatter(
            blocks,
            n,
            lambda x, bit: grow(swap(shrink(x, top), bit, n), top),
            lambda x, bit: grow(swap(shrink(x, low), bit, n), low),
            along,
        )

    base_near, base_far = gather(base)
    starts = probe(me, base_near, activations, n, shifts)
    first, along, bound, sent, current = probe_and_send(
        me, base_far, activations, counts, total_weight, starts, (), n, shifts
    )
    panel, along = scatter(first, along, bound, sent)
    image = panel / total_weight + (RIDGE * base - precise(current / total_weight, base))
    alpha_t, inverse = small(alpha_kernel, "alpha", 2, along, current, total_weight)

    near, far = gather(image)
    starts = probe(me, near + base_near, activations, n, shifts)
    probed, along, bound, sent, _, _, renewed, mixed, beta_t = probe_and_send(
        me, far + base_far, activations, counts, total_weight, starts, (first, current, alpha_t, inverse), n, shifts
    )
    panel, along = scatter(probed, along, bound, sent)
    on_base, on_image, on_panel, out_base, out_image = small(
        last_kernel, "last", 5, along, current, renewed, mixed, beta_t, alpha_t, total_weight
    )
    solution = precise(out_base, base) + precise(out_image, image)
    residual = (precise(on_base, base) + precise(on_image, image)) - precise(on_panel, panel)
    return (solution.T, residual.T)


def solution(mesh):
    in_specs = (P(("groups", "dp"), None), P(("groups", "dp")), P(("groups", "dp")))
    out_specs = (P(("groups", "dp"), None), P(("groups", "dp"), None))
    return jax.shard_map(
        functools.partial(per_device, mesh.shape["dp"]),
        mesh=mesh,
        in_specs=in_specs,
        out_specs=out_specs,
        check_vma=False,
    )
```

```python
import functools

import jax
import jax.numpy as jnp
from jax import lax
from jax.experimental import pallas as pl
from jax.experimental.pallas import tpu as pltpu
from jax.sharding import PartitionSpec as P

K = 64
HALF = K // 2
RIDGE = 0.1
BOUND = 18.0
TOP = 60000.0
TINY = 1e-30
F32, BF16, F16 = jnp.float32, jnp.bfloat16, jnp.float16


def precise(left, right):
    return jnp.dot(left, right, precision=lax.Precision.HIGHEST, preferred_element_type=F32)


def outer(left, right):
    return lax.dot_general(
        left, right, (((1,), (1,)), ((), ())), precision=lax.Precision.HIGHEST, preferred_element_type=F32
    )


def symmetric(matrix):
    return 0.5 * (matrix + matrix.T)


def solve_positive(*works):
    index = lax.broadcasted_iota(jnp.int32, (K, 1), 0)
    works = list(works)
    for k in range(0, K, 2):
        for i, work in enumerate(works):
            a, b = work[k : k + 1], work[k + 1 : k + 2]
            col_a, col_b = work[:, k : k + 1], work[:, k + 1 : k + 2]
            p, q = work[k : k + 1, k : k + 1], work[k : k + 1, k + 1 : k + 2]
            t, r = work[k + 1 : k + 2, k : k + 1], work[k + 1 : k + 2, k + 1 : k + 2]
            inv = 1.0 / (p * r - q * t)
            new_a, new_b = (r * a - q * b) * inv, (p * b - t * a) * inv
            rest = work - (col_a * new_a + col_b * new_b)
            works[i] = jnp.where(index == k, new_a, jnp.where(index == k + 1, new_b, rest))
    return [work[:, K:] for work in works]


def beside(matrix, target):
    return jnp.concatenate([matrix, target], axis=1)


def identity():
    eye = lax.broadcasted_iota(jnp.int32, (K, K), 0) == lax.broadcasted_iota(jnp.int32, (K, K), 1)
    return jnp.where(eye, 1.0, 0.0)


def swap(value, bit, n):
    return lax.ppermute(value, "dp", [(i, i ^ bit) for i in range(n)])


def hop_bits(n):
    bits = [1 << i for i in range(1, n.bit_length() - 1)]
    return bits, bits[1:] + bits[:1]


def _pos(j, shifts):
    p = 0
    for place, shift in enumerate(shifts):
        p = p | (((j >> shift) & 1) << place)
    return p


def block_copy(acts, kept, sems, me, half, t):
    f = kept.shape[2]
    first = pl.multiple_of((me[0] ^ (2 * t + half)) * f, f)
    return pltpu.make_async_copy(acts.at[:, pl.ds(first, f)], kept.at[t], sems.at[t])


def start_copies(acts, kept, sems, me, half):
    def start(t, carry):
        block_copy(acts, kept, sems, me, half, t).start()
        return carry

    lax.fori_loop(0, kept.shape[0], start, 0)


def whole(*shape):
    return pl.BlockSpec(shape, lambda i, me: (0,) * len(shape))


HBM = pl.BlockSpec(memory_space=pltpu.HBM)


def call(kernel, name, n, grid, in_specs, out_shapes, out_specs, acts, scratch=()):
    rows, d = acts.shape
    return pl.pallas_call(
        kernel,
        out_shape=out_shapes,
        grid_spec=pltpu.PrefetchScalarGridSpec(
            num_scalar_prefetch=1,
            grid=(grid,),
            in_specs=in_specs,
            out_specs=out_specs,
            scratch_shapes=[
                pltpu.VMEM((n // 2, rows, d // n), BF16),
                pltpu.SemaphoreType.DMA((n // 2,)),
                *scratch,
            ],
        ),
        compiler_params=pltpu.CompilerParams(vmem_limit_bytes=16 << 20),
        cost_estimate=pl.CostEstimate(flops=K * rows * d, bytes_accessed=rows * d + 2 * K * d, transcendentals=0),
        name=name,
    )


def sums_kernel(half, me, labels, counts, acts, out, weight, kept, sems, member):
    step = pl.program_id(0)

    @pl.when(step == 0)
    def _():
        start_copies(acts, kept, sems, me, half)
        concept = lax.broadcasted_iota(jnp.int32, member.shape, 0)
        full = jnp.where(labels[...] == concept, counts[...].astype(F32), 0.0)
        member[...] = full.astype(BF16)
        weight[...] = jnp.sum(full, axis=1, keepdims=True)

    block_copy(acts, kept, sems, me, half, step).wait()
    out[0] = jnp.dot(member[...], kept[step], preferred_element_type=F32)


def class_sums(me, labels, counts, acts, n, half):
    rows, d = acts.shape
    f = d // n
    return call(
        functools.partial(sums_kernel, half),
        "class_sums",
        n,
        n // 2,
        [whole(1, rows), whole(1, rows), HBM],
        (
            jax.ShapeDtypeStruct((n // 2, K, f), F32),
            jax.ShapeDtypeStruct((K, 1), F32),
        ),
        (pl.BlockSpec((1, K, f), lambda i, me: (i, 0, 0)), whole(K, 1)),
        acts,
        [pltpu.VMEM((K, rows), BF16)],
    )(me, labels, counts, acts)


def inner(left, right):
    return lax.dot_general(left, right, (((1,), (1,)), ((), ())), preferred_element_type=F32)


def v_specs(n, f, shifts_a, shifts_b):
    s = n // 2
    return [
        pl.BlockSpec((1, HALF, f), lambda i, me: (_pos(2 * jnp.minimum(i, s - 1), shifts_a), 0, 0)),
        pl.BlockSpec((1, HALF, f), lambda i, me: (_pos(2 * jnp.minimum(i, s - 1), shifts_b), 0, 0)),
    ]


def add_block(panels, acts, probed, grams):
    both = [jnp.concatenate([panels[i][0], panels[i + 1][0]], axis=0) for i in range(0, len(panels), 2)]
    probed[...] += inner(acts, both[0])
    for gram, other in zip(grams, both):
        gram[...] += inner(other, both[0])


def probe_kernel(count, me, *refs):
    panels, (acts, probed, *grams) = refs[: 2 * count], refs[2 * count : -2]
    kept, sems = refs[-2:]
    step = pl.program_id(0)

    @pl.when(step == 0)
    def _():
        start_copies(acts, kept, sems, me, 0)
        for ref in (probed, *grams):
            ref[...] = jnp.zeros_like(ref)

    block_copy(acts, kept, sems, me, 0, step).wait()
    add_block(panels, kept[step], probed, grams)


def probe(me, panels, acts, n, shifts):
    rows, d = acts.shape
    count = len(panels) // 2
    return call(
        functools.partial(probe_kernel, count),
        "probe",
        n,
        n // 2,
        v_specs(n, d // n, *shifts) * count + [HBM],
        (jax.ShapeDtypeStruct((rows, K), F32),) + (jax.ShapeDtypeStruct((K, K), F32),) * count,
        (whole(rows, K),) + (whole(K, K),) * count,
        acts,
    )(me, *panels, acts)


def column(row_or_matrix):
    eye = lax.broadcasted_iota(jnp.int32, (K, K), 0) == lax.broadcasted_iota(jnp.int32, (K, K), 1)
    diagonal = jnp.where(eye, row_or_matrix, 0.0)
    return jnp.sum(diagonal, axis=1, keepdims=True), jnp.sum(diagonal, axis=0, keepdims=True)


def finish_first(gram, total_weight, bounded):
    current = symmetric(gram[...])
    gram[...] = current
    norms, _ = column(current)
    return bounded(jnp.sqrt(norms), total_weight[...])


def finish_second(probed, image_image, base_image, more, total_weight, bounded):
    first, current, alpha_t, inverse, renewed, mixed, beta_t = more
    moved = outer(base_image[...], alpha_t[...])
    twice = outer(precise(alpha_t[...], symmetric(image_image[...])), alpha_t[...])
    new = symmetric(current[...] - moved - moved.T + twice)
    beta = precise(new, inverse[...])
    renewed[...] = new
    mixed[...] = current[...] - moved
    beta_t[...] = beta
    probed[...] = first[...] + precise(beta, first[...]) - precise(alpha_t[...], probed[...])
    base_col, base_row = column(current[...])
    _, image_row = column(image_image[...])
    norms = jnp.sqrt(base_col)
    norms += jnp.sum(jnp.abs(beta) * jnp.sqrt(base_row), axis=1, keepdims=True)
    norms += jnp.sum(jnp.abs(alpha_t[...]) * jnp.sqrt(image_row), axis=1, keepdims=True)
    return bounded(norms, total_weight[...])


def send_kernel(steps, count, d, me, *refs):
    panels, refs = refs[: 2 * count], refs[2 * count :]
    acts, counts, total_weight, start, refs = refs[0], refs[1], refs[2], refs[3], refs[4:]
    starts, refs = refs[:count], refs[count:]
    second = count == 2
    given, refs = refs[: 4 * second], refs[4 * second :]
    probed, along, bound, out, *refs = refs
    grams, refs = refs[:count], refs[count:]
    made, (kept, sems, weighted, sum_of) = refs[: 3 * second], refs[3 * second :]
    step = pl.program_id(0)

    @pl.when(step == 0)
    def _():
        start_copies(acts, kept, sems, me, 1)
        for ref, begin in zip((sum_of, *grams), (start, *starts)):
            ref[...] = begin[...]

    @pl.when(step < steps)
    def _():
        block_copy(acts, kept, sems, me, 1, step).wait()
        add_block(panels, kept[step], sum_of, grams)

    @pl.when(step == steps)
    def _():
        probed[...] = sum_of[...].T

        def bounded(norms, weight):
            return (1.02 * BOUND * BOUND * d**0.5) * weight * norms

        if second:
            bound[...] = finish_second(probed, *grams, (*given, *made), total_weight, bounded)
        else:
            bound[...] = finish_first(*grams, total_weight, bounded)
        weighted[...] = (counts[...].astype(F32) * probed[...]).astype(BF16)
        along[...] = outer(probed[...], weighted[...].astype(F32))

    @pl.when(step >= steps)
    def _():
        out[0] = jnp.dot(weighted[...], kept[step - steps], preferred_element_type=F32)


def probe_and_send(me, panels, acts, counts, total_weight, starts, given, n, shifts):
    rows, d = acts.shape
    f = d // n
    s = n // 2
    count = len(panels) // 2
    square = jax.ShapeDtypeStruct((K, K), F32)
    made = 3 if given else 0
    return call(
        functools.partial(send_kernel, s, count, d),
        "probe_and_send",
        n,
        2 * s,
        v_specs(n, f, *shifts) * count
        + [HBM, whole(1, rows), whole(1, 1)]
        + [whole(*x.shape) for x in (*starts, *given)],
        (
            jax.ShapeDtypeStruct((K, rows), F32),
            square,
            jax.ShapeDtypeStruct((K, 1), F32),
            jax.ShapeDtypeStruct((s, K, f), F32),
        )
        + (square,) * (count + made),
        (
            whole(K, rows),
            whole(K, K),
            whole(K, 1),
            pl.BlockSpec((1, K, f), lambda i, me: (jnp.maximum(i - s, 0), 0, 0)),
        )
        + (whole(K, K),) * (count + made),
        acts,
        [pltpu.VMEM((K, rows), BF16), pltpu.VMEM((rows, K), F32)],
    )(me, *panels, acts, counts, total_weight, *starts, *given)


def keep_kernel(me, probed, counts, acts, out, kept, sems, weighted):
    step = pl.program_id(0)

    @pl.when(step == 0)
    def _():
        start_copies(acts, kept, sems, me, 0)
        weighted[...] = (counts[...].astype(F32) * probed[...]).astype(BF16)

    block_copy(acts, kept, sems, me, 0, step).wait()
    out[0] = jnp.dot(weighted[...], kept[step], preferred_element_type=F32)


def panel_keep(me, probed, counts, acts, n):
    rows, d = acts.shape
    f = d // n
    return call(
        keep_kernel,
        "panel_keep",
        n,
        n // 2,
        [whole(K, rows), whole(1, rows), HBM],
        jax.ShapeDtypeStruct((n // 2, K, f), F32),
        pl.BlockSpec((1, K, f), lambda i, me: (i, 0, 0)),
        acts,
        [pltpu.VMEM((K, rows), BF16)],
    )(me, probed, counts, acts)


def alpha_kernel(along, current, total_weight, alpha_t, inverse):
    now = current[...]
    curvature = (along[...] - precise(now, now)) / total_weight[...] + RIDGE * now
    alpha, inv = solve_positive(beside(symmetric(curvature), now), beside(now, identity()))
    alpha_t[...] = alpha.T
    inverse[...] = symmetric(inv)


def before_kernel(current, renewed, mixed, beta_t, total_weight, fixed, cross_t):
    now, beta, weight = current[...], beta_t[...], total_weight[...]
    cross = mixed[...] + outer(now, beta)
    length = renewed[...] + outer(mixed[...].T, beta) + precise(beta, cross)
    turned = cross.T
    cross_t[...] = turned
    fixed[...] = RIDGE * length - outer(turned, turned) / weight


def last_kernel(along, fixed, cross_t, renewed, beta_t, alpha_t, total_weight, base, image, solved, rest, on_panel):
    weight = total_weight[...]
    curvature = symmetric(along[...] / weight + fixed[...])
    step = solve_positive(beside(curvature, renewed[...]))[0].T
    on_panel[...] = step / weight
    alpha = alpha_t[...]
    all_three = precise(step, jnp.concatenate([identity() + beta_t[...], alpha, cross_t[...]], axis=1))
    direction_base, direction_image = all_three[:, :K], all_three[:, K : 2 * K]
    crossed = all_three[:, 2 * K :] / weight
    both = jnp.concatenate([base[...], image[...]], axis=0)
    solved[...] = precise(beside(alpha + direction_base, -direction_image), both)
    rest[...] = precise(
        beside(identity() - RIDGE * direction_base + crossed, RIDGE * direction_image - alpha), both
    )


def small(kernel, name, outs, *args):
    return pl.pallas_call(
        kernel, out_shape=tuple(jax.ShapeDtypeStruct(shape, F32) for shape in outs), name=name,
        cost_estimate=pl.CostEstimate(flops=1 << 26, bytes_accessed=1 << 20, transcendentals=0),
    )(*args)


def shrink(value, bound):
    return (value * (TOP / jnp.maximum(bound, TINY))).astype(F16)


def grow(value, bound):
    return value.astype(F32) * (jnp.maximum(bound, TINY) * (1.0 / TOP))


def split_blocks(value, left, bit):
    axis = left.index(bit)
    keep = lax.index_in_dim(value, 0, axis, keepdims=False)
    send = lax.index_in_dim(value, 1, axis, keepdims=False)
    return keep, send, [other for other in left if other != bit]


def reduce_scatter(blocks, n, swap_a, swap_b, along):
    bits = n.bit_length() - 2
    shape = (2,) * bits + (HALF, blocks.shape[2])
    a, b = blocks[:, :HALF].reshape(shape), blocks[:, HALF:].reshape(shape)
    left_a = left_b = [1 << i for i in range(bits, 0, -1)]
    order_a, order_b = hop_bits(n)
    waiting = list(order_a)
    for bit_a, bit_b in zip(order_a, order_b):
        keep_a, send_a, left_a = split_blocks(a, left_a, bit_a)
        keep_b, send_b, left_b = split_blocks(b, left_b, bit_b)
        send_a, send_b, along = lax.optimization_barrier((send_a, send_b, along))
        a, b = keep_a + swap_a(send_a, bit_a), keep_b + swap_b(send_b, bit_b)
        for bit in waiting[:2]:
            along = along + swap(along, bit, n)
        waiting = waiting[2:]
    return a, b, along


class Root:
    def __init__(self, n, bound):
        self.n, self.scale = n, TOP / bound**0.5

    def __call__(self, send, bit):
        root = jnp.sqrt(jnp.abs(send)) * self.scale
        got = swap(jnp.where(send < 0, -root, root).astype(F16), bit, self.n).astype(F32)
        return got * jnp.abs(got) * (1.0 / self.scale**2)


def gather_stream(block, order, n):
    value = block[None]
    for bit in order:
        value = jnp.concatenate([value, swap(value, bit, n)], axis=0)
    return value


def per_device(n, activations, labels, counts):
    rows, d = activations.shape
    activations = pltpu.with_memory_space_constraint(activations, pltpu.HBM)
    me = lax.axis_index("dp").astype(jnp.int32).reshape(1)
    labels = labels.reshape(1, rows)
    counts = counts.reshape(1, rows)
    order_y, order_z = hop_bits(n)
    order_a, order_b = order_y[::-1], order_z
    shifts = [[bit.bit_length() - 1 for bit in order] for order in (order_a, order_b)]

    root = Root(n, BOUND * 4 * rows * n)
    sent, weight = class_sums(me, labels, counts, activations, n, 1)
    weight = weight.T
    got = root(sent, 1)
    weight = weight + swap(weight, 1, n)
    kept, _ = class_sums(me, labels, counts, activations, n, 0)
    top, low, weight = reduce_scatter(kept + got, n, root, root, weight)
    class_weight = weight.T
    total_weight = jnp.sum(class_weight, keepdims=True)
    base = (jnp.concatenate([top, low], axis=0) / class_weight) * jnp.sqrt(class_weight)

    def gather(panel):
        v = panel.astype(BF16)
        near = gather_stream(v[:HALF], order_a, n), gather_stream(v[HALF:], order_b, n)
        return near, tuple(swap(x, 1, n) for x in near)

    def scatter(probed, along, bound, sent):
        got = grow(swap(shrink(sent, bound), 1, n), bound)
        along = along + swap(along, 1, n)
        blocks = panel_keep(me, probed, counts, activations, n) + got
        top, low = bound[:HALF], bound[HALF:]
        a, b, along = reduce_scatter(
            blocks,
            n,
            lambda x, bit: grow(swap(shrink(x, top), bit, n), top),
            lambda x, bit: grow(swap(shrink(x, low), bit, n), low),
            along,
        )
        return jnp.concatenate([a, b], axis=0), along

    square, strip = (K, K), (K, d // n)
    base_near, base_far = gather(base)
    starts = probe(me, base_near, activations, n, shifts)
    first, along, bound, sent, current = probe_and_send(
        me, base_far, activations, counts, total_weight, starts, (), n, shifts
    )
    panel, along = scatter(first, along, bound, sent)
    image = panel / total_weight + (RIDGE * base - precise(current / total_weight, base))
    alpha_t, inverse = small(alpha_kernel, "alpha", (square,) * 2, along, current, total_weight)

    near, far = gather(image)
    starts = probe(me, near + base_near, activations, n, shifts)
    probed, along, bound, sent, _, _, renewed, mixed, beta_t = probe_and_send(
        me, far + base_far, activations, counts, total_weight, starts, (first, current, alpha_t, inverse), n, shifts
    )
    fixed, cross_t = small(before_kernel, "before", (square,) * 2, current, renewed, mixed, beta_t, total_weight)
    panel, along = scatter(probed, along, bound, sent)
    solved, rest, on_panel = small(
        last_kernel, "last", (strip, strip, square),
        along, fixed, cross_t, renewed, beta_t, alpha_t, total_weight, base, image,
    )
    residual = rest - precise(on_panel, panel)
    return (solved.T, residual.T)


def solution(mesh):
    in_specs = (P(("groups", "dp"), None), P(("groups", "dp")), P(("groups", "dp")))
    out_specs = (P(("groups", "dp"), None), P(("groups", "dp"), None))
    return jax.shard_map(
        functools.partial(per_device, mesh.shape["dp"]),
        mesh=mesh,
        in_specs=in_specs,
        out_specs=out_specs,
        check_vma=False,
    )
```

```python
import functools

import jax
import jax.numpy as jnp
from jax import lax
from jax.experimental import pallas as pl
from jax.experimental.pallas import tpu as pltpu
from jax.sharding import PartitionSpec as P

K = 64
HALF = K // 2
RIDGE = 0.1
BOUND = 18.0
TOP = 60000.0
TINY = 1e-30
UNROLL = 4
F32, BF16, F16 = jnp.float32, jnp.bfloat16, jnp.float16


def precise(left, right):
    return jnp.dot(left, right, precision=lax.Precision.HIGHEST, preferred_element_type=F32)


def outer(left, right):
    return lax.dot_general(
        left, right, (((1,), (1,)), ((), ())), precision=lax.Precision.HIGHEST, preferred_element_type=F32
    )


def symmetric(matrix):
    return 0.5 * (matrix + matrix.T)


def solve_positive(*works):
    index = lax.broadcasted_iota(jnp.int32, (K, 1), 0)
    works = list(works)
    for first in range(0, K, 8):
        spread = [[jnp.broadcast_to(w[:, first + j : first + j + 1], w.shape) for j in range(8)] for w in works]
        for k in range(8):
            at = slice(first + k, first + k + 1)
            row = index == first + k
            for i, columns in enumerate(spread):
                column, inv = columns[k], 1.0 / columns[k][at]
                scaled = works[i][at] * inv
                works[i] = jnp.where(row, scaled, works[i] - column * scaled)
                for j in range(k + 1, 8):
                    scaled = columns[j][at] * inv
                    columns[j] = jnp.where(row, scaled, columns[j] - column * scaled)
    return [work[:, K:] for work in works]


def beside(matrix, target):
    return jnp.concatenate([matrix, target], axis=1)


def identity():
    eye = lax.broadcasted_iota(jnp.int32, (K, K), 0) == lax.broadcasted_iota(jnp.int32, (K, K), 1)
    return jnp.where(eye, 1.0, 0.0)


def swap(value, bit, n):
    return lax.ppermute(value, "dp", [(i, i ^ bit) for i in range(n)])


def hop_bits(n):
    bits = [1 << i for i in range(1, n.bit_length() - 1)]
    return bits, bits[1:] + bits[:1]


def _pos(j, shifts):
    p = 0
    for place, shift in enumerate(shifts):
        p = p | (((j >> shift) & 1) << place)
    return p


def block_copy(acts, kept, sems, me, half, t):
    f = kept.shape[2]
    first = pl.multiple_of((me[0] ^ (2 * t + half)) * f, f)
    return pltpu.make_async_copy(acts.at[:, pl.ds(first, f)], kept.at[t], sems.at[t])


def start_copies(acts, kept, sems, me, half):
    def start(t, carry):
        block_copy(acts, kept, sems, me, half, t).start()
        return carry

    lax.fori_loop(0, kept.shape[0], start, 0)


def whole(*shape):
    return pl.BlockSpec(shape, lambda i, me: (0,) * len(shape))


HBM = pl.BlockSpec(memory_space=pltpu.HBM)


def call(kernel, name, n, grid, in_specs, out_shapes, out_specs, acts, scratch=()):
    rows, d = acts.shape
    return pl.pallas_call(
        kernel,
        out_shape=out_shapes,
        grid_spec=pltpu.PrefetchScalarGridSpec(
            num_scalar_prefetch=1,
            grid=(grid,),
            in_specs=in_specs,
            out_specs=out_specs,
            scratch_shapes=[
                pltpu.VMEM((n // 2, rows, d // n), BF16),
                pltpu.SemaphoreType.DMA((n // 2,)),
                *scratch,
            ],
        ),
        compiler_params=pltpu.CompilerParams(vmem_limit_bytes=20 << 20),
        cost_estimate=pl.CostEstimate(flops=K * rows * d, bytes_accessed=rows * d + 2 * K * d, transcendentals=0),
        name=name,
    )


def sums_kernel(half, me, labels, counts, acts, out, weight, kept, sems, member):
    step = pl.program_id(0)

    @pl.when(step == 0)
    def _():
        start_copies(acts, kept, sems, me, half)
        concept = lax.broadcasted_iota(jnp.int32, member.shape, 0)
        full = jnp.where(labels[...] == concept, counts[...].astype(F32), 0.0)
        member[...] = full.astype(BF16)
        weight[...] = jnp.sum(full, axis=1, keepdims=True)

    for u in range(UNROLL):
        t = step * UNROLL + u
        block_copy(acts, kept, sems, me, half, t).wait()
        out[u] = jnp.dot(member[...], kept[t], preferred_element_type=F32)


def class_sums(me, labels, counts, acts, n, half):
    rows, d = acts.shape
    f = d // n
    return call(
        functools.partial(sums_kernel, half),
        "class_sums",
        n,
        n // 2 // UNROLL,
        [whole(1, rows), whole(1, rows), HBM],
        (
            jax.ShapeDtypeStruct((n // 2, K, f), F32),
            jax.ShapeDtypeStruct((K, 1), F32),
        ),
        (pl.BlockSpec((UNROLL, K, f), lambda i, me: (i, 0, 0)), whole(K, 1)),
        acts,
        [pltpu.VMEM((K, rows), BF16)],
    )(me, labels, counts, acts)


def inner(left, right):
    return lax.dot_general(left, right, (((1,), (1,)), ((), ())), preferred_element_type=F32)


def panel_operands(panels, n, f, shifts):
    last = n // 2 // UNROLL - 1
    specs, operands = [], []
    for panel in panels:
        for u in range(UNROLL):
            for stream, order in zip(panel, shifts):
                pick = lambda i, me, u=u, order=order: (_pos(2 * (jnp.minimum(i, last) * UNROLL + u), order), 0, 0)
                specs.append(pl.BlockSpec((1, HALF, f), pick))
                operands.append(stream)
    return specs, operands


def add_blocks(refs, count, block, probed, grams):
    total = probed[...]
    sums = [gram[...] for gram in grams]
    for u in range(UNROLL):
        at = [2 * (panel * UNROLL + u) for panel in range(count)]
        both = [jnp.concatenate([refs[i][0], refs[i + 1][0]], axis=0) for i in at]
        total = total + inner(block(u), both[0])
        sums = [x + inner(other, both[0]) for x, other in zip(sums, both)]
    probed[...] = total
    for gram, x in zip(grams, sums):
        gram[...] = x


def probe_kernel(count, me, *refs):
    panels, refs = refs[: 2 * UNROLL * count], refs[2 * UNROLL * count :]
    acts, probed, *grams, kept, sems = refs
    step = pl.program_id(0)

    @pl.when(step == 0)
    def _():
        start_copies(acts, kept, sems, me, 0)
        for ref in (probed, *grams):
            ref[...] = jnp.zeros_like(ref)

    def block(u):
        block_copy(acts, kept, sems, me, 0, step * UNROLL + u).wait()
        return kept[step * UNROLL + u]

    add_blocks(panels, count, block, probed, grams)


def probe(me, panels, acts, n, shifts):
    rows, d = acts.shape
    count = len(panels)
    specs, operands = panel_operands(panels, n, d // n, shifts)
    return call(
        functools.partial(probe_kernel, count),
        "probe",
        n,
        n // 2 // UNROLL,
        specs + [HBM],
        (jax.ShapeDtypeStruct((rows, K), F32),) + (jax.ShapeDtypeStruct((K, K), F32),) * count,
        (whole(rows, K),) + (whole(K, K),) * count,
        acts,
    )(me, *operands, acts)


def diagonal(matrix):
    kept = matrix * identity()
    return jnp.sum(kept, axis=1, keepdims=True), jnp.sum(kept, axis=0, keepdims=True)


def finish_first(gram):
    current = symmetric(gram[...])
    gram[...] = current
    return jnp.sqrt(diagonal(current)[0])


def finish_second(probed, image_image, base_image, more):
    first, current, alpha_t, inverse, renewed, mixed, beta_t = more
    both = jnp.concatenate([base_image[...], symmetric(image_image[...])], axis=0)
    moved = outer(both, alpha_t[...])
    moved, twice = moved[:K], precise(alpha_t[...], moved[K:])
    new = symmetric(current[...] - moved - moved.T + twice)
    beta = precise(new, inverse[...])
    renewed[...] = new
    mixed[...] = current[...] - moved
    beta_t[...] = beta
    mix = jnp.concatenate([beta, -alpha_t[...]], axis=1)
    probed[...] = first[...] + precise(mix, jnp.concatenate([first[...], probed[...]], axis=0))
    base_col, base_row = diagonal(current[...])
    _, image_row = diagonal(image_image[...])
    norms = jnp.sqrt(base_col)
    norms += jnp.sum(jnp.abs(beta) * jnp.sqrt(base_row), axis=1, keepdims=True)
    return norms + jnp.sum(jnp.abs(alpha_t[...]) * jnp.sqrt(image_row), axis=1, keepdims=True)


def send_kernel(steps, count, d, me, *refs):
    second = count == 2
    parts = [2 * UNROLL * count, 4, count, 4 * second, 4, count, 3 * second, 4]
    refs = list(refs)
    panels, ins, starts, given, outs, grams, made, scratch = (
        [refs.pop(0) for _ in range(size)] for size in parts
    )
    acts, counts, total_weight, start = ins
    probed, along, bound, out = outs
    kept, sems, weighted, sum_of = scratch
    step = pl.program_id(0)

    @pl.when(step == 0)
    def _():
        start_copies(acts, kept, sems, me, 1)
        for ref, begin in zip((sum_of, *grams), (start, *starts)):
            ref[...] = begin[...]

    @pl.when(step < steps)
    def _():
        def block(u):
            block_copy(acts, kept, sems, me, 1, step * UNROLL + u).wait()
            return kept[step * UNROLL + u]

        add_blocks(panels, count, block, sum_of, grams)

    @pl.when(step == steps)
    def _():
        probed[...] = sum_of[...].T
        norms = finish_second(probed, *grams, (*given, *made)) if second else finish_first(*grams)
        bound[...] = (1.02 * BOUND * BOUND * d**0.5) * total_weight[...] * norms
        weighted[...] = (counts[...].astype(F32) * probed[...]).astype(BF16)
        along[...] = outer(probed[...], weighted[...].astype(F32))

    @pl.when(step >= steps)
    def _():
        for u in range(UNROLL):
            out[u] = jnp.dot(weighted[...], kept[(step - steps) * UNROLL + u], preferred_element_type=F32)


def probe_and_send(me, panels, acts, counts, total_weight, starts, given, n, shifts):
    rows, d = acts.shape
    f = d // n
    s = n // 2 // UNROLL
    count = len(panels)
    square = jax.ShapeDtypeStruct((K, K), F32)
    made = 3 if given else 0
    specs, operands = panel_operands(panels, n, f, shifts)
    return call(
        functools.partial(send_kernel, s, count, d),
        "probe_and_send",
        n,
        2 * s,
        specs + [HBM, whole(1, rows), whole(1, 1)] + [whole(*x.shape) for x in (*starts, *given)],
        (
            jax.ShapeDtypeStruct((K, rows), F32),
            square,
            jax.ShapeDtypeStruct((K, 1), F32),
            jax.ShapeDtypeStruct((n // 2, K, f), F32),
        )
        + (square,) * (count + made),
        (
            whole(K, rows),
            whole(K, K),
            whole(K, 1),
            pl.BlockSpec((UNROLL, K, f), lambda i, me: (jnp.maximum(i - s, 0), 0, 0)),
        )
        + (whole(K, K),) * (count + made),
        acts,
        [pltpu.VMEM((K, rows), BF16), pltpu.VMEM((rows, K), F32)],
    )(me, *operands, acts, counts, total_weight, *starts, *given)


def keep_kernel(me, probed, counts, acts, out, kept, sems, weighted):
    step = pl.program_id(0)

    @pl.when(step == 0)
    def _():
        start_copies(acts, kept, sems, me, 0)
        weighted[...] = (counts[...].astype(F32) * probed[...]).astype(BF16)

    for u in range(UNROLL):
        t = step * UNROLL + u
        block_copy(acts, kept, sems, me, 0, t).wait()
        out[u] = jnp.dot(weighted[...], kept[t], preferred_element_type=F32)


def panel_keep(me, probed, counts, acts, n):
    rows, d = acts.shape
    f = d // n
    return call(
        keep_kernel,
        "panel_keep",
        n,
        n // 2 // UNROLL,
        [whole(K, rows), whole(1, rows), HBM],
        jax.ShapeDtypeStruct((n // 2, K, f), F32),
        pl.BlockSpec((UNROLL, K, f), lambda i, me: (i, 0, 0)),
        acts,
        [pltpu.VMEM((K, rows), BF16)],
    )(me, probed, counts, acts)


def alpha_kernel(along, current, total_weight, alpha_t, inverse):
    now = current[...]
    curvature = (along[...] - precise(now, now)) / total_weight[...] + RIDGE * now
    alpha, inv = solve_positive(beside(symmetric(curvature), now), beside(now, identity()))
    alpha_t[...] = alpha.T
    inverse[...] = symmetric(inv)


def offset_kernel(base_a, base_b, current, total_weight, offset):
    base = jnp.concatenate([base_a[...], base_b[...]], axis=0)
    offset[...] = RIDGE * base - precise(current[...] / total_weight[...], base)


def before_kernel(current, renewed, mixed, beta_t, total_weight, fixed, cross_t):
    now, beta, weight = current[...], beta_t[...], total_weight[...]
    cross = mixed[...] + outer(now, beta)
    length = renewed[...] + outer(mixed[...].T, beta) + precise(beta, cross)
    turned = cross.T
    cross_t[...] = turned
    fixed[...] = RIDGE * length - outer(turned, turned) / weight


def last_kernel(
    along, fixed, cross_t, renewed, beta_t, alpha_t, total_weight, base_a, base_b, image_a, image_b,
    solved, rest, on_panel,
):
    weight = total_weight[...]
    curvature = symmetric(along[...] / weight + fixed[...])
    step = solve_positive(beside(curvature, renewed[...]))[0].T
    on_panel[...] = step / weight
    alpha = alpha_t[...]
    all_three = precise(step, jnp.concatenate([identity() + beta_t[...], alpha, cross_t[...]], axis=1))
    direction_base, direction_image = all_three[:, :K], all_three[:, K : 2 * K]
    crossed = all_three[:, 2 * K :] / weight
    both = jnp.concatenate([base_a[...], base_b[...], image_a[...], image_b[...]], axis=0)
    solved[...] = precise(beside(alpha + direction_base, -direction_image), both)
    rest[...] = precise(
        beside(identity() - RIDGE * direction_base + crossed, RIDGE * direction_image - alpha), both
    )


def end_kernel(rest, on_panel, panel_a, panel_b, residual):
    panel = jnp.concatenate([panel_a[...], panel_b[...]], axis=0)
    residual[...] = rest[...] - precise(on_panel[...], panel)


def small(kernel, name, outs, *args):
    return pl.pallas_call(
        kernel, out_shape=tuple(jax.ShapeDtypeStruct(shape, F32) for shape in outs), name=name,
        cost_estimate=pl.CostEstimate(flops=1 << 26, bytes_accessed=1 << 20, transcendentals=0),
    )(*args)


def shrink(value, bound):
    return (value * (TOP / jnp.maximum(bound, TINY))).astype(F16)


def grow(value, bound):
    return value.astype(F32) * (jnp.maximum(bound, TINY) * (1.0 / TOP))


def split_blocks(value, left, bit):
    axis = left.index(bit)
    keep = lax.index_in_dim(value, 0, axis, keepdims=False)
    send = lax.index_in_dim(value, 1, axis, keepdims=False)
    return keep, send, [other for other in left if other != bit]


def reduce_scatter(blocks, n, swap_a, swap_b, along, work=None, args=()):
    bits = n.bit_length() - 2
    shape = (2,) * bits + (HALF, blocks.shape[2])
    a, b = blocks[:, :HALF].reshape(shape), blocks[:, HALF:].reshape(shape)
    left_a = left_b = [1 << i for i in range(bits, 0, -1)]
    order_a, order_b = hop_bits(n)
    waiting, done = list(order_a), ()
    for phase, (bit_a, bit_b) in enumerate(zip(order_a, order_b)):
        keep_a, send_a, left_a = split_blocks(a, left_a, bit_a)
        keep_b, send_b, left_b = split_blocks(b, left_b, bit_b)
        tied = args if phase == 1 else done
        send_a, send_b, along, tied = lax.optimization_barrier((send_a, send_b, along, tied))
        a, b = keep_a + swap_a(send_a, bit_a), keep_b + swap_b(send_b, bit_b)
        for bit in waiting[:2]:
            along = along + swap(along, bit, n)
        waiting = waiting[2:]
        if work is not None and phase >= 1:
            done = work(*tied) if phase == 1 else tied
    return a, b, along, done


class Root:
    def __init__(self, n, bound):
        self.n, self.scale = n, TOP / bound**0.5

    def __call__(self, send, bit):
        root = jnp.sqrt(jnp.abs(send)) * self.scale
        got = swap(jnp.where(send < 0, -root, root).astype(F16), bit, self.n).astype(F32)
        return got * jnp.abs(got) * (1.0 / self.scale**2)


def gather(top, low, n, orders, work=None, args=()):
    a, b = top.astype(BF16)[None], low.astype(BF16)[None]
    done = ()
    for phase, (bit_a, bit_b) in enumerate(zip(*orders)):
        if work is not None and phase >= 1:
            tied = args if phase == 1 else done
            a, b, tied = lax.optimization_barrier((a, b, tied))
            done = work(*tied) if phase == 1 else tied
        a = jnp.concatenate([a, swap(a, bit_a, n)], axis=0)
        b = jnp.concatenate([b, swap(b, bit_b, n)], axis=0)
    return (a, b), (swap(a, 1, n), swap(b, 1, n)), done


def per_device(n, activations, labels, counts):
    rows, d = activations.shape
    activations = pltpu.with_memory_space_constraint(activations, pltpu.HBM)
    me = lax.axis_index("dp").astype(jnp.int32).reshape(1)
    labels = labels.reshape(1, rows)
    counts = counts.reshape(1, rows)
    order_y, order_z = hop_bits(n)
    order_a, order_b = order_y[::-1], order_z
    shifts = [[bit.bit_length() - 1 for bit in order] for order in (order_a, order_b)]

    root = Root(n, BOUND * 4 * rows * n)
    sent, weight = class_sums(me, labels, counts, activations, n, 1)
    weight = weight.T
    got = root(sent, 1)
    weight = weight + swap(weight, 1, n)
    kept, _ = class_sums(me, labels, counts, activations, n, 0)
    top, low, weight, _ = reduce_scatter(kept + got, n, root, root, weight)
    class_weight = weight.T
    total_weight = jnp.sum(class_weight, keepdims=True)
    over, back = class_weight, jnp.sqrt(class_weight)
    base = (top / over[:HALF]) * back[:HALF], (low / over[HALF:]) * back[HALF:]

    def scatter(probed, along, bound, sent, work, args):
        got = grow(swap(shrink(sent, bound), 1, n), bound)
        along = along + swap(along, 1, n)
        blocks = panel_keep(me, probed, counts, activations, n) + got
        top, low = bound[:HALF], bound[HALF:]
        return reduce_scatter(
            blocks,
            n,
            lambda x, bit: grow(swap(shrink(x, top), bit, n), top),
            lambda x, bit: grow(swap(shrink(x, low), bit, n), low),
            along,
            work,
            args,
        )

    square, strip = (K, K), (K, d // n)
    orders = order_a, order_b
    base_near, base_far, _ = gather(*base, n, orders)
    starts = probe(me, (base_near,), activations, n, shifts)
    first, along, bound, sent, current = probe_and_send(
        me, (base_far,), activations, counts, total_weight, starts, (), n, shifts
    )
    panel_a, panel_b, along, (offset,) = scatter(
        first, along, bound, sent,
        lambda *args: small(offset_kernel, "offset", (strip,), *args), (*base, current, total_weight),
    )
    image = panel_a / total_weight + offset[:HALF], panel_b / total_weight + offset[HALF:]

    near, far, (alpha_t, inverse) = gather(
        *image, n, orders,
        lambda *args: small(alpha_kernel, "alpha", (square,) * 2, *args), (along, current, total_weight),
    )
    starts = probe(me, (near, base_near), activations, n, shifts)
    probed, along, bound, sent, _, _, renewed, mixed, beta_t = probe_and_send(
        me, (far, base_far), activations, counts, total_weight, starts, (first, current, alpha_t, inverse), n, shifts
    )
    panel_a, panel_b, along, (fixed, cross_t) = scatter(
        probed, along, bound, sent,
        lambda *args: small(before_kernel, "before", (square,) * 2, *args),
        (current, renewed, mixed, beta_t, total_weight),
    )
    solved, rest, on_panel = small(
        last_kernel, "last", (strip, strip, square),
        along, fixed, cross_t, renewed, beta_t, alpha_t, total_weight, *base, *image,
    )
    (residual,) = small(end_kernel, "end", (strip,), rest, on_panel, panel_a, panel_b)
    return (solved.T, residual.T)


def solution(mesh):
    in_specs = (P(("groups", "dp"), None), P(("groups", "dp")), P(("groups", "dp")))
    out_specs = (P(("groups", "dp"), None), P(("groups", "dp"), None))
    return jax.shard_map(
        functools.partial(per_device, mesh.shape["dp"]),
        mesh=mesh,
        in_specs=in_specs,
        out_specs=out_specs,
        check_vma=False,
    )
```

```python
import functools

import jax
import jax.numpy as jnp
from jax import lax
from jax.experimental import pallas as pl
from jax.experimental.pallas import tpu as pltpu
from jax.sharding import PartitionSpec as P

K = 64
HALF = K // 2
RIDGE = 0.1
BOUND = 18.0
TOP = 60000.0
TINY = 1e-30
UNROLL = 4
F32, BF16, F16 = jnp.float32, jnp.bfloat16, jnp.float16


def precise(left, right):
    return jnp.dot(left, right, precision=lax.Precision.HIGHEST, preferred_element_type=F32)


def outer(left, right):
    return lax.dot_general(
        left, right, (((1,), (1,)), ((), ())), precision=lax.Precision.HIGHEST, preferred_element_type=F32
    )


def symmetric(matrix):
    return 0.5 * (matrix + matrix.T)


def solve_positive(*works):
    index = lax.broadcasted_iota(jnp.int32, (K, 1), 0)
    works = list(works)
    for first in range(0, K, 8):
        spread = [[jnp.broadcast_to(w[:, first + j : first + j + 1], w.shape) for j in range(8)] for w in works]
        for k in range(8):
            at = slice(first + k, first + k + 1)
            row = index == first + k
            for i, columns in enumerate(spread):
                column, inv = columns[k], 1.0 / columns[k][at]
                scaled = works[i][at] * inv
                works[i] = jnp.where(row, scaled, works[i] - column * scaled)
                for j in range(k + 1, 8):
                    scaled = columns[j][at] * inv
                    columns[j] = jnp.where(row, scaled, columns[j] - column * scaled)
    return [work[:, K:] for work in works]


def beside(matrix, target):
    return jnp.concatenate([matrix, target], axis=1)


def identity():
    eye = lax.broadcasted_iota(jnp.int32, (K, K), 0) == lax.broadcasted_iota(jnp.int32, (K, K), 1)
    return jnp.where(eye, 1.0, 0.0)


def swap(value, bit, n):
    return lax.ppermute(value, "dp", [(i, i ^ bit) for i in range(n)])


def hop_bits(n):
    bits = [1 << i for i in range(1, n.bit_length() - 1)]
    return bits, bits[1:] + bits[:1]


def _pos(j, shifts):
    p = 0
    for place, shift in enumerate(shifts):
        p = p | (((j >> shift) & 1) << place)
    return p


def block_copy(acts, kept, sems, me, half, t):
    f = kept.shape[2]
    first = pl.multiple_of((me[0] ^ (2 * t + half)) * f, f)
    return pltpu.make_async_copy(acts.at[:, pl.ds(first, f)], kept.at[t], sems.at[t])


def start_copies(acts, kept, sems, me, half):
    def start(t, carry):
        block_copy(acts, kept, sems, me, half, t).start()
        return carry

    lax.fori_loop(0, kept.shape[0], start, 0)


def whole(*shape):
    return pl.BlockSpec(shape, lambda i, me: (0,) * len(shape))


HBM = pl.BlockSpec(memory_space=pltpu.HBM)


def call(kernel, name, n, grid, in_specs, out_shapes, out_specs, acts, scratch=(), aliases=None):
    rows, d = acts.shape
    return pl.pallas_call(
        kernel,
        out_shape=out_shapes,
        grid_spec=pltpu.PrefetchScalarGridSpec(
            num_scalar_prefetch=1,
            grid=(grid,),
            in_specs=in_specs,
            out_specs=out_specs,
            scratch_shapes=[
                pltpu.VMEM((n // 2, rows, d // n), BF16),
                pltpu.SemaphoreType.DMA((n // 2,)),
                *scratch,
            ],
        ),
        compiler_params=pltpu.CompilerParams(vmem_limit_bytes=20 << 20),
        cost_estimate=pl.CostEstimate(flops=K * rows * d, bytes_accessed=rows * d + 2 * K * d, transcendentals=0),
        input_output_aliases=aliases or {},
        name=name,
    )


def count_of(row_data):
    return lax.shift_right_logical(row_data[...], 6).astype(F32)


def sums_kernel(half, me, row_data, acts, out, weight, kept, sems, member):
    step = pl.program_id(0)

    @pl.when(step == 0)
    def _():
        start_copies(acts, kept, sems, me, half)
        concept = lax.broadcasted_iota(jnp.int32, member.shape, 0)
        label = row_data[...] & (K - 1)
        full = jnp.where(label == concept, count_of(row_data), 0.0)
        member[...] = full.astype(BF16)
        weight[...] = jnp.sum(full, axis=1, keepdims=True)

    for u in range(UNROLL):
        t = step * UNROLL + u
        block_copy(acts, kept, sems, me, half, t).wait()
        out[u] = jnp.dot(member[...], kept[t], preferred_element_type=F32)


def class_sums(me, row_data, acts, n, half):
    rows, d = acts.shape
    f = d // n
    return call(
        functools.partial(sums_kernel, half),
        "class_sums",
        n,
        n // 2 // UNROLL,
        [whole(1, rows), HBM],
        (
            jax.ShapeDtypeStruct((n // 2, K, f), F32),
            jax.ShapeDtypeStruct((K, 1), F32),
        ),
        (pl.BlockSpec((UNROLL, K, f), lambda i, me: (i, 0, 0)), whole(K, 1)),
        acts,
        [pltpu.VMEM((K, rows), BF16)],
    )(me, row_data, acts)


def inner(left, right):
    return lax.dot_general(left, right, (((1,), (1,)), ((), ())), preferred_element_type=F32)


def panel_operands(panels, n, f, shifts):
    last = n // 2 // UNROLL - 1
    specs, operands = [], []
    for panel in panels:
        for u in range(UNROLL):
            for stream, order in zip(panel, shifts):
                pick = lambda i, me, u=u, order=order: (_pos(2 * (jnp.minimum(i, last) * UNROLL + u), order), 0, 0)
                specs.append(pl.BlockSpec((1, HALF, f), pick))
                operands.append(stream)
    return specs, operands


def add_blocks(refs, count, block, probed, grams):
    total = probed[...]
    sums = [gram[...] for gram in grams]
    for u in range(UNROLL):
        at = [2 * (panel * UNROLL + u) for panel in range(count)]
        both = [jnp.concatenate([refs[i][0], refs[i + 1][0]], axis=0) for i in at]
        total = total + inner(block(u), both[0])
        sums = [x + inner(other, both[0]) for x, other in zip(sums, both)]
    probed[...] = total
    for gram, x in zip(grams, sums):
        gram[...] = x


def probe_kernel(count, me, *refs):
    panels, refs = refs[: 2 * UNROLL * count], refs[2 * UNROLL * count :]
    acts, probed, *grams, kept, sems = refs
    step = pl.program_id(0)

    @pl.when(step == 0)
    def _():
        start_copies(acts, kept, sems, me, 0)
        for ref in (probed, *grams):
            ref[...] = jnp.zeros_like(ref)

    def block(u):
        block_copy(acts, kept, sems, me, 0, step * UNROLL + u).wait()
        return kept[step * UNROLL + u]

    add_blocks(panels, count, block, probed, grams)


def probe(me, panels, acts, n, shifts):
    rows, d = acts.shape
    count = len(panels)
    specs, operands = panel_operands(panels, n, d // n, shifts)
    return call(
        functools.partial(probe_kernel, count),
        "probe",
        n,
        n // 2 // UNROLL,
        specs + [HBM],
        (jax.ShapeDtypeStruct((rows, K), F32),) + (jax.ShapeDtypeStruct((K, K), F32),) * count,
        (whole(rows, K),) + (whole(K, K),) * count,
        acts,
    )(me, *operands, acts)


def diagonal(matrix):
    kept = matrix * identity()
    return jnp.sum(kept, axis=1, keepdims=True), jnp.sum(kept, axis=0, keepdims=True)


def finish_first(gram):
    current = symmetric(gram[...])
    gram[...] = current
    return jnp.sqrt(diagonal(current)[0])


def finish_second(probed, image_image, base_image, more):
    first, current, alpha_t, inverse, renewed, mixed, beta_t = more
    both = jnp.concatenate([base_image[...], symmetric(image_image[...])], axis=0)
    moved = outer(both, alpha_t[...])
    moved, twice = moved[:K], precise(alpha_t[...], moved[K:])
    new = symmetric(current[...] - moved - moved.T + twice)
    beta = precise(new, inverse[...])
    renewed[...] = new
    mixed[...] = current[...] - moved
    beta_t[...] = beta
    mix = jnp.concatenate([beta, -alpha_t[...]], axis=1)
    probed[...] = first[...] + precise(mix, jnp.concatenate([first[...], probed[...]], axis=0))
    base_col, base_row = diagonal(current[...])
    _, image_row = diagonal(image_image[...])
    norms = jnp.sqrt(base_col)
    norms += jnp.sum(jnp.abs(beta) * jnp.sqrt(base_row), axis=1, keepdims=True)
    return norms + jnp.sum(jnp.abs(alpha_t[...]) * jnp.sqrt(image_row), axis=1, keepdims=True)


def send_kernel(steps, count, d, me, *refs):
    second = count == 2
    parts = [2 * UNROLL * count, 4, count, 4 * second, 4, count, 3 * second, 4]
    refs = list(refs)
    panels, ins, starts, given, outs, grams, made, scratch = (
        [refs.pop(0) for _ in range(size)] for size in parts
    )
    acts, row_data, total_weight, start = ins
    probed, along, bound, out = outs
    kept, sems, weighted, sum_of = scratch
    step = pl.program_id(0)

    @pl.when(step == 0)
    def _():
        start_copies(acts, kept, sems, me, 1)
        for ref, begin in zip((sum_of, *grams), (start, *starts)):
            ref[...] = begin[...]

    @pl.when(step < steps)
    def _():
        def block(u):
            block_copy(acts, kept, sems, me, 1, step * UNROLL + u).wait()
            return kept[step * UNROLL + u]

        add_blocks(panels, count, block, sum_of, grams)

    @pl.when(step == steps)
    def _():
        probed[...] = sum_of[...].T
        norms = finish_second(probed, *grams, (*given, *made)) if second else finish_first(*grams)
        bound[...] = (1.02 * BOUND * BOUND * d**0.5) * total_weight[...] * norms
        weighted[...] = (count_of(row_data) * probed[...]).astype(BF16)
        along[...] = outer(probed[...], weighted[...].astype(F32))

    @pl.when(step >= steps)
    def _():
        for u in range(UNROLL):
            out[u] = jnp.dot(weighted[...], kept[(step - steps) * UNROLL + u], preferred_element_type=F32)


def probe_and_send(me, panels, acts, row_data, total_weight, starts, given, n, shifts):
    rows, d = acts.shape
    f = d // n
    s = n // 2 // UNROLL
    count = len(panels)
    square = jax.ShapeDtypeStruct((K, K), F32)
    made = 3 if given else 0
    specs, operands = panel_operands(panels, n, f, shifts)
    return call(
        functools.partial(send_kernel, s, count, d),
        "probe_and_send",
        n,
        2 * s,
        specs + [HBM, whole(1, rows), whole(1, 1)] + [whole(*x.shape) for x in (*starts, *given)],
        (
            jax.ShapeDtypeStruct((K, rows), F32),
            square,
            jax.ShapeDtypeStruct((K, 1), F32),
            jax.ShapeDtypeStruct((n // 2, K, f), F32),
        )
        + (square,) * (count + made),
        (
            whole(K, rows),
            whole(K, K),
            whole(K, 1),
            pl.BlockSpec((UNROLL, K, f), lambda i, me: (jnp.maximum(i - s, 0), 0, 0)),
        )
        + (whole(K, K),) * (count + made),
        acts,
        [pltpu.VMEM((K, rows), BF16), pltpu.VMEM((rows, K), F32)],
    )(me, *operands, acts, row_data, total_weight, *starts, *given)


def keep_kernel(base, me, probed, row_data, acts, *refs):
    out, kept, sems, weighted = refs[-4:]
    step = pl.program_id(0)

    def copy(t):
        return block_copy(acts, kept, sems, me, 0, t)

    @pl.when(step == 0)
    def _():
        lax.fori_loop(base, base + pl.num_programs(0) * UNROLL, lambda t, c: (copy(t).start(), c)[1], 0)
        weighted[...] = (count_of(row_data) * probed[...]).astype(BF16)

    for u in range(UNROLL):
        t = base + step * UNROLL + u
        copy(t).wait()
        out[u] = jnp.dot(weighted[...], kept[t], preferred_element_type=F32)


def panel_keep(me, probed, row_data, acts, n, part=None, into=None):
    rows, d = acts.shape
    f = d // n
    steps = n // 2 // UNROLL
    first = 0
    if part is not None:
        steps //= 2
        first = part * steps
    more = () if into is None else (into,)
    return call(
        functools.partial(keep_kernel, first * UNROLL),
        "panel_keep",
        n,
        steps,
        [whole(K, rows), whole(1, rows), HBM] + [pl.BlockSpec(memory_space=pl.ANY)] * len(more),
        jax.ShapeDtypeStruct((n // 2, K, f), F32),
        pl.BlockSpec((UNROLL, K, f), lambda i, me: (i + first, 0, 0)),
        acts,
        [pltpu.VMEM((K, rows), BF16)],
        {4: 0} if more else {},
    )(me, probed, row_data, acts, *more)


def alpha_kernel(along, current, total_weight, alpha_t, inverse):
    now = current[...]
    curvature = (along[...] - precise(now, now)) / total_weight[...] + RIDGE * now
    alpha, inv = solve_positive(beside(symmetric(curvature), now), beside(now, identity()))
    alpha_t[...] = alpha.T
    inverse[...] = symmetric(inv)


def offset_kernel(base_a, base_b, current, total_weight, offset):
    base = jnp.concatenate([base_a[...], base_b[...]], axis=0)
    offset[...] = RIDGE * base - precise(current[...] / total_weight[...], base)


def before_kernel(current, renewed, mixed, beta_t, total_weight, fixed, cross_t):
    now, beta, weight = current[...], beta_t[...], total_weight[...]
    cross = mixed[...] + outer(now, beta)
    length = renewed[...] + outer(mixed[...].T, beta) + precise(beta, cross)
    turned = cross.T
    cross_t[...] = turned
    fixed[...] = RIDGE * length - outer(turned, turned) / weight


def last_kernel(
    along, fixed, cross_t, renewed, beta_t, alpha_t, total_weight, base_a, base_b, image_a, image_b,
    solved, rest, on_panel,
):
    weight = total_weight[...]
    curvature = symmetric(along[...] / weight + fixed[...])
    step = solve_positive(beside(curvature, renewed[...]))[0].T
    on_panel[...] = step / weight
    alpha = alpha_t[...]
    all_three = precise(step, jnp.concatenate([identity() + beta_t[...], alpha, cross_t[...]], axis=1))
    direction_base, direction_image = all_three[:, :K], all_three[:, K : 2 * K]
    crossed = all_three[:, 2 * K :] / weight
    both = jnp.concatenate([base_a[...], base_b[...], image_a[...], image_b[...]], axis=0)
    solved[...] = precise(beside(alpha + direction_base, -direction_image), both)
    rest[...] = precise(
        beside(identity() - RIDGE * direction_base + crossed, RIDGE * direction_image - alpha), both
    )


def end_kernel(rest, on_panel, panel_a, panel_b, residual):
    panel = jnp.concatenate([panel_a[...], panel_b[...]], axis=0)
    residual[...] = rest[...] - precise(on_panel[...], panel)


def small(kernel, name, outs, *args):
    return pl.pallas_call(
        kernel, out_shape=tuple(jax.ShapeDtypeStruct(shape, F32) for shape in outs), name=name,
        cost_estimate=pl.CostEstimate(flops=1 << 26, bytes_accessed=1 << 20, transcendentals=0),
    )(*args)


def shrink(value, bound):
    return (value * (TOP / jnp.maximum(bound, TINY))).astype(F16)


def grow(value, bound):
    return value.astype(F32) * (jnp.maximum(bound, TINY) * (1.0 / TOP))


def split_blocks(value, left, bit):
    axis = left.index(bit)
    keep = lax.index_in_dim(value, 0, axis, keepdims=False)
    send = lax.index_in_dim(value, 1, axis, keepdims=False)
    return keep, send, [other for other in left if other != bit]


def reduce_scatter(blocks, n, swap_a, swap_b, along, waiting, work=None, args=()):
    bits = n.bit_length() - 2
    shape = (2,) * bits + (HALF, blocks.shape[2])
    a, b = blocks[:, :HALF].reshape(shape), blocks[:, HALF:].reshape(shape)
    left_a = left_b = [1 << i for i in range(bits, 0, -1)]
    order_a, order_b = hop_bits(n)
    waiting, done = list(waiting), ()
    for phase, (bit_a, bit_b) in enumerate(zip(order_a, order_b)):
        keep_a, send_a, left_a = split_blocks(a, left_a, bit_a)
        keep_b, send_b, left_b = split_blocks(b, left_b, bit_b)
        tied = args if phase == 1 else done
        send_a, send_b, along, tied = lax.optimization_barrier((send_a, send_b, along, tied))
        a, b = keep_a + swap_a(send_a, bit_a), keep_b + swap_b(send_b, bit_b)
        if waiting:
            along = along + swap(along, waiting.pop(0), n)
        if work is not None and phase >= 1:
            done = work(*tied) if phase == 1 else tied
    return a, b, along, done


class Root:
    def __init__(self, n, bound):
        self.n, self.scale = n, TOP / bound**0.5

    def __call__(self, send, bit):
        root = jnp.sqrt(jnp.abs(send)) * self.scale
        got = swap(jnp.where(send < 0, -root, root).astype(F16), bit, self.n).astype(F32)
        return got * jnp.abs(got) * (1.0 / self.scale**2)


def gather(top, low, n, orders, work=None, args=()):
    a, b = top.astype(BF16)[None], low.astype(BF16)[None]
    done = ()
    for phase, (bit_a, bit_b) in enumerate(zip(*orders)):
        tied = args if phase == 1 else done
        a, b, tied = lax.optimization_barrier((a, b, tied))
        if work is not None and phase >= 1:
            done = work(*tied) if phase == 1 else tied
        a = jnp.concatenate([a, swap(a, bit_a, n)], axis=0)
        b = jnp.concatenate([b, swap(b, bit_b, n)], axis=0)
    return (a, b), (swap(a, 1, n), swap(b, 1, n)), done


def per_device(n, activations, labels, counts):
    rows, d = activations.shape
    activations = pltpu.with_memory_space_constraint(activations, pltpu.HBM)
    me = lax.axis_index("dp").astype(jnp.int32).reshape(1)
    row_data = (counts * K + labels).reshape(1, rows)
    order_y, order_z = hop_bits(n)
    order_a, order_b = order_y[::-1], order_z[::-1]
    shifts = [[bit.bit_length() - 1 for bit in order] for order in (order_a, order_b)]

    root = Root(n, BOUND * 4 * rows * n)
    sent, weight = class_sums(me, row_data, activations, n, 1)
    weight = weight.T
    got = root(sent, 1)
    weight = weight + swap(weight, 1, n)
    kept, _ = class_sums(me, row_data, activations, n, 0)
    top, low, weight, _ = reduce_scatter(kept + got, n, root, root, weight, order_y)
    class_weight = weight.T
    total_weight = jnp.sum(class_weight, keepdims=True)
    over, back = class_weight, jnp.sqrt(class_weight)
    base = (top / over[:HALF]) * back[:HALF], (low / over[HALF:]) * back[HALF:]

    def scatter(probed, along, bound, sent, early, work, args):
        got = grow(swap(shrink(sent, bound), 1, n), bound)
        along = along + swap(along, 1, n)
        waiting = order_y
        if early:
            kept = panel_keep(me, probed, row_data, activations, n, 0)
            kept, along = lax.optimization_barrier((kept, along))
            along = along + swap(along, waiting[0], n)
            kept = panel_keep(me, probed, row_data, activations, n, 1, kept)
            waiting = waiting[1:]
        else:
            kept = panel_keep(me, probed, row_data, activations, n)
        blocks = kept + got
        top, low = bound[:HALF], bound[HALF:]
        return reduce_scatter(
            blocks,
            n,
            lambda x, bit: grow(swap(shrink(x, top), bit, n), top),
            lambda x, bit: grow(swap(shrink(x, low), bit, n), low),
            along,
            waiting,
            work,
            args,
        )

    square, strip = (K, K), (K, d // n)
    orders = order_a, order_b
    base_near, base_far, _ = gather(*base, n, orders)
    starts = probe(me, (base_near,), activations, n, shifts)
    first, along, bound, sent, current = probe_and_send(
        me, (base_far,), activations, row_data, total_weight, starts, (), n, shifts
    )
    panel_a, panel_b, along, (offset,) = scatter(
        first, along, bound, sent, False,
        lambda *args: small(offset_kernel, "offset", (strip,), *args), (*base, current, total_weight),
    )
    image = panel_a / total_weight + offset[:HALF], panel_b / total_weight + offset[HALF:]

    near, far, (alpha_t, inverse) = gather(
        *image, n, orders,
        lambda *args: small(alpha_kernel, "alpha", (square,) * 2, *args), (along, current, total_weight),
    )
    starts = probe(me, (near, base_near), activations, n, shifts)
    probed, along, bound, sent, _, _, renewed, mixed, beta_t = probe_and_send(
        me, (far, base_far), activations, row_data, total_weight, starts, (first, current, alpha_t, inverse), n, shifts
    )
    panel_a, panel_b, along, (fixed, cross_t) = scatter(
        probed, along, bound, sent, True,
        lambda *args: small(before_kernel, "before", (square,) * 2, *args),
        (current, renewed, mixed, beta_t, total_weight),
    )
    solved, rest, on_panel = small(
        last_kernel, "last", (strip, strip, square),
        along, fixed, cross_t, renewed, beta_t, alpha_t, total_weight, *base, *image,
    )
    (residual,) = small(end_kernel, "end", (strip,), rest, on_panel, panel_a, panel_b)
    return (solved.T, residual.T)


def solution(mesh):
    in_specs = (P(("groups", "dp"), None), P(("groups", "dp")), P(("groups", "dp")))
    out_specs = (P(("groups", "dp"), None), P(("groups", "dp"), None))
    return jax.shard_map(
        functools.partial(per_device, mesh.shape["dp"]),
        mesh=mesh,
        in_specs=in_specs,
        out_specs=out_specs,
        check_vma=False,
    )
```

```python
import functools

import jax
import jax.numpy as jnp
from jax import lax
from jax.experimental import pallas as pl
from jax.experimental.pallas import tpu as pltpu
from jax.sharding import PartitionSpec as P

K = 64
HALF = K // 2
RIDGE = 0.1
BOUND = 18.0
TOP = 60000.0
TINY = 1e-30
F32, BF16, F16 = jnp.float32, jnp.bfloat16, jnp.float16


def precise(left, right):
    return jnp.dot(left, right, precision=lax.Precision.HIGHEST, preferred_element_type=F32)


def outer(left, right):
    return lax.dot_general(
        left, right, (((1,), (1,)), ((), ())), precision=lax.Precision.HIGHEST, preferred_element_type=F32
    )


def symmetric(matrix):
    return 0.5 * (matrix + matrix.T)


def solve_positive(*works):
    index = lax.broadcasted_iota(jnp.int32, (K, 1), 0)
    works = list(works)
    for first in range(0, K, 8):
        spread = [[jnp.broadcast_to(w[:, first + j : first + j + 1], w.shape) for j in range(8)] for w in works]
        for k in range(8):
            at = slice(first + k, first + k + 1)
            row = index == first + k
            for i, columns in enumerate(spread):
                column, inv = columns[k], 1.0 / columns[k][at]
                scaled = works[i][at] * inv
                works[i] = jnp.where(row, scaled, works[i] - column * scaled)
                for j in range(k + 1, 8):
                    scaled = columns[j][at] * inv
                    columns[j] = jnp.where(row, scaled, columns[j] - column * scaled)
    return [work[:, K:] for work in works]


def beside(matrix, target):
    return jnp.concatenate([matrix, target], axis=1)


def identity():
    eye = lax.broadcasted_iota(jnp.int32, (K, K), 0) == lax.broadcasted_iota(jnp.int32, (K, K), 1)
    return jnp.where(eye, 1.0, 0.0)


def rows_of(core, first, second):
    return jnp.where(core == 0, jnp.concatenate([first, second], axis=0), jnp.concatenate([second, first], axis=0))


class Hops:
    def __init__(self, n):
        self.n = n
        self.count = n.bit_length() - 2
        ups = list(range(self.count))
        self.orders = ups, ups[1:] + ups[:1]

    def swap(self, value, bit):
        return lax.ppermute(value, "dp", [(i, i ^ bit) for i in range(self.n)])

    def across(self, value, hop):
        return lax.ppermute(value, "dp", [(i, i ^ (2 << self.orders[i & 1][hop])) for i in range(self.n)])

    def _both(self, core, fn):
        zero, one = fn(self.orders[0]), fn(self.orders[1])
        return zero + core * (one - zero)

    def chip(self, seat, core):
        def place(order):
            return sum(((seat >> (self.count - 1 - i)) & 1) << b for i, b in enumerate(order))

        return self._both(core, place)

    def seat(self, chip, core):
        def place(order):
            return sum(((chip >> b) & 1) << (self.count - 1 - i) for i, b in enumerate(order))

        return self._both(core, place)

    def other_seat(self, seat, core):
        return self.seat(self.chip(seat, core), 1 - core)


def block_copy(hops, acts, kept, sems, me, t):
    f = kept.shape[2]
    index = me[0]
    first = pl.multiple_of(((index >> 1) ^ hops.chip(t, index & 1)) * f, f)
    return pltpu.make_async_copy(acts.at[:, pl.ds(first, f)], kept.at[t], sems.at[t])


def start_copies(hops, acts, kept, sems, me):
    def start(t, carry):
        block_copy(hops, acts, kept, sems, me, t).start()
        return carry

    lax.fori_loop(0, kept.shape[0], start, 0)


def whole(*shape):
    return pl.BlockSpec(shape, lambda i, me: (0,) * len(shape))


HBM = pl.BlockSpec(memory_space=pltpu.HBM)


def call(kernel, name, n, grid, in_specs, outs, acts, scratch):
    rows, d = acts.shape
    return pl.pallas_call(
        kernel,
        out_shape=tuple(jax.ShapeDtypeStruct(shape, F32) for shape, _ in outs),
        grid_spec=pltpu.PrefetchScalarGridSpec(
            num_scalar_prefetch=1,
            grid=(grid,),
            in_specs=in_specs,
            out_specs=tuple(spec for _, spec in outs),
            scratch_shapes=[
                pltpu.VMEM((n // 2, rows, 2 * d // n), BF16),
                pltpu.SemaphoreType.DMA((n // 2,)),
                *scratch,
            ],
        ),
        compiler_params=pltpu.CompilerParams(vmem_limit_bytes=28 << 20),
        cost_estimate=pl.CostEstimate(
            flops=2 * grid * K * rows * d // n, bytes_accessed=2 * rows * d + 4 * K * d, transcendentals=0
        ),
        name=name,
    )


def block_outs(hops, n, f, before):
    def here(i, me):
        return (jnp.maximum(i - before, 0), 0, 0)

    def there(i, me):
        return (hops.other_seat(jnp.maximum(i - before, 0), me[0] & 1), 0, 0)

    shape = (n // 2, HALF, f)
    return [(shape, pl.BlockSpec((1, HALF, f), here)), (shape, pl.BlockSpec((1, HALF, f), there))]


def count_of(row_data):
    return lax.shift_right_logical(row_data[...], 6).astype(F32)


def sums_kernel(hops, me, row_data, acts, keep, send, weight, kept, sems, member):
    step = pl.program_id(0)

    @pl.when(step == 0)
    def _():
        start_copies(hops, acts, kept, sems, me)
        concept = lax.broadcasted_iota(jnp.int32, member.shape, 0)
        full = jnp.where((row_data[...] & (K - 1)) == concept, count_of(row_data), 0.0)
        weight[...] = jnp.sum(full, axis=1, keepdims=True)
        member[...] = rows_of(me[0] & 1, full[:HALF], full[HALF:]).astype(BF16)

    block_copy(hops, acts, kept, sems, me, step).wait()
    block = jnp.dot(member[...], kept[step], preferred_element_type=F32)
    keep[0] = block[:HALF]
    send[0] = block[HALF:]


def class_sums(hops, me, row_data, acts):
    n = hops.n
    rows, d = acts.shape
    return call(
        functools.partial(sums_kernel, hops),
        "class_sums",
        n,
        n // 2,
        [whole(1, rows), HBM],
        block_outs(hops, n, 2 * d // n, 0) + [((K, 1), whole(K, 1))],
        acts,
        [pltpu.VMEM((K, rows), BF16)],
    )(me, row_data, acts)


def inner(left, right):
    return lax.dot_general(left, right, (((1,), (1,)), ((), ())), preferred_element_type=F32)


def diagonal(matrix):
    kept = matrix * identity()
    return jnp.sum(kept, axis=1, keepdims=True), jnp.sum(kept, axis=0, keepdims=True)


def finish_first(gram):
    current = symmetric(gram[...])
    gram[...] = current
    return jnp.sqrt(diagonal(current)[0])


def finish_second(probed, image_image, base_image, more):
    first, current, alpha_t, inverse, renewed, mixed, beta_t = more
    both = jnp.concatenate([base_image[...], symmetric(image_image[...])], axis=0)
    moved = outer(both, alpha_t[...])
    moved, twice = moved[:K], precise(alpha_t[...], moved[K:])
    new = symmetric(current[...] - moved - moved.T + twice)
    beta = precise(new, inverse[...])
    renewed[...] = new
    mixed[...] = current[...] - moved
    beta_t[...] = beta
    mix = jnp.concatenate([beta, -alpha_t[...]], axis=1)
    probed[...] = first[...] + precise(mix, jnp.concatenate([first[...], probed[...]], axis=0))
    base_col, base_row = diagonal(current[...])
    _, image_row = diagonal(image_image[...])
    norms = jnp.sqrt(base_col)
    norms += jnp.sum(jnp.abs(beta) * jnp.sqrt(base_row), axis=1, keepdims=True)
    return norms + jnp.sum(jnp.abs(alpha_t[...]) * jnp.sqrt(image_row), axis=1, keepdims=True)


def covariance_kernel(hops, count, d, me, *refs):
    steps = hops.n // 2
    second = count == 2
    refs = list(refs)
    panels, ins, given, outs, grams, made, scratch = (
        [refs.pop(0) for _ in range(size)] for size in (4 * count, 3, 4 * second, 6, count, 3 * second, 5)
    )
    acts, row_data, total_weight = ins
    keep, send, probed, along, back, back_row = outs
    kept, sems, weighted, sum_of, inv = scratch
    step = pl.program_id(0)
    core = me[0] & 1

    @pl.when(step == 0)
    def _():
        start_copies(hops, acts, kept, sems, me)
        for ref in (sum_of, *grams):
            ref[...] = jnp.zeros_like(ref)

    @pl.when(step < steps)
    def _():
        across = hops.other_seat(step, core)
        both = []
        for i in range(count):
            own_low, own_high, low, high = panels[4 * i : 4 * i + 4]
            own = jnp.where(step < steps // 2, own_low[0], own_high[0])
            other = jnp.where(across < steps // 2, low[0], high[0])
            both.append(rows_of(core, own, other))
        block_copy(hops, acts, kept, sems, me, step).wait()
        sum_of[...] += inner(kept[step], both[0])
        for gram, panel in zip(grams, both):
            gram[...] += inner(panel, both[0])

    @pl.when(step == steps)
    def _():
        probed[...] = sum_of[...].T
        norms = finish_second(probed, *grams, (*given, *made)) if second else finish_first(*grams)
        bound = jnp.maximum((1.02 * BOUND * BOUND * d**0.5) * total_weight[...] * norms, TINY)
        scale = bound * (1.0 / TOP)
        back[...] = jnp.where(core == 0, scale[:HALF], scale[HALF:])
        back_row[...] = jnp.sum(scale * identity(), axis=0, keepdims=True)
        inv[...] = rows_of(core, TOP / bound[:HALF], TOP / bound[HALF:])
        whole_weighted = count_of(row_data) * probed[...]
        rounded = whole_weighted.astype(BF16)
        weighted[...] = rows_of(core, rounded[:HALF], rounded[HALF:])
        along[...] = outer(probed[...], rounded.astype(F32))

    @pl.when(step >= steps)
    def _():
        block = jnp.dot(weighted[...], kept[step - steps], preferred_element_type=F32) * inv[...]
        keep[0] = block[:HALF]
        send[0] = block[HALF:]


def covariance(hops, me, panels, acts, row_data, total_weight, given):
    n = hops.n
    rows, d = acts.shape
    f = 2 * d // n
    s = n // 2
    count = len(panels)
    made = 3 if given else 0

    def spec(other, high):
        def pick(i, me):
            seat = jnp.minimum(i, s - 1)
            if other:
                seat = hops.other_seat(seat, me[0] & 1)
            return (jnp.maximum(seat - s // 2, 0) if high else jnp.minimum(seat, s // 2 - 1), 0, 0)

        return pl.BlockSpec((1, HALF, f), pick)

    specs = [spec(False, False), spec(False, True), spec(True, False), spec(True, True)] * count
    return call(
        functools.partial(covariance_kernel, hops, count, d),
        "covariance",
        n,
        2 * s,
        specs + [HBM, whole(1, rows), whole(1, 1)] + [whole(*x.shape) for x in given],
        block_outs(hops, n, f, s)
        + [(shape, whole(*shape)) for shape in ((K, rows), (K, K), (HALF, 1), (1, K))]
        + [((K, K), whole(K, K))] * (count + made),
        acts,
        [pltpu.VMEM((K, rows), BF16), pltpu.VMEM((rows, K), F32), pltpu.VMEM((K, 1), F32)],
    )(me, *[x for panel in panels for x in panel], acts, row_data, total_weight, *given)


def alpha_kernel(along, current, total_weight, alpha_t, inverse):
    now = current[...]
    curvature = (along[...] - precise(now, now)) / total_weight[...] + RIDGE * now
    alpha, inv = solve_positive(beside(symmetric(curvature), now), beside(now, identity()))
    alpha_t[...] = alpha.T
    inverse[...] = symmetric(inv)


def offset_kernel(me, own, other, current, total_weight, offset):
    core = me[0] & 1
    part = jnp.where(core == 0, current[:HALF], current[HALF:]) / total_weight[...]
    offset[...] = RIDGE * own[...] - precise(part, rows_of(core, own[...], other[...]))


def before_kernel(current, renewed, mixed, beta_t, total_weight, fixed, cross_t):
    now, beta, weight = current[...], beta_t[...], total_weight[...]
    cross = mixed[...] + outer(now, beta)
    length = renewed[...] + outer(mixed[...].T, beta) + precise(beta, cross)
    turned = cross.T
    cross_t[...] = turned
    fixed[...] = RIDGE * length - outer(turned, turned) / weight


def last_kernel(
    me, along, fixed, cross_t, renewed, beta_t, alpha_t, total_weight, back_row,
    base_own, base_other, image_own, image_other, solved, rest, on_panel,
):
    core = me[0] & 1
    weight = total_weight[...]
    curvature = symmetric(along[...] / weight + fixed[...])
    step = solve_positive(beside(curvature, renewed[...]))[0].T
    scaled = step * (back_row[...] / weight)
    on_panel[...] = jnp.where(core == 0, scaled, beside(scaled[:, HALF:], scaled[:, :HALF]))
    alpha = alpha_t[...]
    all_three = precise(step, jnp.concatenate([identity() + beta_t[...], alpha, cross_t[...]], axis=1))
    direction_base, direction_image = all_three[:, :K], all_three[:, K : 2 * K]
    crossed = all_three[:, 2 * K :] / weight
    f = solved.shape[1]
    here = pl.ds(pl.multiple_of(core * f, f), f)
    base = rows_of(core, base_own[:, here], base_other[:, here])
    image = rows_of(core, image_own[:, here], image_other[:, here])
    both = jnp.concatenate([base, image], axis=0)
    solved[...] = precise(beside(alpha + direction_base, -direction_image), both)
    rest[...] = precise(
        beside(identity() - RIDGE * direction_base + crossed, RIDGE * direction_image - alpha), both
    )


def small(kernel, name, outs, *args):
    specs = [pl.BlockSpec(memory_space=pltpu.SMEM if x.dtype == jnp.int32 else pltpu.VMEM) for x in args]
    return pl.pallas_call(
        kernel, out_shape=tuple(jax.ShapeDtypeStruct(shape, F32) for shape in outs), name=name, in_specs=specs,
        cost_estimate=pl.CostEstimate(flops=1 << 26, bytes_accessed=1 << 20, transcendentals=0),
    )(*args)


def plain(value):
    return value.astype(F16)


def widen(value):
    return value.astype(F32)


def root_code(bound):
    scale = TOP / bound**0.5

    def code(value):
        root = jnp.sqrt(jnp.abs(value)) * scale
        return jnp.where(value < 0, -root, root).astype(F16)

    def decode(value):
        value = value.astype(F32)
        return value * jnp.abs(value) * (1.0 / scale**2)

    return code, decode


def reduce_scatter(hops, keep, send, codec, along, early=0, work=None, args=()):
    code, decode = codec
    got = hops.swap(code(send), 1)
    along = along + hops.swap(along, 1)
    value, done = keep + decode(got), ()
    for hop in range(hops.count):
        half = value.shape[0] // 2
        tied = args if hop == 1 else done
        send, along, tied = lax.optimization_barrier((code(value[half:]), along, tied))
        value = value[:half] + decode(hops.across(send, hop))
        along = along + hops.swap(along, 2 << hop)
        if work is not None and hop >= 1:
            done = work(*tied) if hop == 1 else tied
    value, along = lax.optimization_barrier((value, along)) if not early else (value, along)
    return value[0], along, done


def gather(hops, own, work=None, args=()):
    value, done = own.astype(BF16)[None], ()
    for hop in reversed(range(hops.count)):
        second = hop == hops.count - 2
        tied = args if second else done
        value, tied = lax.optimization_barrier((value, tied))
        got = hops.across(value, hop)
        if hop == 0:
            low = hops.swap(value, 1)
            return (value, got, low, hops.swap(got, 1)), tied
        if work is not None and (second or done):
            done = work(*tied) if second else tied
        value = jnp.concatenate([value, got], axis=0)


def per_device(n, activations, labels, counts):
    rows, d = activations.shape
    hops = Hops(n)
    activations = pltpu.with_memory_space_constraint(activations, pltpu.HBM)
    index = lax.axis_index("dp").astype(jnp.int32)
    core, me = index & 1, index.reshape(1)
    row_data = (counts * K + labels).reshape(1, rows)
    square, strip, chip_strip = (K, K), (K, d // n), (HALF, 2 * d // n)

    keep, send, weight = class_sums(hops, me, row_data, activations)
    sums, weight, _ = reduce_scatter(hops, keep, send, root_code(BOUND * 4 * rows * n), weight.T)
    total_weight = jnp.sum(weight, keepdims=True)
    class_weight = lax.dynamic_slice_in_dim(weight, core * HALF, HALF, axis=1).T
    base = (sums / class_weight) * jnp.sqrt(class_weight)

    base_all, _ = gather(hops, base)
    keep, send, first, along, back, _, current = covariance(
        hops, me, (base_all,), activations, row_data, total_weight, ()
    )
    base_other = hops.swap(base, 1)
    panel, along, (offset,) = reduce_scatter(
        hops, keep, send, (plain, widen), along, 0,
        lambda *args: small(offset_kernel, "offset", (chip_strip,), *args),
        (me, base, base_other, current, total_weight),
    )
    image = panel * (back / total_weight) + offset

    image_all, (alpha_t, inverse) = gather(
        hops, image,
        lambda *args: small(alpha_kernel, "alpha", (square,) * 2, *args), (along, current, total_weight),
    )
    keep, send, _, along, _, back_row, _, _, renewed, mixed, beta_t = covariance(
        hops, me, (image_all, base_all), activations, row_data, total_weight, (first, current, alpha_t, inverse)
    )
    image_other = hops.swap(image, 1)
    panel, along, (fixed, cross_t) = reduce_scatter(
        hops, keep, send, (plain, widen), along, 1,
        lambda *args: small(before_kernel, "before", (square,) * 2, *args),
        (current, renewed, mixed, beta_t, total_weight),
    )
    by_core = panel.reshape(HALF, 2, d // n)
    mine = lax.dynamic_index_in_dim(by_core, core, 1, keepdims=False)
    theirs = widen(hops.swap(plain(lax.dynamic_index_in_dim(by_core, 1 - core, 1, keepdims=False)), 1))
    solved, rest, on_panel = small(
        last_kernel, "last", (strip, strip, square),
        me, along, fixed, cross_t, renewed, beta_t, alpha_t, total_weight, back_row,
        base, base_other, image, image_other,
    )
    residual = rest - precise(on_panel, jnp.concatenate([mine, theirs], axis=0))
    return (solved.T, residual.T)


def solution(mesh):
    in_specs = (P(("groups", "dp"), None), P(("groups", "dp")), P(("groups", "dp")))
    out_specs = (P(("groups", "dp"), None), P(("groups", "dp"), None))
    return jax.shard_map(
        functools.partial(per_device, mesh.shape["dp"]),
        mesh=mesh,
        in_specs=in_specs,
        out_specs=out_specs,
        check_vma=False,
    )
```

```python
import functools

import jax
import jax.numpy as jnp
from jax import lax
from jax.experimental import pallas as pl
from jax.experimental.pallas import tpu as pltpu
from jax.sharding import PartitionSpec as P

K = 64
HALF = K // 2
RIDGE = 0.1
BOUND = 18.0
TOP = 60000.0
TINY = 1e-30
UNROLL = 4
F32, BF16, F16 = jnp.float32, jnp.bfloat16, jnp.float16


def precise(left, right):
    return jnp.dot(left, right, precision=lax.Precision.HIGHEST, preferred_element_type=F32)


def outer(left, right):
    return lax.dot_general(
        left, right, (((1,), (1,)), ((), ())), precision=lax.Precision.HIGHEST, preferred_element_type=F32
    )


def symmetric(matrix):
    return 0.5 * (matrix + matrix.T)


def solve_positive(*works):
    index = lax.broadcasted_iota(jnp.int32, (K, 1), 0)
    works = list(works)
    for first in range(0, K, 8):
        spread = [[jnp.broadcast_to(w[:, first + j : first + j + 1], w.shape) for j in range(8)] for w in works]
        for k in range(8):
            at = slice(first + k, first + k + 1)
            row = index == first + k
            for i, columns in enumerate(spread):
                column, inv = columns[k], 1.0 / columns[k][at]
                scaled = works[i][at] * inv
                works[i] = jnp.where(row, scaled, works[i] - column * scaled)
                for j in range(k + 1, 8):
                    scaled = columns[j][at] * inv
                    columns[j] = jnp.where(row, scaled, columns[j] - column * scaled)
    return [work[:, K:] for work in works]


def beside(matrix, target):
    return jnp.concatenate([matrix, target], axis=1)


def identity():
    eye = lax.broadcasted_iota(jnp.int32, (K, K), 0) == lax.broadcasted_iota(jnp.int32, (K, K), 1)
    return jnp.where(eye, 1.0, 0.0)


def swap(value, bit, n):
    return lax.ppermute(value, "dp", [(i, i ^ bit) for i in range(n)])


def hop_bits(n):
    bits = [1 << i for i in range(1, n.bit_length() - 1)]
    return bits, bits[1:] + bits[:1]


def _pos(j, shifts):
    p = 0
    for place, shift in enumerate(shifts):
        p = p | (((j >> shift) & 1) << place)
    return p


def block_copy(acts, kept, sems, me, half, t):
    f = kept.shape[2]
    first = pl.multiple_of((me[0] ^ (2 * t + half)) * f, f)
    return pltpu.make_async_copy(acts.at[:, pl.ds(first, f)], kept.at[t], sems.at[t])


def start_copies(acts, kept, sems, me, half):
    def start(t, carry):
        block_copy(acts, kept, sems, me, half, t).start()
        return carry

    lax.fori_loop(0, kept.shape[0], start, 0)


def whole(*shape):
    return pl.BlockSpec(shape, lambda i, me: (0,) * len(shape))


HBM = pl.BlockSpec(memory_space=pltpu.HBM)


def call(kernel, name, n, grid, in_specs, out_shapes, out_specs, acts, scratch=(), aliases=None):
    rows, d = acts.shape
    return pl.pallas_call(
        kernel,
        out_shape=out_shapes,
        grid_spec=pltpu.PrefetchScalarGridSpec(
            num_scalar_prefetch=1,
            grid=(grid,),
            in_specs=in_specs,
            out_specs=out_specs,
            scratch_shapes=[
                pltpu.VMEM((n // 2, rows, d // n), BF16),
                pltpu.SemaphoreType.DMA((n // 2,)),
                *scratch,
            ],
        ),
        compiler_params=pltpu.CompilerParams(vmem_limit_bytes=20 << 20),
        cost_estimate=pl.CostEstimate(flops=K * rows * d, bytes_accessed=rows * d + 2 * K * d, transcendentals=0),
        input_output_aliases=aliases or {},
        name=name,
    )


def count_of(row_data):
    return lax.shift_right_logical(row_data[...], 6).astype(F32)


def sums_kernel(half, me, row_data, acts, out, weight, kept, sems, member):
    step = pl.program_id(0)

    @pl.when(step == 0)
    def _():
        start_copies(acts, kept, sems, me, half)
        concept = lax.broadcasted_iota(jnp.int32, member.shape, 0)
        label = row_data[...] & (K - 1)
        full = jnp.where(label == concept, count_of(row_data), 0.0)
        member[...] = full.astype(BF16)
        weight[...] = jnp.sum(full, axis=1, keepdims=True)

    for u in range(UNROLL):
        t = step * UNROLL + u
        block_copy(acts, kept, sems, me, half, t).wait()
        out[u] = jnp.dot(member[...], kept[t], preferred_element_type=F32)


def class_sums(me, row_data, acts, n, half):
    rows, d = acts.shape
    f = d // n
    return call(
        functools.partial(sums_kernel, half),
        "class_sums",
        n,
        n // 2 // UNROLL,
        [whole(1, rows), HBM],
        (
            jax.ShapeDtypeStruct((n // 2, K, f), F32),
            jax.ShapeDtypeStruct((K, 1), F32),
        ),
        (pl.BlockSpec((UNROLL, K, f), lambda i, me: (i, 0, 0)), whole(K, 1)),
        acts,
        [pltpu.VMEM((K, rows), BF16)],
    )(me, row_data, acts)


def inner(left, right):
    return lax.dot_general(left, right, (((1,), (1,)), ((), ())), preferred_element_type=F32)


def panel_operands(panels, n, f, shifts):
    last = n // 2 // UNROLL - 1
    specs, operands = [], []
    for panel in panels:
        for u in range(UNROLL):
            for stream, order in zip(panel, shifts):
                pick = lambda i, me, u=u, order=order: (_pos(2 * (jnp.minimum(i, last) * UNROLL + u), order), 0, 0)
                specs.append(pl.BlockSpec((1, HALF, f), pick))
                operands.append(stream)
    return specs, operands


def add_blocks(refs, count, block, probed, grams):
    total = probed[...]
    sums = [gram[...] for gram in grams]
    for u in range(UNROLL):
        at = [2 * (panel * UNROLL + u) for panel in range(count)]
        both = [jnp.concatenate([refs[i][0], refs[i + 1][0]], axis=0) for i in at]
        total = total + inner(block(u), both[0])
        sums = [x + inner(other, both[0]) for x, other in zip(sums, both)]
    probed[...] = total
    for gram, x in zip(grams, sums):
        gram[...] = x


def probe_kernel(count, me, *refs):
    panels, refs = refs[: 2 * UNROLL * count], refs[2 * UNROLL * count :]
    acts, probed, *grams, kept, sems = refs
    step = pl.program_id(0)

    @pl.when(step == 0)
    def _():
        start_copies(acts, kept, sems, me, 0)
        for ref in (probed, *grams):
            ref[...] = jnp.zeros_like(ref)

    def block(u):
        block_copy(acts, kept, sems, me, 0, step * UNROLL + u).wait()
        return kept[step * UNROLL + u]

    add_blocks(panels, count, block, probed, grams)


def probe(me, panels, acts, n, shifts):
    rows, d = acts.shape
    count = len(panels)
    specs, operands = panel_operands(panels, n, d // n, shifts)
    return call(
        functools.partial(probe_kernel, count),
        "probe",
        n,
        n // 2 // UNROLL,
        specs + [HBM],
        (jax.ShapeDtypeStruct((rows, K), F32),) + (jax.ShapeDtypeStruct((K, K), F32),) * count,
        (whole(rows, K),) + (whole(K, K),) * count,
        acts,
    )(me, *operands, acts)


def diagonal(matrix):
    kept = matrix * identity()
    return jnp.sum(kept, axis=1, keepdims=True), jnp.sum(kept, axis=0, keepdims=True)


def finish_first(gram):
    current = symmetric(gram[...])
    gram[...] = current
    return jnp.sqrt(diagonal(current)[0])


def finish_second(probed, image_image, base_image, more):
    first, current, alpha_t, inverse, renewed, mixed, beta_t = more
    both = jnp.concatenate([base_image[...], symmetric(image_image[...])], axis=0)
    moved = outer(both, alpha_t[...])
    moved, twice = moved[:K], precise(alpha_t[...], moved[K:])
    new = symmetric(current[...] - moved - moved.T + twice)
    beta = precise(new, inverse[...])
    renewed[...] = new
    mixed[...] = current[...] - moved
    beta_t[...] = beta
    mix = jnp.concatenate([beta, -alpha_t[...]], axis=1)
    probed[...] = first[...] + precise(mix, jnp.concatenate([first[...], probed[...]], axis=0))
    base_col, base_row = diagonal(current[...])
    _, image_row = diagonal(image_image[...])
    norms = jnp.sqrt(base_col)
    norms += jnp.sum(jnp.abs(beta) * jnp.sqrt(base_row), axis=1, keepdims=True)
    return norms + jnp.sum(jnp.abs(alpha_t[...]) * jnp.sqrt(image_row), axis=1, keepdims=True)


def send_kernel(steps, count, d, me, *refs):
    second = count == 2
    parts = [2 * UNROLL * count, 4, count, 4 * second, 6, count, 3 * second, 4]
    refs = list(refs)
    panels, ins, starts, given, outs, grams, made, scratch = (
        [refs.pop(0) for _ in range(size)] for size in parts
    )
    acts, row_data, total_weight, start = ins
    probed, along, inv, back, back_row, out = outs
    kept, sems, weighted, sum_of = scratch
    step = pl.program_id(0)

    @pl.when(step == 0)
    def _():
        start_copies(acts, kept, sems, me, 1)
        for ref, begin in zip((sum_of, *grams), (start, *starts)):
            ref[...] = begin[...]

    @pl.when(step < steps)
    def _():
        def block(u):
            block_copy(acts, kept, sems, me, 1, step * UNROLL + u).wait()
            return kept[step * UNROLL + u]

        add_blocks(panels, count, block, sum_of, grams)

    @pl.when(step == steps)
    def _():
        probed[...] = sum_of[...].T
        norms = finish_second(probed, *grams, (*given, *made)) if second else finish_first(*grams)
        bound = jnp.maximum((1.02 * BOUND * BOUND * d**0.5) * total_weight[...] * norms, TINY)
        inv[...] = TOP / bound
        back[...] = bound * (1.0 / TOP)
        back_row[...] = jnp.sum(bound * (1.0 / TOP) * identity(), axis=0, keepdims=True)
        weighted[...] = (count_of(row_data) * probed[...]).astype(BF16)
        along[...] = outer(probed[...], weighted[...].astype(F32))

    @pl.when(step >= steps)
    def _():
        for u in range(UNROLL):
            block = jnp.dot(weighted[...], kept[(step - steps) * UNROLL + u], preferred_element_type=F32)
            out[u] = block * inv[...]


def probe_and_send(me, panels, acts, row_data, total_weight, starts, given, n, shifts):
    rows, d = acts.shape
    f = d // n
    s = n // 2 // UNROLL
    count = len(panels)
    square = jax.ShapeDtypeStruct((K, K), F32)
    made = 3 if given else 0
    specs, operands = panel_operands(panels, n, f, shifts)
    return call(
        functools.partial(send_kernel, s, count, d),
        "probe_and_send",
        n,
        2 * s,
        specs + [HBM, whole(1, rows), whole(1, 1)] + [whole(*x.shape) for x in (*starts, *given)],
        (
            jax.ShapeDtypeStruct((K, rows), F32),
            square,
            jax.ShapeDtypeStruct((K, 1), F32),
            jax.ShapeDtypeStruct((K, 1), F32),
            jax.ShapeDtypeStruct((1, K), F32),
            jax.ShapeDtypeStruct((n // 2, K, f), F32),
        )
        + (square,) * (count + made),
        (
            whole(K, rows),
            whole(K, K),
            whole(K, 1),
            whole(K, 1),
            whole(1, K),
            pl.BlockSpec((UNROLL, K, f), lambda i, me: (jnp.maximum(i - s, 0), 0, 0)),
        )
        + (whole(K, K),) * (count + made),
        acts,
        [pltpu.VMEM((K, rows), BF16), pltpu.VMEM((rows, K), F32)],
    )(me, *operands, acts, row_data, total_weight, *starts, *given)


def keep_kernel(base, me, probed, row_data, inv, acts, *refs):
    out, kept, sems, weighted = refs[-4:]
    step = pl.program_id(0)

    def copy(t):
        return block_copy(acts, kept, sems, me, 0, t)

    @pl.when(step == 0)
    def _():
        lax.fori_loop(base, base + pl.num_programs(0) * UNROLL, lambda t, c: (copy(t).start(), c)[1], 0)
        weighted[...] = (count_of(row_data) * probed[...]).astype(BF16)

    for u in range(UNROLL):
        t = base + step * UNROLL + u
        copy(t).wait()
        out[u] = jnp.dot(weighted[...], kept[t], preferred_element_type=F32) * inv[...]


def panel_keep(me, probed, row_data, inv, acts, n, part=None, into=None):
    rows, d = acts.shape
    f = d // n
    steps = n // 2 // UNROLL
    first = 0
    if part is not None:
        steps //= 2
        first = part * steps
    more = () if into is None else (into,)
    return call(
        functools.partial(keep_kernel, first * UNROLL),
        "panel_keep",
        n,
        steps,
        [whole(K, rows), whole(1, rows), whole(K, 1), HBM] + [pl.BlockSpec(memory_space=pl.ANY)] * len(more),
        jax.ShapeDtypeStruct((n // 2, K, f), F32),
        pl.BlockSpec((UNROLL, K, f), lambda i, me: (i + first, 0, 0)),
        acts,
        [pltpu.VMEM((K, rows), BF16)],
        {5: 0} if more else {},
    )(me, probed, row_data, inv, acts, *more)


def alpha_kernel(along, current, total_weight, alpha_t, inverse):
    now = current[...]
    curvature = (along[...] - precise(now, now)) / total_weight[...] + RIDGE * now
    alpha, inv = solve_positive(beside(symmetric(curvature), now), beside(now, identity()))
    alpha_t[...] = alpha.T
    inverse[...] = symmetric(inv)


def offset_kernel(base_a, base_b, current, total_weight, offset):
    base = jnp.concatenate([base_a[...], base_b[...]], axis=0)
    offset[...] = RIDGE * base - precise(current[...] / total_weight[...], base)


def before_kernel(current, renewed, mixed, beta_t, total_weight, fixed, cross_t):
    now, beta, weight = current[...], beta_t[...], total_weight[...]
    cross = mixed[...] + outer(now, beta)
    length = renewed[...] + outer(mixed[...].T, beta) + precise(beta, cross)
    turned = cross.T
    cross_t[...] = turned
    fixed[...] = RIDGE * length - outer(turned, turned) / weight


def last_kernel(
    along, fixed, cross_t, renewed, beta_t, alpha_t, total_weight, back_row, base_a, base_b, image_a, image_b,
    solved, rest, on_panel,
):
    weight = total_weight[...]
    curvature = symmetric(along[...] / weight + fixed[...])
    step = solve_positive(beside(curvature, renewed[...]))[0].T
    on_panel[...] = step * (back_row[...] / weight)
    alpha = alpha_t[...]
    all_three = precise(step, jnp.concatenate([identity() + beta_t[...], alpha, cross_t[...]], axis=1))
    direction_base, direction_image = all_three[:, :K], all_three[:, K : 2 * K]
    crossed = all_three[:, 2 * K :] / weight
    both = jnp.concatenate([base_a[...], base_b[...], image_a[...], image_b[...]], axis=0)
    solved[...] = precise(beside(alpha + direction_base, -direction_image), both)
    rest[...] = precise(
        beside(identity() - RIDGE * direction_base + crossed, RIDGE * direction_image - alpha), both
    )


def small(kernel, name, outs, *args):
    return pl.pallas_call(
        kernel, out_shape=tuple(jax.ShapeDtypeStruct(shape, F32) for shape in outs), name=name,
        cost_estimate=pl.CostEstimate(flops=1 << 26, bytes_accessed=1 << 20, transcendentals=0),
    )(*args)


def plain(n):
    return lambda value, bit: swap(value.astype(F16), bit, n).astype(F32)


def split_blocks(value, left, bit):
    axis = left.index(bit)
    keep = lax.index_in_dim(value, 0, axis, keepdims=False)
    send = lax.index_in_dim(value, 1, axis, keepdims=False)
    return keep, send, [other for other in left if other != bit]


def reduce_scatter(blocks, n, swap_a, swap_b, along, waiting, work=None, args=(), along_ends=True):
    bits = n.bit_length() - 2
    shape = (2,) * bits + (HALF, blocks.shape[2])
    a, b = blocks[:, :HALF].reshape(shape), blocks[:, HALF:].reshape(shape)
    left_a = left_b = [1 << i for i in range(bits, 0, -1)]
    order_a, order_b = hop_bits(n)
    waiting, done = list(waiting), ()
    for phase, (bit_a, bit_b) in enumerate(zip(order_a, order_b)):
        keep_a, send_a, left_a = split_blocks(a, left_a, bit_a)
        keep_b, send_b, left_b = split_blocks(b, left_b, bit_b)
        tied = args if phase == 1 else done
        send_a, send_b, along, tied = lax.optimization_barrier((send_a, send_b, along, tied))
        a, b = keep_a + swap_a(send_a, bit_a), keep_b + swap_b(send_b, bit_b)
        if waiting:
            along = along + swap(along, waiting.pop(0), n)
        if work is not None and phase >= 1:
            done = work(*tied) if phase == 1 else tied
    if along_ends:
        a, b, along = lax.optimization_barrier((a, b, along))
    return a, b, along, done


class Root:
    def __init__(self, n, bound):
        self.n, self.scale = n, TOP / bound**0.5

    def __call__(self, send, bit):
        root = jnp.sqrt(jnp.abs(send)) * self.scale
        got = swap(jnp.where(send < 0, -root, root).astype(F16), bit, self.n).astype(F32)
        return got * jnp.abs(got) * (1.0 / self.scale**2)


def gather(top, low, n, orders, work=None, args=()):
    a, b = top.astype(BF16)[None], low.astype(BF16)[None]
    done = ()
    for phase, (bit_a, bit_b) in enumerate(zip(*orders)):
        tied = args if phase == 1 else done
        a, b, tied = lax.optimization_barrier((a, b, tied))
        if work is not None and phase >= 1:
            done = work(*tied) if phase == 1 else tied
        a = jnp.concatenate([a, swap(a, bit_a, n)], axis=0)
        b = jnp.concatenate([b, swap(b, bit_b, n)], axis=0)
    return (a, b), (swap(a, 1, n), swap(b, 1, n)), done


def per_device(n, activations, labels, counts):
    rows, d = activations.shape
    activations = pltpu.with_memory_space_constraint(activations, pltpu.HBM)
    me = lax.axis_index("dp").astype(jnp.int32).reshape(1)
    row_data = (counts * K + labels).reshape(1, rows)
    order_y, order_z = hop_bits(n)
    order_a, order_b = order_y[::-1], order_z[::-1]
    shifts = [[bit.bit_length() - 1 for bit in order] for order in (order_a, order_b)]

    root = Root(n, BOUND * 4 * rows * n)
    sent, weight = class_sums(me, row_data, activations, n, 1)
    weight = weight.T
    got = root(sent, 1)
    weight = weight + swap(weight, 1, n)
    kept, _ = class_sums(me, row_data, activations, n, 0)
    top, low, weight, _ = reduce_scatter(kept + got, n, root, root, weight, order_y)
    class_weight = weight.T
    total_weight = jnp.sum(class_weight, keepdims=True)
    over, back = class_weight, jnp.sqrt(class_weight)
    base = (top / over[:HALF]) * back[:HALF], (low / over[HALF:]) * back[HALF:]

    def scatter(probed, along, inv, sent, early, work, args):
        hop = plain(n)
        got = hop(sent, 1)
        along = along + swap(along, 1, n)
        waiting = order_y
        if early:
            kept = panel_keep(me, probed, row_data, inv, activations, n, 0)
            kept, along = lax.optimization_barrier((kept, along))
            along = along + swap(along, waiting[0], n)
            kept = panel_keep(me, probed, row_data, inv, activations, n, 1, kept)
            waiting = waiting[1:]
        else:
            kept = panel_keep(me, probed, row_data, inv, activations, n)
        return reduce_scatter(kept + got, n, hop, hop, along, waiting, work, args, not early)

    square, strip = (K, K), (K, d // n)
    orders = order_a, order_b
    base_near, base_far, _ = gather(*base, n, orders)
    starts = probe(me, (base_near,), activations, n, shifts)
    first, along, inv, back, _, sent, current = probe_and_send(
        me, (base_far,), activations, row_data, total_weight, starts, (), n, shifts
    )
    panel_a, panel_b, along, (offset,) = scatter(
        first, along, inv, sent, False,
        lambda *args: small(offset_kernel, "offset", (strip,), *args), (*base, current, total_weight),
    )
    back = back / total_weight
    image = panel_a * back[:HALF] + offset[:HALF], panel_b * back[HALF:] + offset[HALF:]

    near, far, (alpha_t, inverse) = gather(
        *image, n, orders,
        lambda *args: small(alpha_kernel, "alpha", (square,) * 2, *args), (along, current, total_weight),
    )
    starts = probe(me, (near, base_near), activations, n, shifts)
    probed, along, inv, _, back_row, sent, _, _, renewed, mixed, beta_t = probe_and_send(
        me, (far, base_far), activations, row_data, total_weight, starts, (first, current, alpha_t, inverse), n, shifts
    )
    panel_a, panel_b, along, (fixed, cross_t) = scatter(
        probed, along, inv, sent, True,
        lambda *args: small(before_kernel, "before", (square,) * 2, *args),
        (current, renewed, mixed, beta_t, total_weight),
    )
    solved, rest, on_panel = small(
        last_kernel, "last", (strip, strip, square),
        along, fixed, cross_t, renewed, beta_t, alpha_t, total_weight, back_row, *base, *image,
    )
    residual = rest - precise(on_panel, jnp.concatenate([panel_a, panel_b], axis=0))
    return (solved.T, residual.T)


def solution(mesh):
    in_specs = (P(("groups", "dp"), None), P(("groups", "dp")), P(("groups", "dp")))
    out_specs = (P(("groups", "dp"), None), P(("groups", "dp"), None))
    return jax.shard_map(
        functools.partial(per_device, mesh.shape["dp"]),
        mesh=mesh,
        in_specs=in_specs,
        out_specs=out_specs,
        check_vma=False,
    )
```

```python
import functools

import jax
import jax.numpy as jnp
from jax import lax
from jax.experimental import pallas as pl
from jax.experimental.pallas import tpu as pltpu
from jax.sharding import PartitionSpec as P

K = 64
HALF = K // 2
RIDGE = 0.1
BOUND = 18.0
TOP = 60000.0
TINY = 1e-30
UNROLL = 2
F32, BF16, F16 = jnp.float32, jnp.bfloat16, jnp.float16


def precise(left, right):
    return jnp.dot(left, right, precision=lax.Precision.HIGHEST, preferred_element_type=F32)


def outer(left, right):
    return lax.dot_general(
        left, right, (((1,), (1,)), ((), ())), precision=lax.Precision.HIGHEST, preferred_element_type=F32
    )


def symmetric(matrix):
    return 0.5 * (matrix + matrix.T)


def solve_positive(*works):
    index = lax.broadcasted_iota(jnp.int32, (K, 1), 0)
    works = list(works)
    for first in range(0, K, 8):
        spread = [[jnp.broadcast_to(w[:, first + j : first + j + 1], w.shape) for j in range(8)] for w in works]
        for k in range(8):
            at = slice(first + k, first + k + 1)
            row = index == first + k
            for i, columns in enumerate(spread):
                column, inv = columns[k], 1.0 / columns[k][at]
                scaled = works[i][at] * inv
                works[i] = jnp.where(row, scaled, works[i] - column * scaled)
                for j in range(k + 1, 8):
                    scaled = columns[j][at] * inv
                    columns[j] = jnp.where(row, scaled, columns[j] - column * scaled)
    return [work[:, K:] for work in works]


def beside(matrix, target):
    return jnp.concatenate([matrix, target], axis=1)


def identity():
    eye = lax.broadcasted_iota(jnp.int32, (K, K), 0) == lax.broadcasted_iota(jnp.int32, (K, K), 1)
    return jnp.where(eye, 1.0, 0.0)


def swap(value, bit, n):
    return lax.ppermute(value, "dp", [(i, i ^ bit) for i in range(n)])


def hop_bits(n):
    bits = [1 << i for i in range(1, n.bit_length() - 1)]
    return bits, bits[1:] + bits[:1]


def _pos(j, shifts):
    p = 0
    for place, shift in enumerate(shifts):
        p = p | (((j >> shift) & 1) << place)
    return p


def block_copy(acts, kept, sems, me, half, t):
    f = kept.shape[2]
    first = pl.multiple_of((me[0] ^ (2 * t + half)) * f, f)
    return pltpu.make_async_copy(acts.at[:, pl.ds(first, f)], kept.at[t], sems.at[t])


def start_copies(acts, kept, sems, me, half):
    def start(t, carry):
        block_copy(acts, kept, sems, me, half, t).start()
        return carry

    lax.fori_loop(0, kept.shape[0], start, 0)


def whole(*shape):
    return pl.BlockSpec(shape, lambda i, me: (0,) * len(shape))


HBM = pl.BlockSpec(memory_space=pltpu.HBM)


def call(kernel, name, n, grid, in_specs, out_shapes, out_specs, acts, scratch=(), aliases=None):
    rows, d = acts.shape
    return pl.pallas_call(
        kernel,
        out_shape=out_shapes,
        grid_spec=pltpu.PrefetchScalarGridSpec(
            num_scalar_prefetch=1,
            grid=(grid,),
            in_specs=in_specs,
            out_specs=out_specs,
            scratch_shapes=[
                pltpu.VMEM((n // 2, rows, d // n), BF16),
                pltpu.SemaphoreType.DMA((n // 2,)),
                *scratch,
            ],
        ),
        compiler_params=pltpu.CompilerParams(vmem_limit_bytes=20 << 20),
        cost_estimate=pl.CostEstimate(flops=K * rows * d, bytes_accessed=rows * d + 2 * K * d, transcendentals=0),
        input_output_aliases=aliases or {},
        name=name,
    )


def count_of(row_data):
    return lax.shift_right_logical(row_data[...], 6).astype(F32)


def sums_kernel(half, me, row_data, acts, out, weight, kept, sems, member):
    step = pl.program_id(0)

    @pl.when(step == 0)
    def _():
        start_copies(acts, kept, sems, me, half)
        concept = lax.broadcasted_iota(jnp.int32, member.shape, 0)
        label = row_data[...] & (K - 1)
        full = jnp.where(label == concept, count_of(row_data), 0.0)
        member[...] = full.astype(BF16)
        weight[...] = jnp.sum(full, axis=1, keepdims=True)

    for u in range(UNROLL):
        t = step * UNROLL + u
        block_copy(acts, kept, sems, me, half, t).wait()
        out[u] = jnp.dot(member[...], kept[t], preferred_element_type=F32)


def class_sums(me, row_data, acts, n, half):
    rows, d = acts.shape
    f = d // n
    return call(
        functools.partial(sums_kernel, half),
        "class_sums",
        n,
        n // 2 // UNROLL,
        [whole(1, rows), HBM],
        (
            jax.ShapeDtypeStruct((n // 2, K, f), F32),
            jax.ShapeDtypeStruct((K, 1), F32),
        ),
        (pl.BlockSpec((UNROLL, K, f), lambda i, me: (i, 0, 0)), whole(K, 1)),
        acts,
        [pltpu.VMEM((K, rows), BF16)],
    )(me, row_data, acts)


def inner(left, right):
    return lax.dot_general(left, right, (((1,), (1,)), ((), ())), preferred_element_type=F32)


def panel_operands(panels, n, f, shifts):
    last = n // 2 // UNROLL - 1
    specs, operands = [], []
    for panel in panels:
        for u in range(UNROLL):
            for stream, order in zip(panel, shifts):
                pick = lambda i, me, u=u, order=order: (_pos(2 * (jnp.minimum(i, last) * UNROLL + u), order), 0, 0)
                specs.append(pl.BlockSpec((1, HALF, f), pick))
                operands.append(stream)
    return specs, operands


def add_blocks(refs, count, block, probed, grams):
    total = probed[...]
    sums = [gram[...] for gram in grams]
    for u in range(UNROLL):
        at = [2 * (panel * UNROLL + u) for panel in range(count)]
        both = [jnp.concatenate([refs[i][0], refs[i + 1][0]], axis=0) for i in at]
        total = total + inner(block(u), both[0])
        sums = [x + inner(other, both[0]) for x, other in zip(sums, both)]
    probed[...] = total
    for gram, x in zip(grams, sums):
        gram[...] = x


def load_kernel(acts, out, sems):
    count = sems.shape[0]
    f = acts.shape[1] // count

    def copy(t):
        columns = pl.ds(pl.multiple_of(t * f, f), f)
        return pltpu.make_async_copy(acts.at[:, columns], out.at[:, columns], sems.at[t])

    lax.fori_loop(0, count, lambda t, c: (copy(t).start(), c)[1], 0)
    lax.fori_loop(0, count, lambda t, c: (copy(t).wait(), c)[1], 0)


def load(acts):
    return pl.pallas_call(
        load_kernel,
        out_shape=jax.ShapeDtypeStruct(acts.shape, acts.dtype),
        in_specs=[HBM],
        out_specs=pl.BlockSpec(memory_space=pltpu.VMEM),
        scratch_shapes=[pltpu.SemaphoreType.DMA((8,))],
        compiler_params=pltpu.CompilerParams(vmem_limit_bytes=16 << 20),
        cost_estimate=pl.CostEstimate(flops=0, bytes_accessed=4 * acts.size, transcendentals=0),
        name="load",
    )(acts)


def near_call(kernel, name, n, grid, in_specs, out_shapes, out_specs, acts, scratch=(), aliases=None):
    rows, d = acts.shape
    return pl.pallas_call(
        kernel,
        out_shape=out_shapes,
        grid_spec=pltpu.PrefetchScalarGridSpec(
            num_scalar_prefetch=1, grid=(grid,), in_specs=in_specs, out_specs=out_specs, scratch_shapes=scratch
        ),
        compiler_params=pltpu.CompilerParams(vmem_limit_bytes=12 << 20),
        cost_estimate=pl.CostEstimate(flops=K * rows * d, bytes_accessed=rows * d + 2 * K * d, transcendentals=0),
        input_output_aliases=aliases or {},
        name=name,
    )


def act_specs(rows, f, half, block):
    return [
        pl.BlockSpec((rows, f), lambda i, me, u=u: (0, me[0] ^ (2 * (block(i) + u) + half))) for u in range(UNROLL)
    ]


def probe_kernel(count, me, *refs):
    panels, acts, outs = refs[: 2 * UNROLL * count], refs[2 * UNROLL * count : -1 - count], refs[-1 - count :]
    probed, *grams = outs

    @pl.when(pl.program_id(0) == 0)
    def _():
        for ref in outs:
            ref[...] = jnp.zeros_like(ref)

    add_blocks(panels, count, lambda u: acts[u][...], probed, grams)


def probe(me, panels, acts, n, shifts):
    rows, d = acts.shape
    f = d // n
    count = len(panels)
    specs, operands = panel_operands(panels, n, f, shifts)
    return near_call(
        functools.partial(probe_kernel, count),
        "probe",
        n,
        n // 2 // UNROLL,
        specs + act_specs(rows, f, 0, lambda i: i * UNROLL),
        (jax.ShapeDtypeStruct((rows, K), F32),) + (jax.ShapeDtypeStruct((K, K), F32),) * count,
        (whole(rows, K),) + (whole(K, K),) * count,
        acts,
    )(me, *operands, *[acts] * UNROLL)


def diagonal(matrix):
    kept = matrix * identity()
    return jnp.sum(kept, axis=1, keepdims=True), jnp.sum(kept, axis=0, keepdims=True)


def finish_first(gram):
    current = symmetric(gram[...])
    gram[...] = current
    return jnp.sqrt(diagonal(current)[0])


def finish_second(probed, image_image, base_image, more):
    first, current, alpha_t, inverse, renewed, mixed, beta_t = more
    both = jnp.concatenate([base_image[...], symmetric(image_image[...])], axis=0)
    moved = outer(both, alpha_t[...])
    moved, twice = moved[:K], precise(alpha_t[...], moved[K:])
    new = symmetric(current[...] - moved - moved.T + twice)
    beta = precise(new, inverse[...])
    renewed[...] = new
    mixed[...] = current[...] - moved
    beta_t[...] = beta
    mix = jnp.concatenate([beta, -alpha_t[...]], axis=1)
    probed[...] = first[...] + precise(mix, jnp.concatenate([first[...], probed[...]], axis=0))
    base_col, base_row = diagonal(current[...])
    _, image_row = diagonal(image_image[...])
    norms = jnp.sqrt(base_col)
    norms += jnp.sum(jnp.abs(beta) * jnp.sqrt(base_row), axis=1, keepdims=True)
    return norms + jnp.sum(jnp.abs(alpha_t[...]) * jnp.sqrt(image_row), axis=1, keepdims=True)


def send_kernel(steps, count, d, me, *refs):
    second = count == 2
    parts = [2 * UNROLL * count, UNROLL, 3, count, 4 * second, 6, count, 3 * second, 2]
    refs = list(refs)
    panels, acts, ins, starts, given, outs, grams, made, scratch = (
        [refs.pop(0) for _ in range(size)] for size in parts
    )
    row_data, total_weight, start = ins
    probed, along, inv, back, back_row, out = outs
    weighted, sum_of = scratch
    step = pl.program_id(0)

    @pl.when(step == 0)
    def _():
        for ref, begin in zip((sum_of, *grams), (start, *starts)):
            ref[...] = begin[...]

    @pl.when(step < steps)
    def _():
        add_blocks(panels, count, lambda u: acts[u][...], sum_of, grams)

    @pl.when(step == steps)
    def _():
        probed[...] = sum_of[...].T
        norms = finish_second(probed, *grams, (*given, *made)) if second else finish_first(*grams)
        bound = jnp.maximum((1.02 * BOUND * BOUND * d**0.5) * total_weight[...] * norms, TINY)
        inv[...] = TOP / bound
        back[...] = bound * (1.0 / TOP)
        back_row[...] = jnp.sum(bound * (1.0 / TOP) * identity(), axis=0, keepdims=True)
        weighted[...] = (count_of(row_data) * probed[...]).astype(BF16)
        along[...] = outer(probed[...], weighted[...].astype(F32))

    @pl.when(step >= steps)
    def _():
        for u in range(UNROLL):
            block = jnp.dot(weighted[...], acts[u][...], preferred_element_type=F32)
            out[u] = block * inv[...]


def probe_and_send(me, panels, acts, row_data, total_weight, starts, given, n, shifts):
    rows, d = acts.shape
    f = d // n
    s = n // 2 // UNROLL
    count = len(panels)
    square = jax.ShapeDtypeStruct((K, K), F32)
    made = 3 if given else 0
    specs, operands = panel_operands(panels, n, f, shifts)
    return near_call(
        functools.partial(send_kernel, s, count, d),
        "probe_and_send",
        n,
        2 * s,
        specs
        + act_specs(rows, f, 1, lambda i: jnp.where(i < s, i, i - s) * UNROLL)
        + [whole(1, rows), whole(1, 1)]
        + [whole(*x.shape) for x in (*starts, *given)],
        (
            jax.ShapeDtypeStruct((K, rows), F32),
            square,
            jax.ShapeDtypeStruct((K, 1), F32),
            jax.ShapeDtypeStruct((K, 1), F32),
            jax.ShapeDtypeStruct((1, K), F32),
            jax.ShapeDtypeStruct((n // 2, K, f), F32),
        )
        + (square,) * (count + made),
        (
            whole(K, rows),
            whole(K, K),
            whole(K, 1),
            whole(K, 1),
            whole(1, K),
            pl.BlockSpec((UNROLL, K, f), lambda i, me: (jnp.maximum(i - s, 0), 0, 0)),
        )
        + (whole(K, K),) * (count + made),
        acts,
        [pltpu.VMEM((K, rows), BF16), pltpu.VMEM((rows, K), F32)],
    )(me, *operands, *[acts] * UNROLL, row_data, total_weight, *starts, *given)


def keep_kernel(me, probed, row_data, inv, *refs):
    acts, out, weighted = refs[:UNROLL], refs[-2], refs[-1]

    @pl.when(pl.program_id(0) == 0)
    def _():
        weighted[...] = (count_of(row_data) * probed[...]).astype(BF16)

    for u in range(UNROLL):
        out[u] = jnp.dot(weighted[...], acts[u][...], preferred_element_type=F32) * inv[...]


def panel_keep(me, probed, row_data, inv, acts, n, part=None, into=None):
    rows, d = acts.shape
    f = d // n
    steps = n // 2 // UNROLL
    first = 0
    if part is not None:
        steps //= 2
        first = part * steps
    more = () if into is None else (into,)
    return near_call(
        keep_kernel,
        "panel_keep",
        n,
        steps,
        [whole(K, rows), whole(1, rows), whole(K, 1)]
        + act_specs(rows, f, 0, lambda i: (i + first) * UNROLL)
        + [pl.BlockSpec(memory_space=pl.ANY)] * len(more),
        jax.ShapeDtypeStruct((n // 2, K, f), F32),
        pl.BlockSpec((UNROLL, K, f), lambda i, me: (i + first, 0, 0)),
        acts,
        [pltpu.VMEM((K, rows), BF16)],
        {4 + UNROLL: 0} if more else {},
    )(me, probed, row_data, inv, *[acts] * UNROLL, *more)


def alpha_kernel(along, current, total_weight, alpha_t, inverse):
    now = current[...]
    curvature = (along[...] - precise(now, now)) / total_weight[...] + RIDGE * now
    alpha, inv = solve_positive(beside(symmetric(curvature), now), beside(now, identity()))
    alpha_t[...] = alpha.T
    inverse[...] = symmetric(inv)


def offset_kernel(base_a, base_b, current, total_weight, offset):
    base = jnp.concatenate([base_a[...], base_b[...]], axis=0)
    offset[...] = RIDGE * base - precise(current[...] / total_weight[...], base)


def before_kernel(current, renewed, mixed, beta_t, total_weight, fixed, cross_t):
    now, beta, weight = current[...], beta_t[...], total_weight[...]
    cross = mixed[...] + outer(now, beta)
    length = renewed[...] + outer(mixed[...].T, beta) + precise(beta, cross)
    turned = cross.T
    cross_t[...] = turned
    fixed[...] = RIDGE * length - outer(turned, turned) / weight


def last_kernel(
    along, fixed, cross_t, renewed, beta_t, alpha_t, total_weight, back_row, base_a, base_b, image_a, image_b,
    solved, rest, on_panel,
):
    weight = total_weight[...]
    curvature = symmetric(along[...] / weight + fixed[...])
    step = solve_positive(beside(curvature, renewed[...]))[0].T
    on_panel[...] = step * (back_row[...] / weight)
    alpha = alpha_t[...]
    all_three = precise(step, jnp.concatenate([identity() + beta_t[...], alpha, cross_t[...]], axis=1))
    direction_base, direction_image = all_three[:, :K], all_three[:, K : 2 * K]
    crossed = all_three[:, 2 * K :] / weight
    both = jnp.concatenate([base_a[...], base_b[...], image_a[...], image_b[...]], axis=0)
    solved[...] = precise(beside(alpha + direction_base, -direction_image), both)
    rest[...] = precise(
        beside(identity() - RIDGE * direction_base + crossed, RIDGE * direction_image - alpha), both
    )


def small(kernel, name, outs, *args):
    return pl.pallas_call(
        kernel, out_shape=tuple(jax.ShapeDtypeStruct(shape, F32) for shape in outs), name=name,
        cost_estimate=pl.CostEstimate(flops=1 << 26, bytes_accessed=1 << 20, transcendentals=0),
    )(*args)


def plain(n):
    return lambda value, bit: swap(value.astype(F16), bit, n).astype(F32)


def split_blocks(value, left, bit):
    axis = left.index(bit)
    keep = lax.index_in_dim(value, 0, axis, keepdims=False)
    send = lax.index_in_dim(value, 1, axis, keepdims=False)
    return keep, send, [other for other in left if other != bit]


def reduce_scatter(blocks, n, swap_a, swap_b, along, waiting, work=None, args=(), along_ends=True):
    bits = n.bit_length() - 2
    shape = (2,) * bits + (HALF, blocks.shape[2])
    a, b = blocks[:, :HALF].reshape(shape), blocks[:, HALF:].reshape(shape)
    left_a = left_b = [1 << i for i in range(bits, 0, -1)]
    order_a, order_b = hop_bits(n)
    waiting, done = list(waiting), ()
    for phase, (bit_a, bit_b) in enumerate(zip(order_a, order_b)):
        keep_a, send_a, left_a = split_blocks(a, left_a, bit_a)
        keep_b, send_b, left_b = split_blocks(b, left_b, bit_b)
        tied = args if phase == 1 else done
        send_a, send_b, along, tied = lax.optimization_barrier((send_a, send_b, along, tied))
        a, b = keep_a + swap_a(send_a, bit_a), keep_b + swap_b(send_b, bit_b)
        if waiting:
            along = along + swap(along, waiting.pop(0), n)
        if work is not None and phase >= 1:
            done = work(*tied) if phase == 1 else tied
    if along_ends:
        a, b, along = lax.optimization_barrier((a, b, along))
    return a, b, along, done


class Root:
    def __init__(self, n, bound):
        self.n, self.scale = n, TOP / bound**0.5

    def __call__(self, send, bit):
        root = jnp.sqrt(jnp.abs(send)) * self.scale
        got = swap(jnp.where(send < 0, -root, root).astype(F16), bit, self.n).astype(F32)
        return got * jnp.abs(got) * (1.0 / self.scale**2)


def gather(top, low, n, orders, acts, work=None, args=()):
    a, b = top.astype(BF16)[None], low.astype(BF16)[None]
    done = ()
    for phase, (bit_a, bit_b) in enumerate(zip(*orders)):
        tied = args if phase == 1 else done
        a, b, tied, acts = lax.optimization_barrier((a, b, tied, acts))
        if work is not None and phase >= 1:
            done = work(*tied) if phase == 1 else tied
        a = jnp.concatenate([a, swap(a, bit_a, n)], axis=0)
        b = jnp.concatenate([b, swap(b, bit_b, n)], axis=0)
    near, a, b = lax.optimization_barrier((load(acts), a, b))
    return (a, b), (swap(a, 1, n), swap(b, 1, n)), near, done


def per_device(n, activations, labels, counts):
    rows, d = activations.shape
    activations = pltpu.with_memory_space_constraint(activations, pltpu.HBM)
    me = lax.axis_index("dp").astype(jnp.int32).reshape(1)
    row_data = (counts * K + labels).reshape(1, rows)
    order_y, order_z = hop_bits(n)
    order_a, order_b = order_y[::-1], order_z[::-1]
    shifts = [[bit.bit_length() - 1 for bit in order] for order in (order_a, order_b)]

    root = Root(n, BOUND * 4 * rows * n)
    sent, weight = class_sums(me, row_data, activations, n, 1)
    weight = weight.T
    got = root(sent, 1)
    weight = weight + swap(weight, 1, n)
    kept, _ = class_sums(me, row_data, activations, n, 0)
    top, low, weight, _ = reduce_scatter(kept + got, n, root, root, weight, order_y)
    class_weight = weight.T
    total_weight = jnp.sum(class_weight, keepdims=True)
    factor = 1.0 / jnp.sqrt(class_weight)
    base = top * factor[:HALF], low * factor[HALF:]

    def scatter(close, probed, along, inv, sent, early, work, args):
        hop = plain(n)
        got = hop(sent, 1)
        along = along + swap(along, 1, n)
        waiting = order_y
        if early:
            kept = panel_keep(me, probed, row_data, inv, close, n, 0)
            kept, along = lax.optimization_barrier((kept, along))
            along = along + swap(along, waiting[0], n)
            kept = panel_keep(me, probed, row_data, inv, close, n, 1, kept)
            waiting = waiting[1:]
        else:
            kept = panel_keep(me, probed, row_data, inv, close, n)
        return reduce_scatter(kept + got, n, hop, hop, along, waiting, work, args, not early)

    square, strip = (K, K), (K, d // n)
    orders = order_a, order_b
    base_near, base_far, close, _ = gather(*base, n, orders, activations)
    starts = probe(me, (base_near,), close, n, shifts)
    first, along, inv, back, _, sent, current = probe_and_send(
        me, (base_far,), close, row_data, total_weight, starts, (), n, shifts
    )
    panel_a, panel_b, along, (offset,) = scatter(
        close, first, along, inv, sent, False,
        lambda *args: small(offset_kernel, "offset", (strip,), *args), (*base, current, total_weight),
    )
    back = back / total_weight
    image = panel_a * back[:HALF] + offset[:HALF], panel_b * back[HALF:] + offset[HALF:]

    near, far, close, (alpha_t, inverse) = gather(
        *image, n, orders, activations,
        lambda *args: small(alpha_kernel, "alpha", (square,) * 2, *args), (along, current, total_weight),
    )
    starts = probe(me, (near, base_near), close, n, shifts)
    probed, along, inv, _, back_row, sent, _, _, renewed, mixed, beta_t = probe_and_send(
        me, (far, base_far), close, row_data, total_weight, starts, (first, current, alpha_t, inverse), n, shifts
    )
    panel_a, panel_b, along, (fixed, cross_t) = scatter(
        close, probed, along, inv, sent, True,
        lambda *args: small(before_kernel, "before", (square,) * 2, *args),
        (current, renewed, mixed, beta_t, total_weight),
    )
    solved, rest, on_panel = small(
        last_kernel, "last", (strip, strip, square),
        along, fixed, cross_t, renewed, beta_t, alpha_t, total_weight, back_row, *base, *image,
    )
    residual = rest - precise(on_panel, jnp.concatenate([panel_a, panel_b], axis=0))
    return (solved.T, residual.T)


def solution(mesh):
    in_specs = (P(("groups", "dp"), None), P(("groups", "dp")), P(("groups", "dp")))
    out_specs = (P(("groups", "dp"), None), P(("groups", "dp"), None))
    return jax.shard_map(
        functools.partial(per_device, mesh.shape["dp"]),
        mesh=mesh,
        in_specs=in_specs,
        out_specs=out_specs,
        check_vma=False,
    )
```

```python
import functools

import jax
import jax.numpy as jnp
from jax import lax
from jax.experimental import pallas as pl
from jax.experimental.pallas import tpu as pltpu
from jax.sharding import PartitionSpec as P

K = 64
HALF = K // 2
RIDGE = 0.1
BOUND = 18.0
TOP = 60000.0
TINY = 1e-30
UNROLL = 2
F32, BF16, F16 = jnp.float32, jnp.bfloat16, jnp.float16


def precise(left, right):
    return jnp.dot(left, right, precision=lax.Precision.HIGHEST, preferred_element_type=F32)


def outer(left, right):
    return lax.dot_general(
        left, right, (((1,), (1,)), ((), ())), precision=lax.Precision.HIGHEST, preferred_element_type=F32
    )


def symmetric(matrix):
    return 0.5 * (matrix + matrix.T)


def solve_positive(*works):
    index = lax.broadcasted_iota(jnp.int32, (K, 1), 0)
    works = list(works)
    for first in range(0, K, 8):
        spread = [[jnp.broadcast_to(w[:, first + j : first + j + 1], w.shape) for j in range(8)] for w in works]
        for k in range(8):
            at = slice(first + k, first + k + 1)
            row = index == first + k
            for i, columns in enumerate(spread):
                column, inv = columns[k], 1.0 / columns[k][at]
                scaled = works[i][at] * inv
                works[i] = jnp.where(row, scaled, works[i] - column * scaled)
                for j in range(k + 1, 8):
                    scaled = columns[j][at] * inv
                    columns[j] = jnp.where(row, scaled, columns[j] - column * scaled)
    return [work[:, K:] for work in works]


def beside(matrix, target):
    return jnp.concatenate([matrix, target], axis=1)


def identity():
    eye = lax.broadcasted_iota(jnp.int32, (K, K), 0) == lax.broadcasted_iota(jnp.int32, (K, K), 1)
    return jnp.where(eye, 1.0, 0.0)


def swap(value, bit, n):
    return lax.ppermute(value, "dp", [(i, i ^ bit) for i in range(n)])


def quad(value, n):
    return (value + swap(value, 1, n)) + (swap(value, 2, n) + swap(value, 3, n))


def hop_bits(n):
    bits = [1 << i for i in range(1, n.bit_length() - 1)]
    return bits, bits[1:] + bits[:1]


def _pos(j, shifts):
    p = 0
    for place, shift in enumerate(shifts):
        p = p | (((j >> shift) & 1) << place)
    return p


def block_copy(acts, kept, sems, me, half, t):
    f = kept.shape[2]
    first = pl.multiple_of((me[0] ^ (2 * t + half)) * f, f)
    return pltpu.make_async_copy(acts.at[:, pl.ds(first, f)], kept.at[t], sems.at[t])


def start_copies(acts, kept, sems, me, half):
    def start(t, carry):
        block_copy(acts, kept, sems, me, half, t).start()
        return carry

    lax.fori_loop(0, kept.shape[0], start, 0)


def whole(*shape):
    return pl.BlockSpec(shape, lambda i, me: (0,) * len(shape))


HBM = pl.BlockSpec(memory_space=pltpu.HBM)


def call(kernel, name, n, grid, in_specs, out_shapes, out_specs, acts, scratch=()):
    rows, d = acts.shape
    return pl.pallas_call(
        kernel,
        out_shape=out_shapes,
        grid_spec=pltpu.PrefetchScalarGridSpec(
            num_scalar_prefetch=1,
            grid=(grid,),
            in_specs=in_specs,
            out_specs=out_specs,
            scratch_shapes=[
                pltpu.VMEM((n // 2, rows, d // n), BF16),
                pltpu.SemaphoreType.DMA((n // 2,)),
                *scratch,
            ],
        ),
        compiler_params=pltpu.CompilerParams(vmem_limit_bytes=20 << 20),
        cost_estimate=pl.CostEstimate(flops=K * rows * d, bytes_accessed=rows * d + 2 * K * d, transcendentals=0),
        name=name,
    )


def count_of(row_data):
    return lax.shift_right_logical(row_data[...], 6).astype(F32)


def sums_kernel(half, me, row_data, acts, out, weight, kept, sems, member):
    step = pl.program_id(0)

    @pl.when(step == 0)
    def _():
        start_copies(acts, kept, sems, me, half)
        concept = lax.broadcasted_iota(jnp.int32, member.shape, 0)
        label = row_data[...] & (K - 1)
        full = jnp.where(label == concept, count_of(row_data), 0.0)
        member[...] = full.astype(BF16)
        weight[...] = jnp.sum(full, axis=1, keepdims=True)

    for u in range(UNROLL):
        t = step * UNROLL + u
        block_copy(acts, kept, sems, me, half, t).wait()
        out[u] = jnp.dot(member[...], kept[t], preferred_element_type=F32)


def class_sums(me, row_data, acts, n, half):
    rows, d = acts.shape
    f = d // n
    return call(
        functools.partial(sums_kernel, half),
        "class_sums",
        n,
        n // 2 // UNROLL,
        [whole(1, rows), HBM],
        (
            jax.ShapeDtypeStruct((n // 2, K, f), F32),
            jax.ShapeDtypeStruct((K, 1), F32),
        ),
        (pl.BlockSpec((UNROLL, K, f), lambda i, me: (i, 0, 0)), whole(K, 1)),
        acts,
        [pltpu.VMEM((K, rows), BF16)],
    )(me, row_data, acts)


def inner(left, right):
    return lax.dot_general(left, right, (((1,), (1,)), ((), ())), preferred_element_type=F32)


def panel_operands(panels, n, f, shifts):
    last = n // 2 // UNROLL - 1
    specs, operands = [], []
    for panel in panels:
        for u in range(UNROLL):
            for stream, order in zip(panel, shifts):
                pick = lambda i, me, u=u, order=order: (_pos(2 * (jnp.minimum(i, last) * UNROLL + u), order), 0, 0)
                specs.append(pl.BlockSpec((1, HALF, f), pick))
                operands.append(stream)
    return specs, operands


def add_blocks(refs, count, block, probed, grams):
    total = probed[...]
    sums = [gram[...] for gram in grams]
    for u in range(UNROLL):
        at = [2 * (panel * UNROLL + u) for panel in range(count)]
        both = [jnp.concatenate([refs[i][0], refs[i + 1][0]], axis=0) for i in at]
        total = total + inner(block(u), both[0])
        sums = [x + inner(other, both[0]) for x, other in zip(sums, both)]
    probed[...] = total
    for gram, x in zip(grams, sums):
        gram[...] = x


def load_kernel(acts, out, sems):
    count = sems.shape[0]
    f = acts.shape[1] // count

    def copy(t):
        columns = pl.ds(pl.multiple_of(t * f, f), f)
        return pltpu.make_async_copy(acts.at[:, columns], out.at[:, columns], sems.at[t])

    lax.fori_loop(0, count, lambda t, c: (copy(t).start(), c)[1], 0)
    lax.fori_loop(0, count, lambda t, c: (copy(t).wait(), c)[1], 0)


def load(acts):
    return pl.pallas_call(
        load_kernel,
        out_shape=jax.ShapeDtypeStruct(acts.shape, acts.dtype),
        in_specs=[HBM],
        out_specs=pl.BlockSpec(memory_space=pltpu.VMEM),
        scratch_shapes=[pltpu.SemaphoreType.DMA((8,))],
        compiler_params=pltpu.CompilerParams(vmem_limit_bytes=16 << 20),
        cost_estimate=pl.CostEstimate(flops=0, bytes_accessed=4 * acts.size, transcendentals=0),
        name="load",
    )(acts)


def near_call(kernel, name, n, grid, in_specs, out_shapes, out_specs, acts, scratch=()):
    rows, d = acts.shape
    return pl.pallas_call(
        kernel,
        out_shape=out_shapes,
        grid_spec=pltpu.PrefetchScalarGridSpec(
            num_scalar_prefetch=1, grid=(grid,), in_specs=in_specs, out_specs=out_specs, scratch_shapes=scratch
        ),
        compiler_params=pltpu.CompilerParams(vmem_limit_bytes=12 << 20),
        cost_estimate=pl.CostEstimate(flops=K * rows * d, bytes_accessed=rows * d + 2 * K * d, transcendentals=0),
        name=name,
    )


def act_specs(rows, f, half, block):
    return [
        pl.BlockSpec((rows, f), lambda i, me, u=u: (0, me[0] ^ (2 * (block(i) + u) + half))) for u in range(UNROLL)
    ]


def probe_kernel(count, me, *refs):
    panels, acts, outs = refs[: 2 * UNROLL * count], refs[2 * UNROLL * count : -1 - count], refs[-1 - count :]
    probed, *grams = outs

    @pl.when(pl.program_id(0) == 0)
    def _():
        for ref in outs:
            ref[...] = jnp.zeros_like(ref)

    add_blocks(panels, count, lambda u: acts[u][...], probed, grams)


def probe(me, panels, acts, n, shifts):
    rows, d = acts.shape
    f = d // n
    count = len(panels)
    specs, operands = panel_operands(panels, n, f, shifts)
    return near_call(
        functools.partial(probe_kernel, count),
        "probe",
        n,
        n // 2 // UNROLL,
        specs + act_specs(rows, f, 0, lambda i: i * UNROLL),
        (jax.ShapeDtypeStruct((rows, K), F32),) + (jax.ShapeDtypeStruct((K, K), F32),) * count,
        (whole(rows, K),) + (whole(K, K),) * count,
        acts,
    )(me, *operands, *[acts] * UNROLL)


def diagonal(matrix):
    kept = matrix * identity()
    return jnp.sum(kept, axis=1, keepdims=True), jnp.sum(kept, axis=0, keepdims=True)


def finish_first(gram):
    current = symmetric(gram[...])
    gram[...] = current
    return jnp.sqrt(diagonal(current)[0])


def finish_second(probed, image_image, base_image, more):
    first, current, alpha_t, inverse, renewed, mixed, beta_t = more
    both = jnp.concatenate([base_image[...], symmetric(image_image[...])], axis=0)
    moved = outer(both, alpha_t[...])
    moved, twice = moved[:K], precise(alpha_t[...], moved[K:])
    new = symmetric(current[...] - moved - moved.T + twice)
    beta = precise(new, inverse[...])
    renewed[...] = new
    mixed[...] = current[...] - moved
    beta_t[...] = beta
    mix = jnp.concatenate([beta, -alpha_t[...]], axis=1)
    probed[...] = first[...] + precise(mix, jnp.concatenate([first[...], probed[...]], axis=0))
    base_col, base_row = diagonal(current[...])
    _, image_row = diagonal(image_image[...])
    norms = jnp.sqrt(base_col)
    norms += jnp.sum(jnp.abs(beta) * jnp.sqrt(base_row), axis=1, keepdims=True)
    return norms + jnp.sum(jnp.abs(alpha_t[...]) * jnp.sqrt(image_row), axis=1, keepdims=True)


def send_kernel(steps, count, d, me, *refs):
    second = count == 2
    parts = [2 * UNROLL * count, UNROLL, 3, count, 4 * second, 6, count, 3 * second, 2]
    refs = list(refs)
    panels, acts, ins, starts, given, outs, grams, made, scratch = (
        [refs.pop(0) for _ in range(size)] for size in parts
    )
    row_data, total_weight, start = ins
    probed, along, inv, back, back_row, out = outs
    weighted, sum_of = scratch
    step = pl.program_id(0)

    @pl.when(step == 0)
    def _():
        for ref, begin in zip((sum_of, *grams), (start, *starts)):
            ref[...] = begin[...]

    @pl.when(step < steps)
    def _():
        add_blocks(panels, count, lambda u: acts[u][...], sum_of, grams)

    @pl.when(step == steps)
    def _():
        probed[...] = sum_of[...].T
        norms = finish_second(probed, *grams, (*given, *made)) if second else finish_first(*grams)
        bound = jnp.maximum((1.02 * BOUND * BOUND * d**0.5) * total_weight[...] * norms, TINY)
        inv[...] = TOP / bound
        back[...] = bound * (1.0 / TOP)
        back_row[...] = jnp.sum(bound * (1.0 / TOP) * identity(), axis=0, keepdims=True)
        weighted[...] = (count_of(row_data) * probed[...]).astype(BF16)
        along[...] = outer(probed[...], weighted[...].astype(F32))

    @pl.when(step >= steps)
    def _():
        for u in range(UNROLL):
            block = jnp.dot(weighted[...], acts[u][...], preferred_element_type=F32)
            out[u] = block * inv[...]


def probe_and_send(me, panels, acts, row_data, total_weight, starts, given, n, shifts):
    rows, d = acts.shape
    f = d // n
    s = n // 2 // UNROLL
    count = len(panels)
    square = jax.ShapeDtypeStruct((K, K), F32)
    made = 3 if given else 0
    specs, operands = panel_operands(panels, n, f, shifts)
    return near_call(
        functools.partial(send_kernel, s, count, d),
        "probe_and_send",
        n,
        2 * s,
        specs
        + act_specs(rows, f, 1, lambda i: jnp.where(i < s, i, i - s) * UNROLL)
        + [whole(1, rows), whole(1, 1)]
        + [whole(*x.shape) for x in (*starts, *given)],
        (
            jax.ShapeDtypeStruct((K, rows), F32),
            square,
            jax.ShapeDtypeStruct((K, 1), F32),
            jax.ShapeDtypeStruct((K, 1), F32),
            jax.ShapeDtypeStruct((1, K), F32),
            jax.ShapeDtypeStruct((n // 2, K, f), F32),
        )
        + (square,) * (count + made),
        (
            whole(K, rows),
            whole(K, K),
            whole(K, 1),
            whole(K, 1),
            whole(1, K),
            pl.BlockSpec((UNROLL, K, f), lambda i, me: (jnp.maximum(i - s, 0), 0, 0)),
        )
        + (whole(K, K),) * (count + made),
        acts,
        [pltpu.VMEM((K, rows), BF16), pltpu.VMEM((rows, K), F32)],
    )(me, *operands, *[acts] * UNROLL, row_data, total_weight, *starts, *given)


def keep_kernel(me, probed, row_data, inv, *refs):
    acts, out, weighted = refs[:UNROLL], refs[-2], refs[-1]

    @pl.when(pl.program_id(0) == 0)
    def _():
        weighted[...] = (count_of(row_data) * probed[...]).astype(BF16)

    for u in range(UNROLL):
        out[u] = jnp.dot(weighted[...], acts[u][...], preferred_element_type=F32) * inv[...]


def panel_keep(me, probed, row_data, inv, acts, n):
    rows, d = acts.shape
    f = d // n
    return near_call(
        keep_kernel,
        "panel_keep",
        n,
        n // 2 // UNROLL,
        [whole(K, rows), whole(1, rows), whole(K, 1)] + act_specs(rows, f, 0, lambda i: i * UNROLL),
        jax.ShapeDtypeStruct((n // 2, K, f), F32),
        pl.BlockSpec((UNROLL, K, f), lambda i, me: (i, 0, 0)),
        acts,
        [pltpu.VMEM((K, rows), BF16)],
    )(me, probed, row_data, inv, *[acts] * UNROLL)


def alpha_kernel(along, current, total_weight, alpha_t, inverse):
    now = current[...]
    curvature = (along[...] - precise(now, now)) / total_weight[...] + RIDGE * now
    alpha, inv = solve_positive(beside(symmetric(curvature), now), beside(now, identity()))
    alpha_t[...] = alpha.T
    inverse[...] = symmetric(inv)


def offset_kernel(base_a, base_b, current, total_weight, offset):
    base = jnp.concatenate([base_a[...], base_b[...]], axis=0)
    offset[...] = RIDGE * base - precise(current[...] / total_weight[...], base)


def before_kernel(current, renewed, mixed, beta_t, total_weight, fixed, cross_t):
    now, beta, weight = current[...], beta_t[...], total_weight[...]
    cross = mixed[...] + outer(now, beta)
    length = renewed[...] + outer(mixed[...].T, beta) + precise(beta, cross)
    turned = cross.T
    cross_t[...] = turned
    fixed[...] = RIDGE * length - outer(turned, turned) / weight


def last_kernel(
    along, fixed, cross_t, renewed, beta_t, alpha_t, total_weight, back_row, base_a, base_b, image_a, image_b,
    solved, rest, on_panel,
):
    weight = total_weight[...]
    curvature = symmetric(along[...] / weight + fixed[...])
    step = solve_positive(beside(curvature, renewed[...]))[0].T
    on_panel[...] = step * (back_row[...] / weight)
    alpha = alpha_t[...]
    all_three = precise(step, jnp.concatenate([identity() + beta_t[...], alpha, cross_t[...]], axis=1))
    direction_base, direction_image = all_three[:, :K], all_three[:, K : 2 * K]
    crossed = all_three[:, 2 * K :] / weight
    both = jnp.concatenate([base_a[...], base_b[...], image_a[...], image_b[...]], axis=0)
    solved[...] = precise(beside(alpha + direction_base, -direction_image), both)
    rest[...] = precise(
        beside(identity() - RIDGE * direction_base + crossed, RIDGE * direction_image - alpha), both
    )


def small(kernel, name, outs, *args):
    return pl.pallas_call(
        kernel, out_shape=tuple(jax.ShapeDtypeStruct(shape, F32) for shape in outs), name=name,
        cost_estimate=pl.CostEstimate(flops=1 << 26, bytes_accessed=1 << 20, transcendentals=0),
    )(*args)


def plain(n):
    return lambda value, bit: swap(value.astype(F16), bit, n).astype(F32)


def split_blocks(value, left, bit):
    axis = left.index(bit)
    keep = lax.index_in_dim(value, 0, axis, keepdims=False)
    send = lax.index_in_dim(value, 1, axis, keepdims=False)
    return keep, send, [other for other in left if other != bit]


def reduce_scatter(blocks, n, swap_a, swap_b, along, waiting, work=None, args=()):
    bits = n.bit_length() - 2
    shape = (2,) * bits + (HALF, blocks.shape[2])
    a, b = blocks[:, :HALF].reshape(shape), blocks[:, HALF:].reshape(shape)
    left_a = left_b = [1 << i for i in range(bits, 0, -1)]
    order_a, order_b = hop_bits(n)
    waiting, done = list(waiting), ()
    for phase, (bit_a, bit_b) in enumerate(zip(order_a, order_b)):
        keep_a, send_a, left_a = split_blocks(a, left_a, bit_a)
        keep_b, send_b, left_b = split_blocks(b, left_b, bit_b)
        tied = args if phase == 1 else done
        send_a, send_b, along, tied = lax.optimization_barrier((send_a, send_b, along, tied))
        a, b = keep_a + swap_a(send_a, bit_a), keep_b + swap_b(send_b, bit_b)
        if waiting:
            along = along + swap(along, waiting.pop(0), n)
        if work is not None and phase >= 1:
            done = work(*tied) if phase == 1 else tied
    return a, b, along, done


class Root:
    def __init__(self, n, bound):
        self.n, self.scale = n, TOP / bound**0.5

    def __call__(self, send, bit):
        root = jnp.sqrt(jnp.abs(send)) * self.scale
        got = swap(jnp.where(send < 0, -root, root).astype(F16), bit, self.n).astype(F32)
        return got * jnp.abs(got) * (1.0 / self.scale**2)


def gather(top, low, n, orders, acts, work=None, args=()):
    a, b = top.astype(BF16)[None], low.astype(BF16)[None]
    done = ()
    for phase, (bit_a, bit_b) in enumerate(zip(*orders)):
        tied = args if phase == 1 else done
        a, b, tied, acts = lax.optimization_barrier((a, b, tied, acts))
        if work is not None and phase >= 1:
            done = work(*tied) if phase == 1 else tied
        a = jnp.concatenate([a, swap(a, bit_a, n)], axis=0)
        b = jnp.concatenate([b, swap(b, bit_b, n)], axis=0)
    near, a, b = lax.optimization_barrier((load(acts), a, b))
    return (a, b), (swap(a, 1, n), swap(b, 1, n)), near, done


def per_device(n, activations, labels, counts):
    rows, d = activations.shape
    activations = pltpu.with_memory_space_constraint(activations, pltpu.HBM)
    me = lax.axis_index("dp").astype(jnp.int32).reshape(1)
    row_data = (counts * K + labels).reshape(1, rows)
    order_y, order_z = hop_bits(n)
    order_a, order_b = order_y[::-1], order_z[::-1]
    shifts = [[bit.bit_length() - 1 for bit in order] for order in (order_a, order_b)]

    root = Root(n, BOUND * 4 * rows * n)
    sent, weight = class_sums(me, row_data, activations, n, 1)
    weight = weight.T
    got = root(sent, 1)
    weight = quad(weight, n)
    kept, _ = class_sums(me, row_data, activations, n, 0)
    top, low, weight, _ = reduce_scatter(kept + got, n, root, root, weight, order_y[1:])
    class_weight = weight.T
    total_weight = jnp.sum(class_weight, keepdims=True)
    factor = 1.0 / jnp.sqrt(class_weight)
    base = top * factor[:HALF], low * factor[HALF:]

    def scatter(close, probed, along, inv, sent, work, args):
        hop = plain(n)
        got = hop(sent, 1)
        along = quad(along, n)
        kept = panel_keep(me, probed, row_data, inv, close, n)
        return reduce_scatter(kept + got, n, hop, hop, along, order_y[1:], work, args)

    square, strip = (K, K), (K, d // n)
    orders = order_a, order_b
    base_near, base_far, close, _ = gather(*base, n, orders, activations)
    starts = probe(me, (base_near,), close, n, shifts)
    first, along, inv, back, _, sent, current = probe_and_send(
        me, (base_far,), close, row_data, total_weight, starts, (), n, shifts
    )
    panel_a, panel_b, along, (offset,) = scatter(
        close, first, along, inv, sent,
        lambda *args: small(offset_kernel, "offset", (strip,), *args), (*base, current, total_weight),
    )
    back = back / total_weight
    image = panel_a * back[:HALF] + offset[:HALF], panel_b * back[HALF:] + offset[HALF:]

    near, far, close, (alpha_t, inverse) = gather(
        *image, n, orders, activations,
        lambda *args: small(alpha_kernel, "alpha", (square,) * 2, *args), (along, current, total_weight),
    )
    starts = probe(me, (near, base_near), close, n, shifts)
    probed, along, inv, _, back_row, sent, _, _, renewed, mixed, beta_t = probe_and_send(
        me, (far, base_far), close, row_data, total_weight, starts, (first, current, alpha_t, inverse), n, shifts
    )
    panel_a, panel_b, along, (fixed, cross_t) = scatter(
        close, probed, along, inv, sent,
        lambda *args: small(before_kernel, "before", (square,) * 2, *args),
        (current, renewed, mixed, beta_t, total_weight),
    )
    solved, rest, on_panel = small(
        last_kernel, "last", (strip, strip, square),
        along, fixed, cross_t, renewed, beta_t, alpha_t, total_weight, back_row, *base, *image,
    )
    residual = (rest - precise(on_panel[:, HALF:], panel_b)) - precise(on_panel[:, :HALF], panel_a)
    return (solved.T, residual.T)


def solution(mesh):
    in_specs = (P(("groups", "dp"), None), P(("groups", "dp")), P(("groups", "dp")))
    out_specs = (P(("groups", "dp"), None), P(("groups", "dp"), None))
    return jax.shard_map(
        functools.partial(per_device, mesh.shape["dp"]),
        mesh=mesh,
        in_specs=in_specs,
        out_specs=out_specs,
        check_vma=False,
    )
```

```python
import functools

import jax
import jax.numpy as jnp
from jax import lax
from jax.experimental import pallas as pl
from jax.experimental.pallas import tpu as pltpu
from jax.sharding import PartitionSpec as P

K = 64
HALF = K // 2
RIDGE = 0.1
BOUND = 18.0
TOP = 60000.0
TINY = 1e-30
UNROLL = 2
F32, BF16, F16 = jnp.float32, jnp.bfloat16, jnp.float16


def precise(left, right):
    return jnp.dot(left, right, precision=lax.Precision.HIGHEST, preferred_element_type=F32)


def outer(left, right):
    return lax.dot_general(
        left, right, (((1,), (1,)), ((), ())), precision=lax.Precision.HIGHEST, preferred_element_type=F32
    )


def symmetric(matrix):
    return 0.5 * (matrix + matrix.T)


def solve_positive(*works):
    index = lax.broadcasted_iota(jnp.int32, (K, 1), 0)
    works = list(works)
    for first in range(0, K, 8):
        spread = [[jnp.broadcast_to(w[:, first + j : first + j + 1], w.shape) for j in range(8)] for w in works]
        for k in range(8):
            at = slice(first + k, first + k + 1)
            row = index == first + k
            for i, columns in enumerate(spread):
                column, inv = columns[k], 1.0 / columns[k][at]
                scaled = works[i][at] * inv
                works[i] = jnp.where(row, scaled, works[i] - column * scaled)
                for j in range(k + 1, 8):
                    scaled = columns[j][at] * inv
                    columns[j] = jnp.where(row, scaled, columns[j] - column * scaled)
    return [work[:, K:] for work in works]


def beside(matrix, target):
    return jnp.concatenate([matrix, target], axis=1)


def identity():
    eye = lax.broadcasted_iota(jnp.int32, (K, K), 0) == lax.broadcasted_iota(jnp.int32, (K, K), 1)
    return jnp.where(eye, 1.0, 0.0)


def swap(value, bit, n):
    return lax.ppermute(value, "dp", [(i, i ^ bit) for i in range(n)])


def hop_bits(n):
    bits = [1 << i for i in range(1, n.bit_length() - 1)]
    return bits, bits[1:] + bits[:1]


def _pos(j, shifts):
    p = 0
    for place, shift in enumerate(shifts):
        p = p | (((j >> shift) & 1) << place)
    return p


def block_copy(acts, kept, sems, me, half, t):
    f = kept.shape[2]
    first = pl.multiple_of((me[0] ^ (2 * t + half)) * f, f)
    return pltpu.make_async_copy(acts.at[:, pl.ds(first, f)], kept.at[t], sems.at[t])


def start_copies(acts, kept, sems, me, half):
    def start(t, carry):
        block_copy(acts, kept, sems, me, half, t).start()
        return carry

    lax.fori_loop(0, kept.shape[0], start, 0)


def whole(*shape):
    return pl.BlockSpec(shape, lambda i, me: (0,) * len(shape))


HBM = pl.BlockSpec(memory_space=pltpu.HBM)


def call(kernel, name, n, grid, in_specs, out_shapes, out_specs, acts, scratch=(), aliases=None):
    rows, d = acts.shape
    return pl.pallas_call(
        kernel,
        out_shape=out_shapes,
        grid_spec=pltpu.PrefetchScalarGridSpec(
            num_scalar_prefetch=1,
            grid=(grid,),
            in_specs=in_specs,
            out_specs=out_specs,
            scratch_shapes=[
                pltpu.VMEM((n // 2, rows, d // n), BF16),
                pltpu.SemaphoreType.DMA((n // 2,)),
                *scratch,
            ],
        ),
        compiler_params=pltpu.CompilerParams(vmem_limit_bytes=20 << 20),
        cost_estimate=pl.CostEstimate(flops=K * rows * d, bytes_accessed=rows * d + 2 * K * d, transcendentals=0),
        input_output_aliases=aliases or {},
        name=name,
    )


def count_of(row_data):
    return lax.shift_right_logical(row_data[...], 6).astype(F32)


def sums_kernel(half, me, row_data, acts, out, weight, kept, sems, member):
    step = pl.program_id(0)

    @pl.when(step == 0)
    def _():
        start_copies(acts, kept, sems, me, half)
        concept = lax.broadcasted_iota(jnp.int32, member.shape, 0)
        label = row_data[...] & (K - 1)
        full = jnp.where(label == concept, count_of(row_data), 0.0)
        member[...] = full.astype(BF16)
        weight[...] = jnp.sum(full, axis=1, keepdims=True)

    for u in range(UNROLL):
        t = step * UNROLL + u
        block_copy(acts, kept, sems, me, half, t).wait()
        out[u] = jnp.dot(member[...], kept[t], preferred_element_type=F32)


def class_sums(me, row_data, acts, n, half):
    rows, d = acts.shape
    f = d // n
    return call(
        functools.partial(sums_kernel, half),
        "class_sums",
        n,
        n // 2 // UNROLL,
        [whole(1, rows), HBM],
        (
            jax.ShapeDtypeStruct((n // 2, K, f), F32),
            jax.ShapeDtypeStruct((K, 1), F32),
        ),
        (pl.BlockSpec((UNROLL, K, f), lambda i, me: (i, 0, 0)), whole(K, 1)),
        acts,
        [pltpu.VMEM((K, rows), BF16)],
    )(me, row_data, acts)


def inner(left, right):
    return lax.dot_general(left, right, (((1,), (1,)), ((), ())), preferred_element_type=F32)


def panel_operands(panels, n, f, shifts):
    last = n // 2 // UNROLL - 1
    specs, operands = [], []
    for panel in panels:
        for u in range(UNROLL):
            for stream, order in zip(panel, shifts):
                pick = lambda i, me, u=u, order=order: (_pos(2 * (jnp.minimum(i, last) * UNROLL + u), order), 0, 0)
                specs.append(pl.BlockSpec((1, HALF, f), pick))
                operands.append(stream)
    return specs, operands


def add_blocks(refs, count, block, probed, grams):
    total = probed[...]
    sums = [gram[...] for gram in grams]
    for u in range(UNROLL):
        at = [2 * (panel * UNROLL + u) for panel in range(count)]
        both = [jnp.concatenate([refs[i][0], refs[i + 1][0]], axis=0) for i in at]
        total = total + inner(block(u), both[0])
        sums = [x + inner(other, both[0]) for x, other in zip(sums, both)]
    probed[...] = total
    for gram, x in zip(grams, sums):
        gram[...] = x


def load_kernel(acts, out, sems):
    count = sems.shape[0]
    f = acts.shape[1] // count

    def copy(t):
        columns = pl.ds(pl.multiple_of(t * f, f), f)
        return pltpu.make_async_copy(acts.at[:, columns], out.at[:, columns], sems.at[t])

    lax.fori_loop(0, count, lambda t, c: (copy(t).start(), c)[1], 0)
    lax.fori_loop(0, count, lambda t, c: (copy(t).wait(), c)[1], 0)


def load(acts):
    return pl.pallas_call(
        load_kernel,
        out_shape=jax.ShapeDtypeStruct(acts.shape, acts.dtype),
        in_specs=[HBM],
        out_specs=pl.BlockSpec(memory_space=pltpu.VMEM),
        scratch_shapes=[pltpu.SemaphoreType.DMA((8,))],
        compiler_params=pltpu.CompilerParams(vmem_limit_bytes=16 << 20),
        cost_estimate=pl.CostEstimate(flops=0, bytes_accessed=4 * acts.size, transcendentals=0),
        name="load",
    )(acts)


def near_call(kernel, name, n, grid, in_specs, out_shapes, out_specs, acts, scratch=(), aliases=None):
    rows, d = acts.shape
    return pl.pallas_call(
        kernel,
        out_shape=out_shapes,
        grid_spec=pltpu.PrefetchScalarGridSpec(
            num_scalar_prefetch=1, grid=(grid,), in_specs=in_specs, out_specs=out_specs, scratch_shapes=scratch
        ),
        compiler_params=pltpu.CompilerParams(vmem_limit_bytes=12 << 20),
        cost_estimate=pl.CostEstimate(flops=K * rows * d, bytes_accessed=rows * d + 2 * K * d, transcendentals=0),
        input_output_aliases=aliases or {},
        name=name,
    )


def act_specs(rows, f, half, block):
    return [
        pl.BlockSpec((rows, f), lambda i, me, u=u: (0, me[0] ^ (2 * (block(i) + u) + half))) for u in range(UNROLL)
    ]


def probe_kernel(count, me, *refs):
    panels, acts, outs = refs[: 2 * UNROLL * count], refs[2 * UNROLL * count : -1 - count], refs[-1 - count :]
    probed, *grams = outs

    @pl.when(pl.program_id(0) == 0)
    def _():
        for ref in outs:
            ref[...] = jnp.zeros_like(ref)

    add_blocks(panels, count, lambda u: acts[u][...], probed, grams)


def probe(me, panels, acts, n, shifts):
    rows, d = acts.shape
    f = d // n
    count = len(panels)
    specs, operands = panel_operands(panels, n, f, shifts)
    return near_call(
        functools.partial(probe_kernel, count),
        "probe",
        n,
        n // 2 // UNROLL,
        specs + act_specs(rows, f, 0, lambda i: i * UNROLL),
        (jax.ShapeDtypeStruct((rows, K), F32),) + (jax.ShapeDtypeStruct((K, K), F32),) * count,
        (whole(rows, K),) + (whole(K, K),) * count,
        acts,
    )(me, *operands, *[acts] * UNROLL)


def diagonal(matrix):
    kept = matrix * identity()
    return jnp.sum(kept, axis=1, keepdims=True), jnp.sum(kept, axis=0, keepdims=True)


def finish_first(gram):
    current = symmetric(gram[...])
    gram[...] = current
    return jnp.sqrt(diagonal(current)[0])


def finish_second(probed, image_image, base_image, more):
    first, current, alpha_t, inverse, renewed, mixed, beta_t = more
    both = jnp.concatenate([base_image[...], symmetric(image_image[...])], axis=0)
    moved = outer(both, alpha_t[...])
    moved, twice = moved[:K], precise(alpha_t[...], moved[K:])
    new = symmetric(current[...] - moved - moved.T + twice)
    beta = precise(new, inverse[...])
    renewed[...] = new
    mixed[...] = current[...] - moved
    beta_t[...] = beta
    mix = jnp.concatenate([beta, -alpha_t[...]], axis=1)
    probed[...] = first[...] + precise(mix, jnp.concatenate([first[...], probed[...]], axis=0))
    base_col, base_row = diagonal(current[...])
    _, image_row = diagonal(image_image[...])
    norms = jnp.sqrt(base_col)
    norms += jnp.sum(jnp.abs(beta) * jnp.sqrt(base_row), axis=1, keepdims=True)
    return norms + jnp.sum(jnp.abs(alpha_t[...]) * jnp.sqrt(image_row), axis=1, keepdims=True)


def send_kernel(steps, count, d, me, *refs):
    second = count == 2
    parts = [2 * UNROLL * count, UNROLL, 3, count, 4 * second, 6, count, 3 * second, 2]
    refs = list(refs)
    panels, acts, ins, starts, given, outs, grams, made, scratch = (
        [refs.pop(0) for _ in range(size)] for size in parts
    )
    row_data, total_weight, start = ins
    probed, along, inv, back, back_row, out = outs
    weighted, sum_of = scratch
    step = pl.program_id(0)

    @pl.when(step == 0)
    def _():
        for ref, begin in zip((sum_of, *grams), (start, *starts)):
            ref[...] = begin[...]

    @pl.when(step < steps)
    def _():
        add_blocks(panels, count, lambda u: acts[u][...], sum_of, grams)

    @pl.when(step == steps)
    def _():
        probed[...] = sum_of[...].T
        norms = finish_second(probed, *grams, (*given, *made)) if second else finish_first(*grams)
        bound = jnp.maximum((1.02 * BOUND * BOUND * d**0.5) * total_weight[...] * norms, TINY)
        inv[...] = TOP / bound
        back[...] = bound * (1.0 / TOP)
        back_row[...] = jnp.sum(bound * (1.0 / TOP) * identity(), axis=0, keepdims=True)
        weighted[...] = (count_of(row_data) * probed[...]).astype(BF16)
        along[...] = outer(probed[...], weighted[...].astype(F32))

    @pl.when(step >= steps)
    def _():
        for u in range(UNROLL):
            block = jnp.dot(weighted[...], acts[u][...], preferred_element_type=F32)
            out[u] = block * inv[...]


def probe_and_send(me, panels, acts, row_data, total_weight, starts, given, n, shifts):
    rows, d = acts.shape
    f = d // n
    s = n // 2 // UNROLL
    count = len(panels)
    square = jax.ShapeDtypeStruct((K, K), F32)
    made = 3 if given else 0
    specs, operands = panel_operands(panels, n, f, shifts)
    return near_call(
        functools.partial(send_kernel, s, count, d),
        "probe_and_send",
        n,
        2 * s,
        specs
        + act_specs(rows, f, 1, lambda i: jnp.where(i < s, i, i - s) * UNROLL)
        + [whole(1, rows), whole(1, 1)]
        + [whole(*x.shape) for x in (*starts, *given)],
        (
            jax.ShapeDtypeStruct((K, rows), F32),
            square,
            jax.ShapeDtypeStruct((K, 1), F32),
            jax.ShapeDtypeStruct((K, 1), F32),
            jax.ShapeDtypeStruct((1, K), F32),
            jax.ShapeDtypeStruct((n // 2, K, f), F32),
        )
        + (square,) * (count + made),
        (
            whole(K, rows),
            whole(K, K),
            whole(K, 1),
            whole(K, 1),
            whole(1, K),
            pl.BlockSpec((UNROLL, K, f), lambda i, me: (jnp.maximum(i - s, 0), 0, 0)),
        )
        + (whole(K, K),) * (count + made),
        acts,
        [pltpu.VMEM((K, rows), BF16), pltpu.VMEM((rows, K), F32)],
    )(me, *operands, *[acts] * UNROLL, row_data, total_weight, *starts, *given)


def keep_kernel(me, probed, row_data, inv, *refs):
    acts, out, weighted = refs[:UNROLL], refs[-2], refs[-1]

    @pl.when(pl.program_id(0) == 0)
    def _():
        weighted[...] = (count_of(row_data) * probed[...]).astype(BF16)

    for u in range(UNROLL):
        out[u] = jnp.dot(weighted[...], acts[u][...], preferred_element_type=F32) * inv[...]


def panel_keep(me, probed, row_data, inv, acts, n, part=None, into=None):
    rows, d = acts.shape
    f = d // n
    steps = n // 2 // UNROLL
    first = 0
    if part is not None:
        steps //= 2
        first = part * steps
    more = () if into is None else (into,)
    return near_call(
        keep_kernel,
        "panel_keep",
        n,
        steps,
        [whole(K, rows), whole(1, rows), whole(K, 1)]
        + act_specs(rows, f, 0, lambda i: (i + first) * UNROLL)
        + [pl.BlockSpec(memory_space=pl.ANY)] * len(more),
        jax.ShapeDtypeStruct((n // 2, K, f), F32),
        pl.BlockSpec((UNROLL, K, f), lambda i, me: (i + first, 0, 0)),
        acts,
        [pltpu.VMEM((K, rows), BF16)],
        {4 + UNROLL: 0} if more else {},
    )(me, probed, row_data, inv, *[acts] * UNROLL, *more)


def alpha_kernel(along, current, total_weight, alpha_t, inverse):
    now = current[...]
    curvature = (along[...] - precise(now, now)) / total_weight[...] + RIDGE * now
    alpha, inv = solve_positive(beside(symmetric(curvature), now), beside(now, identity()))
    alpha_t[...] = alpha.T
    inverse[...] = symmetric(inv)


def offset_kernel(base_a, base_b, current, total_weight, offset):
    base = jnp.concatenate([base_a[...], base_b[...]], axis=0)
    offset[...] = RIDGE * base - precise(current[...] / total_weight[...], base)


def before_kernel(current, renewed, mixed, beta_t, total_weight, fixed, cross_t):
    now, beta, weight = current[...], beta_t[...], total_weight[...]
    cross = mixed[...] + outer(now, beta)
    length = renewed[...] + outer(mixed[...].T, beta) + precise(beta, cross)
    turned = cross.T
    cross_t[...] = turned
    fixed[...] = RIDGE * length - outer(turned, turned) / weight


def last_kernel(
    along, fixed, cross_t, renewed, beta_t, alpha_t, total_weight, back_row, base_a, base_b, image_a, image_b,
    solved, rest, on_panel,
):
    weight = total_weight[...]
    curvature = symmetric(along[...] / weight + fixed[...])
    step = solve_positive(beside(curvature, renewed[...]))[0].T
    on_panel[...] = step * (back_row[...] / weight)
    alpha = alpha_t[...]
    all_three = precise(step, jnp.concatenate([identity() + beta_t[...], alpha, cross_t[...]], axis=1))
    direction_base, direction_image = all_three[:, :K], all_three[:, K : 2 * K]
    crossed = all_three[:, 2 * K :] / weight
    both = jnp.concatenate([base_a[...], base_b[...], image_a[...], image_b[...]], axis=0)
    solved[...] = precise(beside(alpha + direction_base, -direction_image), both)
    rest[...] = precise(
        beside(identity() - RIDGE * direction_base + crossed, RIDGE * direction_image - alpha), both
    )


def small(kernel, name, outs, *args):
    return pl.pallas_call(
        kernel, out_shape=tuple(jax.ShapeDtypeStruct(shape, F32) for shape in outs), name=name,
        cost_estimate=pl.CostEstimate(flops=1 << 26, bytes_accessed=1 << 20, transcendentals=0),
    )(*args)


def plain(n):
    return lambda value, bit: swap(value.astype(F16), bit, n).astype(F32)


def split_blocks(value, left, bit):
    axis = left.index(bit)
    keep = lax.index_in_dim(value, 0, axis, keepdims=False)
    send = lax.index_in_dim(value, 1, axis, keepdims=False)
    return keep, send, [other for other in left if other != bit]


def reduce_scatter(blocks, n, swap_a, swap_b, along, waiting, work=None, args=(), along_ends=True):
    bits = n.bit_length() - 2
    shape = (2,) * bits + (HALF, blocks.shape[2])
    a, b = blocks[:, :HALF].reshape(shape), blocks[:, HALF:].reshape(shape)
    left_a = left_b = [1 << i for i in range(bits, 0, -1)]
    order_a, order_b = hop_bits(n)
    waiting, done = list(waiting), ()
    for phase, (bit_a, bit_b) in enumerate(zip(order_a, order_b)):
        keep_a, send_a, left_a = split_blocks(a, left_a, bit_a)
        keep_b, send_b, left_b = split_blocks(b, left_b, bit_b)
        tied = args if phase == 1 else done
        send_a, send_b, along, tied = lax.optimization_barrier((send_a, send_b, along, tied))
        a, b = keep_a + swap_a(send_a, bit_a), keep_b + swap_b(send_b, bit_b)
        if waiting:
            along = along + swap(along, waiting.pop(0), n)
        if work is not None and phase >= 1:
            done = work(*tied) if phase == 1 else tied
    if along_ends:
        a, b, along = lax.optimization_barrier((a, b, along))
    return a, b, along, done


class Root:
    def __init__(self, n, bound):
        self.n, self.scale = n, TOP / bound**0.5

    def __call__(self, send, bit):
        root = jnp.sqrt(jnp.abs(send)) * self.scale
        got = swap(jnp.where(send < 0, -root, root).astype(F16), bit, self.n).astype(F32)
        return got * jnp.abs(got) * (1.0 / self.scale**2)


def gather(top, low, n, orders, acts, work=None, args=()):
    a, b = top.astype(BF16)[None], low.astype(BF16)[None]
    done = ()
    for phase, (bit_a, bit_b) in enumerate(zip(*orders)):
        tied = args if phase == 1 else done
        a, b, tied, acts = lax.optimization_barrier((a, b, tied, acts))
        if work is not None and phase >= 1:
            done = work(*tied) if phase == 1 else tied
        a = jnp.concatenate([a, swap(a, bit_a, n)], axis=0)
        b = jnp.concatenate([b, swap(b, bit_b, n)], axis=0)
    near, a, b = lax.optimization_barrier((load(acts), a, b))
    return (a, b), (swap(a, 1, n), swap(b, 1, n)), near, done


def per_device(n, activations, labels, counts):
    rows, d = activations.shape
    activations = pltpu.with_memory_space_constraint(activations, pltpu.HBM)
    me = lax.axis_index("dp").astype(jnp.int32).reshape(1)
    row_data = (counts * K + labels).reshape(1, rows)
    order_y, order_z = hop_bits(n)
    order_a, order_b = order_y[::-1], order_z[::-1]
    shifts = [[bit.bit_length() - 1 for bit in order] for order in (order_a, order_b)]

    root = Root(n, BOUND * 4 * rows * n)
    sent, weight = class_sums(me, row_data, activations, n, 1)
    weight = weight.T
    got = root(sent, 1)
    weight = weight + swap(weight, 1, n)
    kept, _ = class_sums(me, row_data, activations, n, 0)
    top, low, weight, _ = reduce_scatter(kept + got, n, root, root, weight, order_y)
    class_weight = weight.T
    total_weight = jnp.sum(class_weight, keepdims=True)
    factor = 1.0 / jnp.sqrt(class_weight)
    base = top * factor[:HALF], low * factor[HALF:]

    def scatter(close, probed, along, inv, sent, early, work, args):
        hop = plain(n)
        got = hop(sent, 1)
        along = along + swap(along, 1, n)
        waiting = order_y
        if early:
            kept = panel_keep(me, probed, row_data, inv, close, n, 0)
            kept, along = lax.optimization_barrier((kept, along))
            along = along + swap(along, waiting[0], n)
            kept = panel_keep(me, probed, row_data, inv, close, n, 1, kept)
            waiting = waiting[1:]
        else:
            kept = panel_keep(me, probed, row_data, inv, close, n)
        return reduce_scatter(kept + got, n, hop, hop, along, waiting, work, args, not early)

    square, strip = (K, K), (K, d // n)
    orders = order_a, order_b
    base_near, base_far, close, _ = gather(*base, n, orders, activations)
    starts = probe(me, (base_near,), close, n, shifts)
    first, along, inv, back, _, sent, current = probe_and_send(
        me, (base_far,), close, row_data, total_weight, starts, (), n, shifts
    )
    panel_a, panel_b, along, (offset,) = scatter(
        close, first, along, inv, sent, False,
        lambda *args: small(offset_kernel, "offset", (strip,), *args), (*base, current, total_weight),
    )
    back = back / total_weight
    image = panel_a * back[:HALF] + offset[:HALF], panel_b * back[HALF:] + offset[HALF:]

    near, far, close, (alpha_t, inverse) = gather(
        *image, n, orders, activations,
        lambda *args: small(alpha_kernel, "alpha", (square,) * 2, *args), (along, current, total_weight),
    )
    starts = probe(me, (near, base_near), close, n, shifts)
    probed, along, inv, _, back_row, sent, _, _, renewed, mixed, beta_t = probe_and_send(
        me, (far, base_far), close, row_data, total_weight, starts, (first, current, alpha_t, inverse), n, shifts
    )
    panel_a, panel_b, along, (fixed, cross_t) = scatter(
        close, probed, along, inv, sent, True,
        lambda *args: small(before_kernel, "before", (square,) * 2, *args),
        (current, renewed, mixed, beta_t, total_weight),
    )
    solved, rest, on_panel = small(
        last_kernel, "last", (strip, strip, square),
        along, fixed, cross_t, renewed, beta_t, alpha_t, total_weight, back_row, *base, *image,
    )
    residual = (rest - precise(on_panel[:, HALF:], panel_b)) - precise(on_panel[:, :HALF], panel_a)
    return (solved.T, residual.T)


def solution(mesh):
    in_specs = (P(("groups", "dp"), None), P(("groups", "dp")), P(("groups", "dp")))
    out_specs = (P(("groups", "dp"), None), P(("groups", "dp"), None))
    return jax.shard_map(
        functools.partial(per_device, mesh.shape["dp"]),
        mesh=mesh,
        in_specs=in_specs,
        out_specs=out_specs,
        check_vma=False,
    )
```
